128 devices in a mesh: aa: 16 (over x, z), ba: 8 (over y, core).
Axes of the slice: x: 4, y: 4, z: 4, core: 2. Of those that a mesh axis runs over, the one named last changes fastest.
Arguments:
- tokens: bfloat16 [16384, 1024], P(('aa', 'ba')), may hold values from -24 to 24, as said below
- attn_gain: float32 [1024], replicated, may hold values from 0.25 to 1.75
- w_query: bfloat16 [1024, 1024], replicated, may hold values from -0.1875 to 0.1875
- w_key: bfloat16 [1024, 1024], replicated, may hold values from -0.1875 to 0.1875
- w_value: bfloat16 [1024, 1024], replicated, may hold values from -0.1875 to 0.1875
- head_gain: float32 [1024], P('ba'), may hold values from 0.25 to 1.75
- w_output: bfloat16 [1024, 1024], replicated, may hold values from -0.1875 to 0.1875
- mlp_gain: float32 [1024], replicated, may hold values from 0.25 to 1.75
- w_in: bfloat16 [1024, 4096], replicated, may hold values from -0.1875 to 0.1875
- w_out: bfloat16 [4096, 1024], replicated, may hold values from -0.09375 to 0.09375
Outputs:
- attended: bfloat16 [16384, 1024], P(('aa', 'ba'))
- result: bfloat16 [16384, 1024], P(('aa', 'ba'))
The draws below stay inside these ranges and needn't reach their ends.
Inputs may be any that keep to these rules, and one draw needn't show every extreme that they name: `tokens`: entries have magnitude at most 24.
All inputs are finite; a program needn't handle non-finite values.
Results may differ from the reference program's by a relative error of at most 0.013.
Values may be sent and summed in bfloat16 or wider, within the bound.
No kernel may reach another device: no remote copies, remote signals or barrier semaphores. Data moves between devices by JAX's collectives and lax.ppermute only.
A program may use at most 128 MiB of HBM per device.

```python
import math
import jax
import jax.numpy as jnp
from jax import lax

D = 1024
H = 16
FF = 4096
BLOCK = 1024
TOKENS = 16384


def draw_tokens(key, part):
    key_col = jax.random.fold_in(key, 11)
    key_row = jax.random.fold_in(key, 12)
    key_basis = jax.random.fold_in(key, 13)
    col_scale = jnp.exp(jax.random.uniform(key_col, (D,), jnp.float32, math.log(0.3), math.log(3.0)))
    row_scale = jnp.exp(jax.random.uniform(key_row, (TOKENS, 1), jnp.float32, math.log(0.5), math.log(2.0)))
    basis = jax.random.normal(key_basis, (TOKENS, D), jnp.float32)
    basis = jnp.clip(basis, -4.0, 4.0)
    return (basis * col_scale * row_scale).astype(jnp.bfloat16)


def centred(stream_key, extent, spread, limit, kind=jnp.bfloat16):
    return jnp.clip(spread * jax.random.normal(stream_key, extent, jnp.float32), -limit, limit).astype(kind)


def setup_inputs(seed: int = 0) -> dict:
    arg_keys = jax.random.split(jax.random.key(seed), 11)
    return {
        "tokens": draw_tokens(jax.random.fold_in(arg_keys[10], 71), 0),
        "attn_gain": jnp.clip(1.0 + 0.15 * jax.random.normal(arg_keys[1], (D,), jnp.float32), 0.25, 1.75),
        "w_query": centred(arg_keys[2], (D, D), D ** -0.5, 0.1875),
        "w_key": centred(arg_keys[3], (D, D), D ** -0.5, 0.1875),
        "w_value": centred(arg_keys[4], (D, D), D ** -0.5, 0.1875),
        "head_gain": jnp.clip(1.0 + 0.15 * jax.random.normal(arg_keys[5], (D,), jnp.float32), 0.25, 1.75),
        "w_output": centred(arg_keys[6], (D, D), D ** -0.5, 0.1875),
        "mlp_gain": jnp.clip(1.0 + 0.15 * jax.random.normal(arg_keys[7], (D,), jnp.float32), 0.25, 1.75),
        "w_in": centred(arg_keys[8], (D, FF), D ** -0.5, 0.1875),
        "w_out": centred(arg_keys[9], (FF, D), FF ** -0.5, 0.09375),
    }


HIGHEST = lax.Precision.HIGHEST

def rms_scale(matrix, scale_vec):
    matrix = matrix.astype(jnp.float32)
    return matrix * lax.rsqrt(lax.optimization_barrier(jnp.mean(matrix * matrix, axis=-1, keepdims=True)) + 1e-05) * scale_vec.astype(jnp.float32)

def to_bf_round(matrix):
    return lax.optimization_barrier(matrix.astype(jnp.bfloat16)).astype(jnp.float32)

def pair_features(vectors, weight_pairs):
    vec_width = vectors.shape[-1]
    pieces = []
    for column in range(vec_width):
        product = vectors[..., column:column + 1] * vectors[..., column:]
        if weight_pairs:
            factors = jnp.concatenate([jnp.ones((1,), jnp.float32), jnp.full((vec_width - column - 1,), 2.0, jnp.float32)])
            product = product * factors
        pieces.append(product)
    return jnp.concatenate(pieces, axis=-1)

def power_attention(queries, keys, values):
    length = queries.shape[0]
    head_size = D // H
    block_len = min(512, BLOCK)
    blocks = length // block_len
    query_all = queries.astype(jnp.float32).reshape(blocks, block_len, H, head_size)
    key_all = keys.astype(jnp.float32).reshape(blocks, block_len, H, head_size)
    value_all = values.astype(jnp.float32).reshape(blocks, block_len, H, head_size)
    causal = jnp.arange(block_len)[:, None] >= jnp.arange(block_len)[None, :]
    feat_count = head_size * (head_size + 1) // 2

    def advance(carry_state, block_in):
        query_blk, key_blk, value_blk = block_in
        scores = jnp.einsum('ihd,jhd->hij', query_blk, key_blk, precision=HIGHEST)
        weights = jnp.where(causal[None], to_bf_round(scores * scores), 0.0)
        inside = jnp.einsum('hij,jhd->ihd', weights, value_blk, precision=HIGHEST)
        query_feat = to_bf_round(pair_features(query_blk, False))
        carried = jnp.einsum('ihf,hfd->ihd', query_feat, to_bf_round(carry_state), precision=HIGHEST)
        key_feat = to_bf_round(pair_features(key_blk, True))
        grown_state = carry_state + jnp.einsum('jhf,jhd->hfd', key_feat, value_blk, precision=HIGHEST)
        return (grown_state, inside + carried)
    start_state = jnp.zeros((H, feat_count, head_size), jnp.float32)
    final_state, numerator = lax.scan(advance, start_state, (query_all, key_all, value_all))
    return numerator.reshape(length, H, head_size)

def reference(tokens, attn_gain, w_query, w_key, w_value, head_gain, w_output, mlp_gain, w_in, w_out):
    length = tokens.shape[0]
    normed = rms_scale(tokens, attn_gain).astype(jnp.bfloat16)
    queries = jnp.dot(normed, w_query, preferred_element_type=jnp.float32).astype(jnp.bfloat16)
    keys = jnp.dot(normed, w_key, preferred_element_type=jnp.float32).astype(jnp.bfloat16)
    values = jnp.dot(normed, w_value, preferred_element_type=jnp.float32).astype(jnp.bfloat16)
    numerator = power_attention(queries, keys, values)
    scaled = numerator * lax.rsqrt(lax.optimization_barrier(jnp.mean(numerator * numerator, axis=-1, keepdims=True)) + 1e-05)
    attended = (scaled.reshape(length, D) * head_gain.astype(jnp.float32)).astype(jnp.bfloat16)
    stream = (tokens.astype(jnp.float32) + jnp.dot(attended, w_output, preferred_element_type=jnp.float32)).astype(jnp.bfloat16)
    normed_mlp = rms_scale(stream, mlp_gain).astype(jnp.bfloat16)
    hidden = jax.nn.gelu(jnp.dot(normed_mlp, w_in, preferred_element_type=jnp.float32), approximate=True).astype(jnp.bfloat16)
    result = (stream.astype(jnp.float32) + jnp.dot(hidden, w_out, preferred_element_type=jnp.float32)).astype(jnp.bfloat16)
    return (attended, result)
```

```python
import jax
import jax.numpy as jnp
from jax import lax
from jax.experimental import pallas as pl
from jax.experimental.pallas import tpu as pltpu
from jax.sharding import Mesh
from jax.sharding import PartitionSpec as P

D = 1024
FF = 4096
HS = 64
NF = HS * (HS + 1) // 2
PIECE = NF // 4
ROWS = 128
LEN = 1024
F32 = jnp.float32
BF = jnp.bfloat16
SPLIT = ("x", "z", "y", "c")
BA = ("y", "c")
MIB = 1 << 20


VM = pl.BlockSpec(memory_space=pltpu.VMEM)
HBM = pl.BlockSpec(memory_space=pl.ANY)


def xor_pairs(n, k):
    return [(i, i ^ k) for i in range(n)]


def flip(index, k):
    return jnp.bitwise_xor(index, k) if k else index


def ba_index():
    return lax.axis_index("y") * 2 + lax.axis_index("c")


def rms(matrix, gain):
    return matrix * lax.rsqrt(jnp.mean(matrix * matrix, axis=-1, keepdims=True) + 1e-05) * gain


def qkv_kernel(tok, gain, wq, wk, wv, *rest):
    outs, (wbuf, sems) = rest[:8], rest[8:]
    me = ba_index()
    copies = []
    for k in range(8):
        col = pl.multiple_of(flip(me, k) * 128, 128)
        for j, w in enumerate((wq, wk, wv)):
            copy = pltpu.make_async_copy(
                w.at[:, pl.ds(col, 128)], wbuf.at[k, :, j * 128 : (j + 1) * 128], sems.at[k, j]
            )
            copy.start()
            copies.append(copy)
    normed = rms(tok[...].astype(F32), gain[...]).astype(BF)
    for k in range(8):
        for j in range(3):
            copies[3 * k + j].wait()
        outs[k][...] = jnp.dot(normed, wbuf[k], preferred_element_type=F32).astype(BF)


def fill_pairs(ext, h, phi, col, weighted):
    base = ext[h, 0:HS, :]
    twice = base + base if weighted else base
    for d in range(33):
        rows = HS if d < 32 else 32
        left = base if d == 0 else twice
        phi[d * HS : d * HS + rows, col : col + LEN] = (
            left[0:rows] * ext[h, d : d + rows, :]
        ).astype(BF)


def state_kernel(*refs):
    chunks, outs = refs[:8], refs[8:12]
    ext, vz, phi, state = refs[12:]
    lane = lax.broadcasted_iota(jnp.int32, (ROWS, 128), 1)
    zero = jnp.zeros((ROWS, 128), BF)
    for k in range(8):
        at = slice(k * ROWS, (k + 1) * ROWS)
        turned = chunks[k][:, 128:256].astype(F32).T
        value = chunks[k][:, 256:384]
        for h in range(2):
            part = turned[h * HS : (h + 1) * HS]
            ext[h, 0:HS, at] = part
            ext[h, HS : 2 * HS, at] = part
            mine = (lane >= HS) if h else (lane < HS)
            vz[h * LEN + k * ROWS : h * LEN + (k + 1) * ROWS, :] = jnp.where(mine, value, zero)
    for h in range(2):
        fill_pairs(ext, h, phi, h * LEN, True)
    for c in range(4):
        at = slice(c * PIECE, (c + 1) * PIECE)
        state[at, :] = jnp.dot(phi[at, :], vz[...], preferred_element_type=F32)
    me = lax.axis_index("z")
    for k in range(4):
        row = pl.multiple_of(flip(me, k) * PIECE, 8)
        outs[k][...] = state[pl.ds(row, PIECE), :].astype(BF)


def inside_kernel(*refs):
    chunks, out = refs[:8], refs[8]
    q, kk, v = refs[9:]
    me = ba_index()
    for k in range(8):
        at = pl.ds(pl.multiple_of(flip(me, k) * ROWS, ROWS), ROWS)
        q[at, :] = chunks[k][:, 0:128]
        kk[at, :] = chunks[k][:, 128:256]
        v[at, :] = chunks[k][:, 256:384]
    T = 256
    lane_q = lax.broadcasted_iota(jnp.int32, (T, 128), 1)
    lane_v = lax.broadcasted_iota(jnp.int32, (LEN, 128), 1)
    causal = lax.broadcasted_iota(jnp.int32, (T, T), 0) >= lax.broadcasted_iota(
        jnp.int32, (T, T), 1
    )
    nt = (((1,), (1,)), ((), ()))
    vh = [jnp.where((lane_v >= HS) if h else (lane_v < HS), v[...], jnp.zeros((), BF)) for h in range(2)]
    for i in range(LEN // T):
        rows = slice(i * T, (i + 1) * T)
        total = None
        for h in range(2):
            qh = jnp.where((lane_q >= HS) if h else (lane_q < HS), q[rows, :], jnp.zeros((), BF))
            last = lax.dot_general(qh, kk[rows, :], nt, preferred_element_type=F32)
            last = jnp.where(causal, last * last, 0.0).astype(BF)
            add = jnp.dot(last, vh[h][rows], preferred_element_type=F32)
            total = add if total is None else total + add
            if i:
                full = lax.dot_general(qh, kk[0 : i * T, :], nt, preferred_element_type=F32)
                full = (full * full).astype(BF)
                total = total + jnp.dot(full, vh[h][0 : i * T], preferred_element_type=F32)
        out[rows, :] = total


def total_kernel(*refs):
    pieces, out = refs[:4], refs[4]
    out[...] = sum(p[...].astype(F32) for p in pieces).astype(BF)


def combine_kernel(*refs):
    pieces, totals, outs = refs[:4], refs[4:8], refs[8:12]
    x, z = lax.axis_index("x"), lax.axis_index("z")
    base = jnp.zeros((PIECE, 128), F32)
    for k in range(1, 4):
        base = base + jnp.where(flip(x, k) < x, totals[k][...].astype(F32), 0.0)
    for k in range(4):
        acc = base
        for j in range(4):
            if j != k:
                acc = acc + jnp.where(flip(z, j) < flip(z, k), pieces[j][...].astype(F32), 0.0)
        outs[k][...] = acc.astype(BF)


def apply_kernel(*refs):
    chunks, states, inside, gain, outs = refs[:8], refs[8:12], refs[12], refs[13], refs[14:22]
    ext, phi, state, done = refs[22:]
    me, z = ba_index(), lax.axis_index("z")
    for k in range(4):
        row = pl.multiple_of(flip(z, k) * PIECE, 8)
        state[pl.ds(row, PIECE), :] = states[k][...].astype(F32)
    for k in range(8):
        at = pl.ds(pl.multiple_of(flip(me, k) * ROWS, ROWS), ROWS)
        turned = chunks[k][:, 0:128].astype(F32).T
        for h in range(2):
            part = turned[h * HS : (h + 1) * HS]
            ext[h, 0:HS, at] = part
            ext[h, HS : 2 * HS, at] = part
    turned_state = state[...].T.astype(BF)
    halves = []
    for h in range(2):
        fill_pairs(ext, h, phi, h * LEN, False)
        halves.append(
            jnp.dot(
                turned_state[h * HS : (h + 1) * HS],
                phi[:, h * LEN : (h + 1) * LEN],
                preferred_element_type=F32,
            )
        )
    numer = jnp.concatenate(halves, axis=0).T + inside[...]
    square = numer * numer
    low = lax.broadcasted_iota(jnp.int32, (LEN, 128), 1) < HS
    first = jnp.sum(jnp.where(low, square, 0.0), axis=-1, keepdims=True)
    second = jnp.sum(jnp.where(low, 0.0, square), axis=-1, keepdims=True)
    mean = jnp.where(low, first, second) * (1.0 / HS)
    done[...] = numer * lax.rsqrt(mean + 1e-05) * gain[...]
    for k in range(8):
        at = pl.ds(pl.multiple_of(flip(me, k) * ROWS, ROWS), ROWS)
        outs[k][...] = done[at, :].astype(BF)


FB = 512


def mlp_kernel(*refs):
    parts, tok, gain, wo, wi, wf = refs[:8], refs[8], refs[9], refs[10], refs[11], refs[12]
    att, res = refs[13:15]
    bo, bi, bf, so, si, sf = refs[15:]
    n = FF // FB
    copy_o = pltpu.make_async_copy(wo, bo, so)
    copy_o.start()
    copies = []
    for j in range(n):
        ci = pltpu.make_async_copy(wi.at[:, j * FB : (j + 1) * FB], bi.at[j], si.at[j])
        cf = pltpu.make_async_copy(wf.at[j * FB : (j + 1) * FB, :], bf.at[j], sf.at[j])
        ci.start()
        cf.start()
        copies.append((ci, cf))
    me = ba_index()
    for k in range(8):
        col = pl.multiple_of(flip(me, k) * 128, 128)
        att[:, pl.ds(col, 128)] = parts[k][...]
    copy_o.wait()
    stream = tok[...].astype(F32) + jnp.dot(att[...], bo[...], preferred_element_type=F32)
    stream = stream.astype(BF).astype(F32)
    normed = rms(stream, gain[...]).astype(BF)
    acc = stream
    for j in range(n):
        copies[j][0].wait()
        u = jnp.dot(normed, bi[j], preferred_element_type=F32)
        hidden = 0.5 * u * (1.0 + jnp.tanh(0.7978845608028654 * (u + 0.044715 * u * u * u)))
        copies[j][1].wait()
        acc = acc + jnp.dot(hidden.astype(BF), bf[j], preferred_element_type=F32)
    res[...] = acc.astype(BF)


def call(kernel, outs, scratch, specs, limit, name, flops=0, moved=0):
    return pl.pallas_call(
        kernel,
        out_shape=outs,
        in_specs=specs,
        out_specs=jax.tree.map(lambda _: VM, outs),
        scratch_shapes=scratch,
        compiler_params=pltpu.CompilerParams(vmem_limit_bytes=limit * MIB),
        cost_estimate=pl.CostEstimate(flops=flops, bytes_accessed=moved, transcendentals=0),
        name=name,
    )


def arr(*shape, dtype=BF):
    return jax.ShapeDtypeStruct(shape, dtype)


def body(tokens, attn_gain, w_query, w_key, w_value, head_gain, w_output, mlp_gain, w_in, w_out):
    chunks = call(
        qkv_kernel,
        [arr(ROWS, 384)] * 8,
        [pltpu.VMEM((8, D, 384), BF), pltpu.SemaphoreType.DMA((8, 3))],
        [VM, VM, HBM, HBM, HBM],
        16,
        "qkv",
        flops=2 * 128 * 1024 * 3072,
        moved=7 * MIB,
    )(tokens, attn_gain.reshape(1, D), w_query, w_key, w_value)
    order = (4, 5, 6, 7, 2, 3, 1)
    moved = {k: lax.ppermute(chunks[k], BA, xor_pairs(8, k)) for k in order}
    chunks = [chunks[0]] + [moved[k] for k in range(1, 8)]

    pieces = call(
        state_kernel,
        [arr(PIECE, 128)] * 4,
        [
            pltpu.VMEM((2, 2 * HS, LEN), F32),
            pltpu.VMEM((2 * LEN, 128), BF),
            pltpu.VMEM((NF, 2 * LEN), BF),
            pltpu.VMEM((NF, 128), F32),
        ],
        [VM] * 8,
        24,
        "state",
        flops=2 * NF * 2 * LEN * 256,
        moved=2 * MIB,
    )(*chunks)
    moved = {k: lax.ppermute(pieces[k], "z", xor_pairs(4, k)) for k in (2, 1, 3)}
    pieces = [pieces[0]] + [moved[k] for k in range(1, 4)]

    inside = call(
        inside_kernel,
        arr(LEN, 128, dtype=F32),
        [pltpu.VMEM((LEN, 128), BF)] * 3,
        [VM] * 8,
        16,
        "inside",
        flops=2 * 1024 * 1024 * 256 * 2,
        moved=2 * MIB,
    )(*chunks)

    total = call(total_kernel, arr(PIECE, 128), [], [VM] * 4, 4, "total", moved=MIB)(*pieces)
    moved = {k: lax.ppermute(total, "x", xor_pairs(4, k)) for k in (2, 1, 3)}
    totals = [total] + [moved[k] for k in range(1, 4)]
    states = call(combine_kernel, [arr(PIECE, 128)] * 4, [], [VM] * 8, 8, "combine", moved=MIB)(
        *pieces, *totals
    )
    moved = {k: lax.ppermute(states[k], "z", xor_pairs(4, k)) for k in (2, 1, 3)}
    states = [states[0]] + [moved[k] for k in range(1, 4)]

    parts = call(
        apply_kernel,
        [arr(ROWS, 128)] * 8,
        [
            pltpu.VMEM((2, 2 * HS, LEN), F32),
            pltpu.VMEM((NF, 2 * LEN), BF),
            pltpu.VMEM((NF, 128), F32),
            pltpu.VMEM((LEN, 128), F32),
        ],
        [VM] * 14,
        28,
        "apply",
        flops=2 * NF * 2 * LEN * 256,
        moved=2 * MIB,
    )(*chunks, *states, inside, head_gain.reshape(1, 128))
    moved = {k: lax.ppermute(parts[k], BA, xor_pairs(8, k)) for k in order}
    parts = [parts[0]] + [moved[k] for k in range(1, 8)]

    n = FF // FB
    return call(
        mlp_kernel,
        [arr(ROWS, D)] * 2,
        [
            pltpu.VMEM((D, D), BF),
            pltpu.VMEM((n, D, FB), BF),
            pltpu.VMEM((n, FB, D), BF),
            pltpu.SemaphoreType.DMA(()),
            pltpu.SemaphoreType.DMA((n,)),
            pltpu.SemaphoreType.DMA((n,)),
        ],
        [VM] * 10 + [HBM] * 3,
        32,
        "mlp",
        flops=2 * 128 * 1024 * 9216,
        moved=18 * MIB,
    )(*parts, tokens, mlp_gain.reshape(1, D), w_output, w_in, w_out)


def solution(mesh):
    finer = Mesh(mesh.devices.reshape(4, 4, 4, 2), SPLIT)
    placed = (P(SPLIT, None), P(), P(), P(), P(), P(BA), P(), P(), P(), P())
    return jax.shard_map(
        body,
        mesh=finer,
        in_specs=placed,
        out_specs=(P(SPLIT, None), P(SPLIT, None)),
        check_vma=False,
    )
```

```python
import jax
import jax.numpy as jnp
from jax import lax
from jax.experimental import pallas as pl
from jax.experimental.pallas import tpu as pltpu
from jax.sharding import Mesh
from jax.sharding import PartitionSpec as P

D = 1024
FF = 4096
HS = 64
NF = HS * (HS + 1) // 2
PIECE = NF // 4
ROWS = 128
PAIR = 2 * ROWS
LEN = 1024
F32 = jnp.float32
BF = jnp.bfloat16
SPLIT = ("x", "z", "y", "c")
BA = ("y", "c")
MIB = 1 << 20


VM = pl.BlockSpec(memory_space=pltpu.VMEM)
HBM = pl.BlockSpec(memory_space=pltpu.HBM)


def xor_pairs(n, k):
    return [(i, i ^ k) for i in range(n)]


def flip(index, k):
    return jnp.bitwise_xor(index, k) if k else index


def rms(matrix, gain):
    return matrix * lax.rsqrt(jnp.mean(matrix * matrix, axis=-1, keepdims=True) + 1e-05) * gain


def copy_columns(sources, buf, sems, k):
    col = pl.multiple_of((2 * flip(lax.axis_index("y"), k) + lax.axis_index("c")) * 128, 128)
    copies = []
    for j, w in enumerate(sources):
        copy = pltpu.make_async_copy(
            w.at[:, pl.ds(col, 128)], buf.at[k, :, j * 128 : (j + 1) * 128], sems.at[k, j]
        )
        copy.start()
        copies.append(copy)
    return copies


def kv_kernel(tok, other, gain, wk, wv, *rest):
    outs, normed = rest[:4], rest[4]
    wbuf, tbuf, gbuf, sems, tsems = rest[5:]
    first = [
        pltpu.make_async_copy(src, dst, tsems.at[i])
        for i, (src, dst) in enumerate(
            ((gain, gbuf), (tok, tbuf))
        )
    ]
    for copy in first:
        copy.start()
    copies = [copy_columns((wk, wv), wbuf, sems, k) for k in range(4)]
    c = lax.axis_index("c")
    for copy in first:
        copy.wait()
    for src, place in ((other, 1 - c), (tbuf, c)):
        at = pl.ds(pl.multiple_of(place * ROWS, ROWS), ROWS)
        normed[at, :] = rms(src[...].astype(F32), gbuf[...]).astype(BF)
    for k in range(4):
        for copy in copies[k]:
            copy.wait()
        outs[k][...] = jnp.dot(normed[...], wbuf[k], preferred_element_type=F32).astype(BF)


def q_kernel(normed, wq, after, *rest):
    outs, wbuf, sems = rest[:4], rest[4], rest[5]
    copies = [copy_columns((wq,), wbuf, sems, k) for k in range(4)]
    for k in range(4):
        for copy in copies[k]:
            copy.wait()
        outs[k][...] = jnp.dot(normed[...], wbuf[k], preferred_element_type=F32).astype(BF)


def fill_pairs(ext, h, phi, col, weighted):
    base = ext[h, 0:HS, :]
    twice = base + base if weighted else base
    for d in range(33):
        rows = HS if d < 32 else 32
        left = base if d == 0 else twice
        phi[d * HS : d * HS + rows, col : col + LEN] = (
            left[0:rows] * ext[h, d : d + rows, :]
        ).astype(BF)


def state_kernel(*refs):
    chunks, outs = refs[:4], refs[4:8]
    ext, vz, phi, state = refs[8:]
    lane = lax.broadcasted_iota(jnp.int32, (PAIR, 128), 1)
    zero = jnp.zeros((PAIR, 128), BF)
    for k in range(4):
        at = slice(k * PAIR, (k + 1) * PAIR)
        turned = chunks[k][:, 0:128].astype(F32).T
        value = chunks[k][:, 128:256]
        for h in range(2):
            part = turned[h * HS : (h + 1) * HS]
            ext[h, 0:HS, at] = part
            ext[h, HS : 2 * HS, at] = part
            mine = (lane >= HS) if h else (lane < HS)
            vz[h * LEN + k * PAIR : h * LEN + (k + 1) * PAIR, :] = jnp.where(mine, value, zero)
    for h in range(2):
        fill_pairs(ext, h, phi, h * LEN, True)
    for c in range(4):
        at = slice(c * PIECE, (c + 1) * PIECE)
        state[at, :] = jnp.dot(phi[at, :], vz[...], preferred_element_type=F32)
    me = lax.axis_index("z")
    for k in range(4):
        row = pl.multiple_of(flip(me, k) * PIECE, 8)
        outs[k][...] = state[pl.ds(row, PIECE), :].astype(BF)


def pair_rows(k):
    return pl.ds(pl.multiple_of(flip(lax.axis_index("y"), k) * PAIR, PAIR), PAIR)


def inside_kernel(*refs):
    pairs, queries, out = refs[:4], refs[4:8], refs[8]
    q, kk, v = refs[9:]
    for k in range(4):
        at = pair_rows(k)
        q[at, :] = queries[k][...]
        kk[at, :] = pairs[k][:, 0:128]
        v[at, :] = pairs[k][:, 128:256]
    T = 256
    lane_q = lax.broadcasted_iota(jnp.int32, (T, 128), 1)
    lane_v = lax.broadcasted_iota(jnp.int32, (LEN, 128), 1)
    causal = lax.broadcasted_iota(jnp.int32, (T, T), 0) >= lax.broadcasted_iota(
        jnp.int32, (T, T), 1
    )
    nt = (((1,), (1,)), ((), ()))
    vh = [jnp.where((lane_v >= HS) if h else (lane_v < HS), v[...], jnp.zeros((), BF)) for h in range(2)]
    for i in range(LEN // T):
        rows = slice(i * T, (i + 1) * T)
        total = None
        for h in range(2):
            qh = jnp.where((lane_q >= HS) if h else (lane_q < HS), q[rows, :], jnp.zeros((), BF))
            last = lax.dot_general(qh, kk[rows, :], nt, preferred_element_type=F32)
            last = jnp.where(causal, last * last, 0.0).astype(BF)
            add = jnp.dot(last, vh[h][rows], preferred_element_type=F32)
            total = add if total is None else total + add
            if i:
                full = lax.dot_general(qh, kk[0 : i * T, :], nt, preferred_element_type=F32)
                full = (full * full).astype(BF)
                total = total + jnp.dot(full, vh[h][0 : i * T], preferred_element_type=F32)
        out[rows, :] = total


def total_kernel(*refs):
    pieces, out = refs[:4], refs[4]
    out[...] = sum(p[...].astype(F32) for p in pieces).astype(BF)


def combine_kernel(*refs):
    pieces, totals, outs = refs[:4], refs[4:8], refs[8:12]
    x, z = lax.axis_index("x"), lax.axis_index("z")
    base = jnp.zeros((PIECE, 128), F32)
    for k in range(1, 4):
        base = base + jnp.where(flip(x, k) < x, totals[k][...].astype(F32), 0.0)
    for k in range(4):
        acc = base
        for j in range(4):
            if j != k:
                acc = acc + jnp.where(flip(z, j) < flip(z, k), pieces[j][...].astype(F32), 0.0)
        outs[k][...] = acc.astype(BF)


def apply_kernel(*refs):
    queries, states, inside, gain, outs = refs[:4], refs[4:8], refs[8], refs[9], refs[10:14]
    ext, phi, state, done = refs[14:]
    z = lax.axis_index("z")
    for k in range(4):
        row = pl.multiple_of(flip(z, k) * PIECE, 8)
        state[pl.ds(row, PIECE), :] = states[k][...].astype(F32)
    for k in range(4):
        at = pair_rows(k)
        turned = queries[k][...].astype(F32).T
        for h in range(2):
            part = turned[h * HS : (h + 1) * HS]
            ext[h, 0:HS, at] = part
            ext[h, HS : 2 * HS, at] = part
    turned_state = state[...].T.astype(BF)
    halves = []
    for h in range(2):
        fill_pairs(ext, h, phi, h * LEN, False)
        halves.append(
            jnp.dot(
                turned_state[h * HS : (h + 1) * HS],
                phi[:, h * LEN : (h + 1) * LEN],
                preferred_element_type=F32,
            )
        )
    numer = jnp.concatenate(halves, axis=0).T + inside[...]
    square = numer * numer
    low = lax.broadcasted_iota(jnp.int32, (LEN, 128), 1) < HS
    first = jnp.sum(jnp.where(low, square, 0.0), axis=-1, keepdims=True)
    second = jnp.sum(jnp.where(low, 0.0, square), axis=-1, keepdims=True)
    mean = jnp.where(low, first, second) * (1.0 / HS)
    done[...] = numer * lax.rsqrt(mean + 1e-05) * gain[...]
    for k in range(4):
        outs[k][...] = done[pair_rows(k), :].astype(BF)


def merge_kernel(*refs):
    parts, out = refs[:4], refs[4]
    row = pl.multiple_of((1 - lax.axis_index("c")) * ROWS, ROWS)
    for k in range(4):
        col = pl.multiple_of(flip(lax.axis_index("y"), k) * 128, 128)
        out[:, pl.ds(col, 128)] = parts[k][pl.ds(row, ROWS), :]


FB = 512


def mlp_kernel(*refs):
    parts, other, tok, gain, wo, wi, wf = refs[:4], *refs[4:10]
    att, res = refs[10:12]
    y, c = lax.axis_index("y"), lax.axis_index("c")
    row = pl.multiple_of(c * ROWS, ROWS)
    for k in range(4):
        col = pl.multiple_of((2 * flip(y, k) + c) * 128, 128)
        att[:, pl.ds(col, 128)] = parts[k][pl.ds(row, ROWS), :]
        col = pl.multiple_of((2 * k + 1 - c) * 128, 128)
        att[:, pl.ds(col, 128)] = other[:, k * 128 : (k + 1) * 128]
    stream = tok[...].astype(F32) + jnp.dot(att[...], wo[...], preferred_element_type=F32)
    stream = stream.astype(BF).astype(F32)
    normed = rms(stream, gain[...]).astype(BF)
    acc = stream
    for j in range(FF // FB):
        at = slice(j * FB, (j + 1) * FB)
        u = jnp.dot(normed, wi[:, at], preferred_element_type=F32)
        hidden = 0.5 * u * (1.0 + jnp.tanh(0.7978845608028654 * (u + 0.044715 * u * u * u)))
        acc = acc + jnp.dot(hidden.astype(BF), wf[at, :], preferred_element_type=F32)
    res[...] = acc.astype(BF)


def call(kernel, outs, scratch, specs, limit, name, flops=0, moved=0):
    return pl.pallas_call(
        kernel,
        out_shape=outs,
        in_specs=specs,
        out_specs=jax.tree.map(lambda _: VM, outs),
        scratch_shapes=scratch,
        compiler_params=pltpu.CompilerParams(vmem_limit_bytes=limit * MIB),
        cost_estimate=pl.CostEstimate(flops=flops, bytes_accessed=moved, transcendentals=0),
        name=name,
    )


def arr(*shape, dtype=BF):
    return jax.ShapeDtypeStruct(shape, dtype)


def fixed(array):
    return pltpu.with_memory_space_constraint(array, pltpu.HBM)


def exchange(parts, axis):
    moved = {k: lax.ppermute(parts[k], axis, xor_pairs(4, k)) for k in (2, 1, 3)}
    return [parts[0]] + [moved[k] for k in range(1, 4)]


def body(tokens, attn_gain, w_query, w_key, w_value, head_gain, w_output, mlp_gain, w_in, w_out):
    swapped = lax.ppermute(tokens, "c", xor_pairs(2, 1))
    *pairs, normed = call(
        kv_kernel,
        [arr(PAIR, 256)] * 4 + [arr(PAIR, D)],
        [
            pltpu.VMEM((4, D, 256), BF),
            pltpu.VMEM((ROWS, D), BF),
            pltpu.VMEM((1, D), F32),
            pltpu.SemaphoreType.DMA((4, 2)),
            pltpu.SemaphoreType.DMA((2,)),
        ],
        [HBM, VM, HBM, HBM, HBM],
        10,
        "kv",
        flops=2 * 256 * 1024 * 1024,
        moved=3 * MIB,
    )(fixed(tokens), swapped, fixed(attn_gain.reshape(1, D)), fixed(w_key), fixed(w_value))
    pairs = exchange(pairs, "y")

    pieces = call(
        state_kernel,
        [arr(PIECE, 128)] * 4,
        [
            pltpu.VMEM((2, 2 * HS, LEN), F32),
            pltpu.VMEM((2 * LEN, 128), BF),
            pltpu.VMEM((NF, 2 * LEN), BF),
            pltpu.VMEM((NF, 128), F32),
        ],
        [VM] * 4,
        20,
        "state",
        flops=2 * NF * 2 * LEN * 256,
        moved=2 * MIB,
    )(*pairs)
    queries = call(
        q_kernel,
        [arr(PAIR, 128)] * 4,
        [pltpu.VMEM((4, D, 128), BF), pltpu.SemaphoreType.DMA((4, 1))],
        [VM, HBM, HBM],
        6,
        "q",
        flops=2 * 256 * 1024 * 512,
        moved=MIB,
    )(normed, w_query, pieces[0])
    pieces = exchange(pieces, "z")
    queries = exchange(queries, "y")

    total = call(total_kernel, arr(PIECE, 128), [], [VM] * 4, 4, "total", moved=MIB)(*pieces)
    moved = {k: lax.ppermute(total, "x", xor_pairs(4, k)) for k in (2, 1, 3)}
    totals = [total] + [moved[k] for k in range(1, 4)]
    inside = call(
        inside_kernel,
        arr(LEN, 128, dtype=F32),
        [pltpu.VMEM((LEN, 128), BF)] * 3,
        [VM] * 8,
        16,
        "inside",
        flops=2 * 1024 * 1024 * 256 * 2,
        moved=2 * MIB,
    )(*pairs, *queries)
    states = call(combine_kernel, [arr(PIECE, 128)] * 4, [], [VM] * 8, 8, "combine", moved=MIB)(
        *pieces, *totals
    )
    states = exchange(states, "z")

    parts = call(
        apply_kernel,
        [arr(PAIR, 128)] * 4,
        [
            pltpu.VMEM((2, 2 * HS, LEN), F32),
            pltpu.VMEM((NF, 2 * LEN), BF),
            pltpu.VMEM((NF, 128), F32),
            pltpu.VMEM((LEN, 128), F32),
        ],
        [VM] * 10,
        20,
        "apply",
        flops=2 * NF * 2 * LEN * 256,
        moved=2 * MIB,
    )(*queries, *states, inside, head_gain.reshape(1, 128))
    parts = exchange(parts, "y")
    other = call(merge_kernel, arr(ROWS, 512), [], [VM] * 4, 4, "merge")(*parts)
    other = lax.ppermute(other, "c", xor_pairs(2, 1))

    return call(
        mlp_kernel,
        [arr(ROWS, D)] * 2,
        [],
        [VM] * 10,
        8,
        "mlp",
        flops=2 * 128 * 1024 * 9216,
        moved=18 * MIB,
    )(*parts, other, tokens, mlp_gain.reshape(1, D), w_output, w_in, w_out)


def solution(mesh):
    finer = Mesh(mesh.devices.reshape(4, 4, 4, 2), SPLIT)
    placed = (P(SPLIT, None), P(), P(), P(), P(), P(BA), P(), P(), P(), P())
    return jax.shard_map(
        body,
        mesh=finer,
        in_specs=placed,
        out_specs=(P(SPLIT, None), P(SPLIT, None)),
        check_vma=False,
    )
```

```python
import jax
import jax.numpy as jnp
from jax import lax
from jax.experimental import pallas as pl
from jax.experimental.pallas import tpu as pltpu
from jax.sharding import Mesh
from jax.sharding import PartitionSpec as P

D = 1024
FF = 4096
HS = 64
NF = HS * (HS + 1) // 2
PIECE = NF // 4
ROWS = 128
PAIR = 2 * ROWS
LEN = 1024
F32 = jnp.float32
BF = jnp.bfloat16
SPLIT = ("x", "z", "y", "c")
BA = ("y", "c")
MIB = 1 << 20


VM = pl.BlockSpec(memory_space=pltpu.VMEM)
HBM = pl.BlockSpec(memory_space=pltpu.HBM)
ANY = pl.BlockSpec(memory_space=pl.ANY)


def xor_pairs(n, k):
    return [(i, i ^ k) for i in range(n)]


def flip(index, k):
    return jnp.bitwise_xor(index, k) if k else index


def rms(matrix, gain):
    return matrix * lax.rsqrt(jnp.mean(matrix * matrix, axis=-1, keepdims=True) + 1e-05) * gain


def columns(k):
    return pl.multiple_of((2 * flip(lax.axis_index("y"), k) + lax.axis_index("c")) * 128, 128)


def load_kernel(tok, gain, wk, wv, normed, gout, wout, tbuf, sems, tsems):
    first = [
        pltpu.make_async_copy(gain, gout, tsems.at[0]),
        pltpu.make_async_copy(tok, tbuf, tsems.at[1]),
    ]
    for copy in first:
        copy.start()
    copies = []
    for k in range(4):
        for j, w in enumerate((wk, wv)):
            copy = pltpu.make_async_copy(
                w.at[:, pl.ds(columns(k), 128)],
                wout.at[k, :, j * 128 : (j + 1) * 128],
                sems.at[k, j],
            )
            copy.start()
            copies.append(copy)
    for copy in first:
        copy.wait()
    normed[...] = rms(tbuf[...].astype(F32), gout[...]).astype(BF)
    for copy in copies:
        copy.wait()


def kv_kernel(own, other, gain, wkv, *rest):
    outs, normed = rest[:4], rest[4]
    c = lax.axis_index("c")
    normed[pl.ds(pl.multiple_of(c * ROWS, ROWS), ROWS), :] = own[...]
    at = pl.ds(pl.multiple_of((1 - c) * ROWS, ROWS), ROWS)
    normed[at, :] = rms(other[...].astype(F32), gain[...]).astype(BF)
    for k in (1, 3, 2, 0):
        outs[k][...] = jnp.dot(normed[...], wkv[k], preferred_element_type=F32).astype(BF)


def q_kernel(normed, wq, *rest):
    outs, wbuf, sems = rest[:4], rest[4], rest[5]
    copies = []
    for k in range(4):
        copy = pltpu.make_async_copy(wq.at[:, pl.ds(columns(k), 128)], wbuf.at[k], sems.at[k])
        copy.start()
        copies.append(copy)
    for k in range(4):
        copies[k].wait()
        outs[k][...] = jnp.dot(normed[...], wbuf[k], preferred_element_type=F32).astype(BF)


def fill_pairs(ext, h, phi, col, weighted):
    base = ext[h, 0:HS, :]
    twice = base + base if weighted else base
    for d in range(33):
        rows = HS if d < 32 else 32
        left = base if d == 0 else twice
        phi[d * HS : d * HS + rows, col : col + LEN] = (
            left[0:rows] * ext[h, d : d + rows, :]
        ).astype(BF)


def state_kernel(*refs):
    chunks, outs = refs[:4], refs[4:8]
    ext, vz, phi, state = refs[8:]
    lane = lax.broadcasted_iota(jnp.int32, (PAIR, 128), 1)
    zero = jnp.zeros((PAIR, 128), BF)
    for k in range(4):
        at = slice(k * PAIR, (k + 1) * PAIR)
        turned = chunks[k][:, 0:128].astype(F32).T
        value = chunks[k][:, 128:256]
        for h in range(2):
            part = turned[h * HS : (h + 1) * HS]
            ext[h, 0:HS, at] = part
            ext[h, HS : 2 * HS, at] = part
            mine = (lane >= HS) if h else (lane < HS)
            vz[h * LEN + k * PAIR : h * LEN + (k + 1) * PAIR, :] = jnp.where(mine, value, zero)
    for h in range(2):
        fill_pairs(ext, h, phi, h * LEN, True)
    for c in range(4):
        at = slice(c * PIECE, (c + 1) * PIECE)
        state[at, :] = jnp.dot(phi[at, :], vz[...], preferred_element_type=F32)
    me = lax.axis_index("z")
    for k in range(4):
        row = pl.multiple_of(flip(me, k) * PIECE, 8)
        outs[k][...] = state[pl.ds(row, PIECE), :].astype(BF)


def pair_rows(k):
    return pl.ds(pl.multiple_of(flip(lax.axis_index("y"), k) * PAIR, PAIR), PAIR)


def inside_kernel(*refs):
    pairs, queries, out = refs[:4], refs[4:8], refs[8]
    q, kk, v = refs[9:]
    for k in range(4):
        at = pair_rows(k)
        q[at, :] = queries[k][...]
        kk[at, :] = pairs[k][:, 0:128]
        v[at, :] = pairs[k][:, 128:256]
    T = 256
    lane_q = lax.broadcasted_iota(jnp.int32, (T, 128), 1)
    lane_v = lax.broadcasted_iota(jnp.int32, (LEN, 128), 1)
    causal = lax.broadcasted_iota(jnp.int32, (T, T), 0) >= lax.broadcasted_iota(
        jnp.int32, (T, T), 1
    )
    nt = (((1,), (1,)), ((), ()))
    vh = [jnp.where((lane_v >= HS) if h else (lane_v < HS), v[...], jnp.zeros((), BF)) for h in range(2)]
    for i in range(LEN // T):
        rows = slice(i * T, (i + 1) * T)
        total = None
        for h in range(2):
            qh = jnp.where((lane_q >= HS) if h else (lane_q < HS), q[rows, :], jnp.zeros((), BF))
            last = lax.dot_general(qh, kk[rows, :], nt, preferred_element_type=F32)
            last = jnp.where(causal, last * last, 0.0).astype(BF)
            add = jnp.dot(last, vh[h][rows], preferred_element_type=F32)
            total = add if total is None else total + add
            if i:
                full = lax.dot_general(qh, kk[0 : i * T, :], nt, preferred_element_type=F32)
                full = (full * full).astype(BF)
                total = total + jnp.dot(full, vh[h][0 : i * T], preferred_element_type=F32)
        out[rows, :] = total


def total_kernel(*refs):
    pieces, out = refs[:4], refs[5]
    out[...] = sum(p[...].astype(F32) for p in pieces).astype(BF)


def combine_kernel(*refs):
    pieces, totals, outs = refs[:4], refs[4:8], refs[9:13]
    x, z = lax.axis_index("x"), lax.axis_index("z")
    base = jnp.zeros((PIECE, 128), F32)
    for k in range(1, 4):
        base = base + jnp.where(flip(x, k) < x, totals[k][...].astype(F32), 0.0)
    for k in range(4):
        acc = base
        for j in range(4):
            if j != k:
                acc = acc + jnp.where(flip(z, j) < flip(z, k), pieces[j][...].astype(F32), 0.0)
        outs[k][...] = acc.astype(BF)


def features_kernel(*refs):
    queries, phi, ext = refs[:4], refs[4], refs[5]
    for k in range(4):
        at = pair_rows(k)
        turned = queries[k][...].astype(F32).T
        for h in range(2):
            part = turned[h * HS : (h + 1) * HS]
            ext[h, 0:HS, at] = part
            ext[h, HS : 2 * HS, at] = part
    for h in range(2):
        fill_pairs(ext, h, phi, h * LEN, False)


def apply_kernel(*refs):
    phi, states, inside, gain, outs = refs[0], refs[1:5], refs[5], refs[6], refs[7:11]
    state, done = refs[11:]
    z = lax.axis_index("z")
    for k in range(4):
        row = pl.multiple_of(flip(z, k) * PIECE, 8)
        state[pl.ds(row, PIECE), :] = states[k][...].astype(F32)
    turned_state = state[...].T.astype(BF)
    halves = [
        jnp.dot(
            turned_state[h * HS : (h + 1) * HS],
            phi[:, h * LEN : (h + 1) * LEN],
            preferred_element_type=F32,
        )
        for h in range(2)
    ]
    numer = jnp.concatenate(halves, axis=0).T + inside[...]
    square = numer * numer
    low = lax.broadcasted_iota(jnp.int32, (LEN, 128), 1) < HS
    first = jnp.sum(jnp.where(low, square, 0.0), axis=-1, keepdims=True)
    second = jnp.sum(jnp.where(low, 0.0, square), axis=-1, keepdims=True)
    mean = jnp.where(low, first, second) * (1.0 / HS)
    done[...] = numer * lax.rsqrt(mean + 1e-05) * gain[...]
    for k in range(4):
        outs[k][...] = done[pair_rows(k), :].astype(BF)


def merge_kernel(*refs):
    parts, out = refs[:4], refs[4]
    row = pl.multiple_of((1 - lax.axis_index("c")) * ROWS, ROWS)
    for k in range(4):
        col = pl.multiple_of(flip(lax.axis_index("y"), k) * 128, 128)
        out[:, pl.ds(col, 128)] = parts[k][pl.ds(row, ROWS), :]


FB = 512


def mlp_kernel(*refs):
    parts, other, tok, gain, wo, wi, wf = refs[:4], *refs[4:10]
    att, res = refs[10:12]
    y, c = lax.axis_index("y"), lax.axis_index("c")
    row = pl.multiple_of(c * ROWS, ROWS)
    for k in range(4):
        col = pl.multiple_of((2 * flip(y, k) + c) * 128, 128)
        att[:, pl.ds(col, 128)] = parts[k][pl.ds(row, ROWS), :]
        col = pl.multiple_of((2 * k + 1 - c) * 128, 128)
        att[:, pl.ds(col, 128)] = other[:, k * 128 : (k + 1) * 128]
    stream = tok[...].astype(F32) + jnp.dot(att[...], wo[...], preferred_element_type=F32)
    stream = stream.astype(BF).astype(F32)
    normed = rms(stream, gain[...]).astype(BF)
    acc = stream
    for j in range(FF // FB):
        at = slice(j * FB, (j + 1) * FB)
        u = jnp.dot(normed, wi[:, at], preferred_element_type=F32)
        hidden = 0.5 * u * (1.0 + jnp.tanh(0.7978845608028654 * (u + 0.044715 * u * u * u)))
        acc = acc + jnp.dot(hidden.astype(BF), wf[at, :], preferred_element_type=F32)
    res[...] = acc.astype(BF)


def call(kernel, outs, scratch, specs, limit, name, flops=0, moved=0):
    return pl.pallas_call(
        kernel,
        out_shape=outs,
        in_specs=specs,
        out_specs=jax.tree.map(lambda _: VM, outs),
        scratch_shapes=scratch,
        compiler_params=pltpu.CompilerParams(vmem_limit_bytes=limit * MIB),
        cost_estimate=pl.CostEstimate(flops=flops, bytes_accessed=moved, transcendentals=0),
        name=name,
    )


def arr(*shape, dtype=BF):
    return jax.ShapeDtypeStruct(shape, dtype)


def fixed(array):
    return pltpu.with_memory_space_constraint(array, pltpu.HBM)


ORDER = (1, 3, 2)


def exchange(parts, axis):
    moved = {k: lax.ppermute(parts[k], axis, xor_pairs(4, k)) for k in ORDER}
    return [parts[0]] + [moved[k] for k in range(1, 4)]


def body(tokens, attn_gain, w_query, w_key, w_value, head_gain, w_output, mlp_gain, w_in, w_out):
    swapped = lax.ppermute(tokens, "c", xor_pairs(2, 1))
    own, gain, wkv = call(
        load_kernel,
        [arr(ROWS, D), arr(1, D, dtype=F32), arr(4, D, 256)],
        [
            pltpu.VMEM((ROWS, D), BF),
            pltpu.SemaphoreType.DMA((4, 2)),
            pltpu.SemaphoreType.DMA((2,)),
        ],
        [HBM] * 4,
        4,
        "load",
        flops=128 * 1024 * 1024,
        moved=4 * MIB,
    )(fixed(tokens), fixed(attn_gain.reshape(1, D)), fixed(w_key), fixed(w_value))
    *pairs, normed = call(
        kv_kernel,
        [arr(PAIR, 256)] * 4 + [arr(PAIR, D)],
        [],
        [VM] * 4,
        6,
        "kv",
        flops=2 * 256 * 1024 * 1024,
        moved=3 * MIB,
    )(own, swapped, gain, wkv)
    pairs = exchange(pairs, "y")
    queries = call(
        q_kernel,
        [arr(PAIR, 128)] * 4,
        [pltpu.VMEM((4, D, 128), BF), pltpu.SemaphoreType.DMA((4,))],
        [VM, HBM],
        6,
        "q",
        flops=2 * 256 * 1024 * 512,
        moved=4 * MIB,
    )(normed, fixed(w_query))
    queries = exchange(queries, "y")

    pieces = call(
        state_kernel,
        [arr(PIECE, 128)] * 4,
        [
            pltpu.VMEM((2, 2 * HS, LEN), F32),
            pltpu.VMEM((2 * LEN, 128), BF),
            pltpu.VMEM((NF, 2 * LEN), BF),
            pltpu.VMEM((NF, 128), F32),
        ],
        [VM] * 4,
        20,
        "state",
        flops=2 * NF * 2 * LEN * 256,
        moved=2 * MIB,
    )(*pairs)
    pieces = exchange(pieces, "z")
    inside = call(
        inside_kernel,
        arr(LEN, 128, dtype=F32),
        [pltpu.VMEM((LEN, 128), BF)] * 3,
        [VM] * 8,
        16,
        "inside",
        flops=2 * 1024 * 1024 * 256 * 2,
        moved=2 * MIB,
    )(*pairs, *queries)

    total = call(total_kernel, arr(PIECE, 128), [], [VM] * 4 + [ANY], 4, "total", moved=MIB)(
        *pieces, inside
    )
    moved = {k: lax.ppermute(total, "x", xor_pairs(4, k)) for k in ORDER}
    totals = [total] + [moved[k] for k in range(1, 4)]
    phi = call(
        features_kernel,
        arr(NF, 2 * LEN),
        [pltpu.VMEM((2, 2 * HS, LEN), F32)],
        [VM] * 4,
        6,
        "features",
        flops=NF * 2 * LEN * 128,
        moved=9 * MIB,
    )(*queries)
    states = call(
        combine_kernel, [arr(PIECE, 128)] * 4, [], [VM] * 8 + [ANY], 8, "combine", moved=MIB
    )(*pieces, *totals, phi)
    states = exchange(states, "z")

    parts = call(
        apply_kernel,
        [arr(PAIR, 128)] * 4,
        [
            pltpu.VMEM((NF, 128), F32),
            pltpu.VMEM((LEN, 128), F32),
        ],
        [VM] * 7,
        12,
        "apply",
        flops=2 * NF * 2 * LEN * 256,
        moved=2 * MIB,
    )(phi, *states, inside, head_gain.reshape(1, 128))
    parts = exchange(parts, "y")
    other = call(merge_kernel, arr(ROWS, 512), [], [VM] * 4, 4, "merge")(*parts)
    other = lax.ppermute(other, "c", xor_pairs(2, 1))

    return call(
        mlp_kernel,
        [arr(ROWS, D)] * 2,
        [],
        [VM] * 10,
        8,
        "mlp",
        flops=2 * 128 * 1024 * 9216,
        moved=18 * MIB,
    )(*parts, other, tokens, mlp_gain.reshape(1, D), w_output, w_in, w_out)


def solution(mesh):
    finer = Mesh(mesh.devices.reshape(4, 4, 4, 2), SPLIT)
    placed = (P(SPLIT, None), P(), P(), P(), P(), P(BA), P(), P(), P(), P())
    return jax.shard_map(
        body,
        mesh=finer,
        in_specs=placed,
        out_specs=(P(SPLIT, None), P(SPLIT, None)),
        check_vma=False,
    )
```

```python
import jax
import jax.numpy as jnp
from jax import lax
from jax.experimental import pallas as pl
from jax.experimental.pallas import tpu as pltpu
from jax.sharding import Mesh
from jax.sharding import PartitionSpec as P

D = 1024
FF = 4096
HS = 64
NF = HS * (HS + 1) // 2
PIECE = NF // 4
ROWS = 128
PAIR = 2 * ROWS
LEN = 1024
F32 = jnp.float32
BF = jnp.bfloat16
SPLIT = ("x", "z", "y", "c")
BA = ("y", "c")
MIB = 1 << 20


VM = pl.BlockSpec(memory_space=pltpu.VMEM)
HBM = pl.BlockSpec(memory_space=pltpu.HBM)
ANY = pl.BlockSpec(memory_space=pl.ANY)


def xor_pairs(n, k):
    return [(i, i ^ k) for i in range(n)]


def flip(index, k):
    return jnp.bitwise_xor(index, k) if k else index


def rms(matrix, gain):
    return matrix * lax.rsqrt(jnp.mean(matrix * matrix, axis=-1, keepdims=True) + 1e-05) * gain


def columns(k):
    return pl.multiple_of((2 * flip(lax.axis_index("y"), k) + lax.axis_index("c")) * 128, 128)


def load_kernel(tok, gain, wk, wv, normed, gout, wout, tbuf, sems, tsems):
    first = [
        pltpu.make_async_copy(gain, gout, tsems.at[0]),
        pltpu.make_async_copy(tok, tbuf, tsems.at[1]),
    ]
    for copy in first:
        copy.start()
    copies = []
    for k in range(4):
        for j, w in enumerate((wk, wv)):
            copy = pltpu.make_async_copy(
                w.at[:, pl.ds(columns(k), 128)],
                wout.at[k, :, j * 128 : (j + 1) * 128],
                sems.at[k, j],
            )
            copy.start()
            copies.append(copy)
    for copy in first:
        copy.wait()
    normed[...] = rms(tbuf[...].astype(F32), gout[...]).astype(BF)
    for copy in copies:
        copy.wait()


def kv_kernel(own, other, gain, wkv, *rest):
    outs, normed = rest[:4], rest[4]
    c = lax.axis_index("c")
    normed[pl.ds(pl.multiple_of(c * ROWS, ROWS), ROWS), :] = own[...]
    at = pl.ds(pl.multiple_of((1 - c) * ROWS, ROWS), ROWS)
    normed[at, :] = rms(other[...].astype(F32), gain[...]).astype(BF)
    for k in (1, 3, 2, 0):
        outs[k][...] = jnp.dot(normed[...], wkv[k], preferred_element_type=F32).astype(BF)


def q_kernel(normed, wq, *outs):
    for k in range(4):
        outs[k][...] = jnp.dot(
            normed[...], wq[:, pl.ds(columns(k), 128)], preferred_element_type=F32
        ).astype(BF)


def fill_pairs(ext, h, phi, col, weighted, first=0, last=33):
    for d in range(first, last):
        rows = HS if d < 32 else 32
        left = ext[h, 0:rows, :]
        if weighted and d:
            left = left + left
        phi[d * HS : d * HS + rows, col : col + LEN] = (left * ext[h, d : d + rows, :]).astype(BF)


def state_kernel(*refs):
    chunks, outs = refs[:4], refs[4:8]
    ext, vz, phi, state = refs[8:]
    lane = lax.broadcasted_iota(jnp.int32, (PAIR, 128), 1)
    zero = jnp.zeros((PAIR, 128), BF)
    for k in range(4):
        at = slice(k * PAIR, (k + 1) * PAIR)
        turned = chunks[k][:, 0:128].astype(F32).T
        value = chunks[k][:, 128:256]
        for h in range(2):
            part = turned[h * HS : (h + 1) * HS]
            ext[h, 0:HS, at] = part
            ext[h, HS : 2 * HS, at] = part
            mine = (lane >= HS) if h else (lane < HS)
            vz[h * LEN + k * PAIR : h * LEN + (k + 1) * PAIR, :] = jnp.where(mine, value, zero)
    for first, last in ((0, 8), (8, 16), (16, 24), (24, 33)):
        for h in range(2):
            fill_pairs(ext, h, phi, h * LEN, True, first, last)
        at = slice(first * HS, min(last * HS, NF))
        state[at, :] = jnp.dot(phi[at, :], vz[...], preferred_element_type=F32)
    me = lax.axis_index("z")
    for k in range(4):
        row = pl.multiple_of(flip(me, k) * PIECE, 8)
        outs[k][...] = state[pl.ds(row, PIECE), :].astype(BF)


def pair_rows(k):
    return pl.ds(pl.multiple_of(flip(lax.axis_index("y"), k) * PAIR, PAIR), PAIR)


def inside_kernel(*refs):
    pairs, queries, out = refs[:4], refs[4:8], refs[8]
    q, kk, v = refs[9:]
    for k in range(4):
        at = pair_rows(k)
        q[at, :] = queries[k][...]
        kk[at, :] = pairs[k][:, 0:128]
        v[at, :] = pairs[k][:, 128:256]
    T = 256
    lane_q = lax.broadcasted_iota(jnp.int32, (T, 128), 1)
    lane_v = lax.broadcasted_iota(jnp.int32, (LEN, 128), 1)
    causal = lax.broadcasted_iota(jnp.int32, (T, T), 0) >= lax.broadcasted_iota(
        jnp.int32, (T, T), 1
    )
    nt = (((1,), (1,)), ((), ()))
    vh = [jnp.where((lane_v >= HS) if h else (lane_v < HS), v[...], jnp.zeros((), BF)) for h in range(2)]
    for i in range(LEN // T):
        rows = slice(i * T, (i + 1) * T)
        total = None
        for h in range(2):
            qh = jnp.where((lane_q >= HS) if h else (lane_q < HS), q[rows, :], jnp.zeros((), BF))
            last = lax.dot_general(qh, kk[rows, :], nt, preferred_element_type=F32)
            last = jnp.where(causal, last * last, 0.0).astype(BF)
            add = jnp.dot(last, vh[h][rows], preferred_element_type=F32)
            total = add if total is None else total + add
            if i:
                full = lax.dot_general(qh, kk[0 : i * T, :], nt, preferred_element_type=F32)
                full = (full * full).astype(BF)
                total = total + jnp.dot(full, vh[h][0 : i * T], preferred_element_type=F32)
        out[rows, :] = total


def total_kernel(*refs):
    pieces, out = refs[:4], refs[5]
    out[...] = sum(p[...].astype(F32) for p in pieces).astype(BF)


def combine_kernel(*refs):
    pieces, totals, outs = refs[:4], refs[4:8], refs[9:13]
    x, z = lax.axis_index("x"), lax.axis_index("z")
    base = jnp.zeros((PIECE, 128), F32)
    for k in range(1, 4):
        base = base + jnp.where(flip(x, k) < x, totals[k][...].astype(F32), 0.0)
    for k in range(4):
        acc = base
        for j in range(4):
            if j != k:
                acc = acc + jnp.where(flip(z, j) < flip(z, k), pieces[j][...].astype(F32), 0.0)
        outs[k][...] = acc.astype(BF)


def features_kernel(*refs):
    queries, phi, ext = refs[:4], refs[4], refs[5]
    for k in range(4):
        at = slice(k * PAIR, (k + 1) * PAIR)
        turned = queries[k][...].astype(F32).T
        for h in range(2):
            part = turned[h * HS : (h + 1) * HS]
            ext[h, 0:HS, at] = part
            ext[h, HS : 2 * HS, at] = part
    for h in range(2):
        fill_pairs(ext, h, phi, h * LEN, False)


def attend(turned, phi, inside, gain, first, last):
    halves = [
        jnp.dot(
            turned[h * HS : (h + 1) * HS],
            phi[:, h * LEN + first * PAIR : h * LEN + last * PAIR],
            preferred_element_type=F32,
        )
        for h in range(2)
    ]
    numer = jnp.concatenate(halves, axis=0).T
    low = lax.broadcasted_iota(jnp.int32, (PAIR, 128), 1) < HS
    outs = []
    for k in range(first, last):
        at = slice((k - first) * PAIR, (k - first + 1) * PAIR)
        mine = numer[at] + inside[pair_rows(k), :]
        square = mine * mine
        one = jnp.sum(jnp.where(low, square, 0.0), axis=-1, keepdims=True)
        two = jnp.sum(jnp.where(low, 0.0, square), axis=-1, keepdims=True)
        mean = jnp.where(low, one, two) * (1.0 / HS)
        outs.append((mine * lax.rsqrt(mean + 1e-05) * gain[...]).astype(BF))
    return outs


def apply_kernel(*refs):
    phi, states, inside, gain, outs, turned = refs[0], refs[1:5], refs[5], refs[6], refs[7:10], refs[10]
    state = refs[11]
    z = lax.axis_index("z")
    for k in range(4):
        row = pl.multiple_of(flip(z, k) * PIECE, 8)
        state[pl.ds(row, PIECE), :] = states[k][...].astype(F32)
    turned[...] = state[...].T.astype(BF)
    for out, value in zip(outs, attend(turned[...], phi, inside, gain, 1, 4)):
        out[...] = value


def own_kernel(phi, turned, inside, gain, out):
    out[...] = attend(turned[...], phi, inside, gain, 0, 1)[0]


def merge_kernel(*refs):
    parts, out = refs[:4], refs[4]
    row = pl.multiple_of((1 - lax.axis_index("c")) * ROWS, ROWS)
    for k in range(4):
        col = pl.multiple_of(flip(lax.axis_index("y"), k) * 128, 128)
        out[:, pl.ds(col, 128)] = parts[k][pl.ds(row, ROWS), :]


FB = 2048


def mlp_kernel(*refs):
    parts, other, tok, gain, wo, wi, wf = refs[:4], *refs[4:10]
    att, res = refs[10:12]
    y, c = lax.axis_index("y"), lax.axis_index("c")
    row = pl.multiple_of(c * ROWS, ROWS)
    for k in range(4):
        col = pl.multiple_of((2 * flip(y, k) + c) * 128, 128)
        att[:, pl.ds(col, 128)] = parts[k][pl.ds(row, ROWS), :]
        col = pl.multiple_of((2 * k + 1 - c) * 128, 128)
        att[:, pl.ds(col, 128)] = other[:, k * 128 : (k + 1) * 128]
    stream = tok[...].astype(F32) + jnp.dot(att[...], wo[...], preferred_element_type=F32)
    stream = stream.astype(BF).astype(F32)
    normed = rms(stream, gain[...]).astype(BF)
    acc = stream
    for j in range(FF // FB):
        at = slice(j * FB, (j + 1) * FB)
        u = jnp.dot(normed, wi[:, at], preferred_element_type=F32)
        hidden = 0.5 * u * (1.0 + jnp.tanh(0.7978845608028654 * (u + 0.044715 * u * u * u)))
        acc = acc + jnp.dot(hidden.astype(BF), wf[at, :], preferred_element_type=F32)
    res[...] = acc.astype(BF)


def call(kernel, outs, scratch, specs, limit, name, flops=0, moved=0):
    return pl.pallas_call(
        kernel,
        out_shape=outs,
        in_specs=specs,
        out_specs=jax.tree.map(lambda _: VM, outs),
        scratch_shapes=scratch,
        compiler_params=pltpu.CompilerParams(vmem_limit_bytes=limit * MIB),
        cost_estimate=pl.CostEstimate(flops=flops, bytes_accessed=moved, transcendentals=0),
        name=name,
    )


def arr(*shape, dtype=BF):
    return jax.ShapeDtypeStruct(shape, dtype)


def fixed(array):
    return pltpu.with_memory_space_constraint(array, pltpu.HBM)


ORDER = (1, 3, 2)


def exchange(parts, axis):
    moved = {k: lax.ppermute(parts[k], axis, xor_pairs(4, k)) for k in ORDER}
    return [parts[0]] + [moved[k] for k in range(1, 4)]


def body(tokens, attn_gain, w_query, w_key, w_value, head_gain, w_output, mlp_gain, w_in, w_out):
    swapped = lax.ppermute(tokens, "c", xor_pairs(2, 1))
    own, gain, wkv = call(
        load_kernel,
        [arr(ROWS, D), arr(1, D, dtype=F32), arr(4, D, 256)],
        [
            pltpu.VMEM((ROWS, D), BF),
            pltpu.SemaphoreType.DMA((4, 2)),
            pltpu.SemaphoreType.DMA((2,)),
        ],
        [HBM] * 4,
        4,
        "load",
        flops=128 * 1024 * 1024,
        moved=4 * MIB,
    )(fixed(tokens), fixed(attn_gain.reshape(1, D)), fixed(w_key), fixed(w_value))
    *pairs, normed = call(
        kv_kernel,
        [arr(PAIR, 256)] * 4 + [arr(PAIR, D)],
        [],
        [VM] * 4,
        6,
        "kv",
        flops=2 * 256 * 1024 * 1024,
        moved=3 * MIB,
    )(own, swapped, gain, wkv)
    pairs = exchange(pairs, "y")
    queries = call(
        q_kernel,
        [arr(PAIR, 128)] * 4,
        [],
        [VM] * 2,
        4,
        "q",
        flops=2 * 256 * 1024 * 512,
        moved=4 * MIB,
    )(normed, w_query)
    queries = exchange(queries, "y")

    pieces = call(
        state_kernel,
        [arr(PIECE, 128)] * 4,
        [
            pltpu.VMEM((2, 2 * HS, LEN), F32),
            pltpu.VMEM((2 * LEN, 128), BF),
            pltpu.VMEM((NF, 2 * LEN), BF),
            pltpu.VMEM((NF, 128), F32),
        ],
        [VM] * 4,
        20,
        "state",
        flops=2 * NF * 2 * LEN * 256,
        moved=2 * MIB,
    )(*pairs)
    pieces = exchange(pieces, "z")
    inside = call(
        inside_kernel,
        arr(LEN, 128, dtype=F32),
        [pltpu.VMEM((LEN, 128), BF)] * 3,
        [VM] * 8,
        16,
        "inside",
        flops=2 * 1024 * 1024 * 256 * 2,
        moved=2 * MIB,
    )(*pairs, *queries)

    total = call(total_kernel, arr(PIECE, 128), [], [VM] * 4 + [ANY], 4, "total", moved=MIB)(
        *pieces, inside
    )
    moved = {k: lax.ppermute(total, "x", xor_pairs(4, k)) for k in ORDER}
    totals = [total] + [moved[k] for k in range(1, 4)]
    phi = call(
        features_kernel,
        arr(NF, 2 * LEN),
        [pltpu.VMEM((2, 2 * HS, LEN), F32)],
        [VM] * 4,
        6,
        "features",
        flops=NF * 2 * LEN * 128,
        moved=9 * MIB,
    )(*queries)
    states = call(
        combine_kernel, [arr(PIECE, 128)] * 4, [], [VM] * 8 + [ANY], 8, "combine", moved=MIB
    )(*pieces, *totals, phi)
    states = exchange(states, "z")

    scale = head_gain.reshape(1, 128)
    *parts, turned = call(
        apply_kernel,
        [arr(PAIR, 128)] * 3 + [arr(128, NF)],
        [pltpu.VMEM((NF, 128), F32)],
        [VM] * 7,
        12,
        "apply",
        flops=2 * NF * 2 * LEN * 192,
        moved=2 * MIB,
    )(phi, *states, inside, scale)
    moved = {k: lax.ppermute(parts[k - 1], "y", xor_pairs(4, k)) for k in ORDER}
    mine = call(
        own_kernel,
        arr(PAIR, 128),
        [],
        [VM] * 4,
        8,
        "own",
        flops=2 * NF * 2 * LEN * 64,
        moved=2 * MIB,
    )(phi, turned, inside, scale)
    parts = [mine] + [moved[k] for k in range(1, 4)]
    other = call(merge_kernel, arr(ROWS, 512), [], [VM] * 4, 4, "merge")(*parts)
    other = lax.ppermute(other, "c", xor_pairs(2, 1))

    return call(
        mlp_kernel,
        [arr(ROWS, D)] * 2,
        [],
        [VM] * 10,
        8,
        "mlp",
        flops=2 * 128 * 1024 * 9216,
        moved=18 * MIB,
    )(*parts, other, tokens, mlp_gain.reshape(1, D), w_output, w_in, w_out)


def solution(mesh):
    finer = Mesh(mesh.devices.reshape(4, 4, 4, 2), SPLIT)
    placed = (P(SPLIT, None), P(), P(), P(), P(), P(BA), P(), P(), P(), P())
    return jax.shard_map(
        body,
        mesh=finer,
        in_specs=placed,
        out_specs=(P(SPLIT, None), P(SPLIT, None)),
        check_vma=False,
    )
```

```python
import jax
import jax.numpy as jnp
from jax import lax
from jax.experimental import pallas as pl
from jax.experimental.pallas import tpu as pltpu
from jax.sharding import Mesh
from jax.sharding import PartitionSpec as P

D = 1024
FF = 4096
HS = 64
NF = HS * (HS + 1) // 2
PIECE = NF // 4
ROWS = 128
PAIR = 2 * ROWS
LEN = 1024
F32 = jnp.float32
BF = jnp.bfloat16
SPLIT = ("x", "z", "y", "c")
BA = ("y", "c")
MIB = 1 << 20


VM = pl.BlockSpec(memory_space=pltpu.VMEM)
HBM = pl.BlockSpec(memory_space=pltpu.HBM)
ANY = pl.BlockSpec(memory_space=pl.ANY)


def xor_pairs(n, k):
    return [(i, i ^ k) for i in range(n)]


def flip(index, k):
    return jnp.bitwise_xor(index, k) if k else index


def rms(matrix, gain):
    return matrix * lax.rsqrt(jnp.mean(matrix * matrix, axis=-1, keepdims=True) + 1e-05) * gain


def columns(k):
    return pl.multiple_of((2 * flip(lax.axis_index("y"), k) + lax.axis_index("c")) * 128, 128)


def load_kernel(tok, gain, wk, wv, normed, gout, wout, tbuf, sems, tsems):
    first = [
        pltpu.make_async_copy(gain, gout, tsems.at[0]),
        pltpu.make_async_copy(tok, tbuf, tsems.at[1]),
    ]
    for copy in first:
        copy.start()
    copies = []
    for k in range(4):
        for j, w in enumerate((wk, wv)):
            copy = pltpu.make_async_copy(
                w.at[:, pl.ds(columns(k), 128)],
                wout.at[k, :, j * 128 : (j + 1) * 128],
                sems.at[k, j],
            )
            copy.start()
            copies.append(copy)
    for copy in first:
        copy.wait()
    normed[...] = rms(tbuf[...].astype(F32), gout[...]).astype(BF)
    for copy in copies:
        copy.wait()


def kv_kernel(own, other, gain, wkv, *rest):
    outs, normed = rest[:4], rest[4]
    c = lax.axis_index("c")
    normed[pl.ds(pl.multiple_of(c * ROWS, ROWS), ROWS), :] = own[...]
    at = pl.ds(pl.multiple_of((1 - c) * ROWS, ROWS), ROWS)
    normed[at, :] = rms(other[...].astype(F32), gain[...]).astype(BF)
    for k in (1, 3, 2, 0):
        outs[k][...] = jnp.dot(normed[...], wkv[k], preferred_element_type=F32).astype(BF)


def q_kernel(normed, wq, *outs):
    for k in range(4):
        outs[k][...] = jnp.dot(
            normed[...], wq[:, pl.ds(columns(k), 128)], preferred_element_type=F32
        ).astype(BF)


def fill_pairs(ext, h, phi, col, weighted, first=0, last=33):
    for d in range(first, last):
        rows = HS if d < 32 else 32
        left = ext[h, 0:rows, :]
        if weighted and d:
            left = left + left
        phi[d * HS : d * HS + rows, col : col + LEN] = (left * ext[h, d : d + rows, :]).astype(BF)


def state_kernel(*refs):
    chunks, outs = refs[:4], refs[4:8]
    ext, vz, phi, state = refs[8:]
    lane = lax.broadcasted_iota(jnp.int32, (PAIR, 128), 1)
    zero = jnp.zeros((PAIR, 128), BF)
    for k in range(4):
        at = slice(k * PAIR, (k + 1) * PAIR)
        turned = chunks[k][:, 0:128].astype(F32).T
        value = chunks[k][:, 128:256]
        for h in range(2):
            part = turned[h * HS : (h + 1) * HS]
            ext[h, 0:HS, at] = part
            ext[h, HS : 2 * HS, at] = part
            mine = (lane >= HS) if h else (lane < HS)
            vz[h * LEN + k * PAIR : h * LEN + (k + 1) * PAIR, :] = jnp.where(mine, value, zero)
    for first, last in ((0, 8), (8, 16), (16, 24), (24, 33)):
        for h in range(2):
            fill_pairs(ext, h, phi, h * LEN, True, first, last)
        at = slice(first * HS, min(last * HS, NF))
        state[at, :] = jnp.dot(phi[at, :], vz[...], preferred_element_type=F32)
    me = lax.axis_index("z")
    for k in range(4):
        row = pl.multiple_of(flip(me, k) * PIECE, 8)
        outs[k][...] = state[pl.ds(row, PIECE), :].astype(BF)


def pair_rows(k):
    return pl.ds(pl.multiple_of(flip(lax.axis_index("y"), k) * PAIR, PAIR), PAIR)


def inside_kernel(*refs):
    pairs, queries, out = refs[:4], refs[4:8], refs[8]
    q, kk, v = refs[9:]
    for k in range(4):
        at = pair_rows(k)
        q[at, :] = queries[k][...]
        kk[at, :] = pairs[k][:, 0:128]
        v[at, :] = pairs[k][:, 128:256]
    T = 256
    lane_q = lax.broadcasted_iota(jnp.int32, (T, 128), 1)
    lane_v = lax.broadcasted_iota(jnp.int32, (LEN, 128), 1)
    causal = lax.broadcasted_iota(jnp.int32, (T, T), 0) >= lax.broadcasted_iota(
        jnp.int32, (T, T), 1
    )
    nt = (((1,), (1,)), ((), ()))
    vh = [jnp.where((lane_v >= HS) if h else (lane_v < HS), v[...], jnp.zeros((), BF)) for h in range(2)]
    for i in range(LEN // T):
        rows = slice(i * T, (i + 1) * T)
        total = None
        for h in range(2):
            qh = jnp.where((lane_q >= HS) if h else (lane_q < HS), q[rows, :], jnp.zeros((), BF))
            last = lax.dot_general(qh, kk[rows, :], nt, preferred_element_type=F32)
            last = jnp.where(causal, last * last, 0.0).astype(BF)
            add = jnp.dot(last, vh[h][rows], preferred_element_type=F32)
            total = add if total is None else total + add
            if i:
                full = lax.dot_general(qh, kk[0 : i * T, :], nt, preferred_element_type=F32)
                full = (full * full).astype(BF)
                total = total + jnp.dot(full, vh[h][0 : i * T], preferred_element_type=F32)
        out[rows, :] = total


def total_kernel(*refs):
    pieces, out = refs[:4], refs[4]
    out[...] = sum(p[...].astype(F32) for p in pieces).astype(BF)


def combine_kernel(*refs):
    pieces, totals, outs = refs[:4], refs[4:8], refs[10:14]
    x, z = lax.axis_index("x"), lax.axis_index("z")
    base = jnp.zeros((PIECE, 128), F32)
    for k in range(1, 4):
        base = base + jnp.where(flip(x, k) < x, totals[k][...].astype(F32), 0.0)
    for k in range(4):
        acc = base
        for j in range(4):
            if j != k:
                acc = acc + jnp.where(flip(z, j) < flip(z, k), pieces[j][...].astype(F32), 0.0)
        outs[k][...] = acc.astype(BF)


def features_kernel(*refs):
    queries, phi, ext = refs[:4], refs[4], refs[5]
    for k in range(4):
        at = slice(k * PAIR, (k + 1) * PAIR)
        turned = queries[k][...].astype(F32).T
        for h in range(2):
            part = turned[h * HS : (h + 1) * HS]
            ext[h, 0:HS, at] = part
            ext[h, HS : 2 * HS, at] = part
    for h in range(2):
        fill_pairs(ext, h, phi, h * LEN, False)


def attend(turned, phi, inside, gain, first, last):
    halves = [
        jnp.dot(
            turned[h * HS : (h + 1) * HS],
            phi[:, h * LEN + first * PAIR : h * LEN + last * PAIR],
            preferred_element_type=F32,
        )
        for h in range(2)
    ]
    numer = jnp.concatenate(halves, axis=0).T
    low = lax.broadcasted_iota(jnp.int32, (PAIR, 128), 1) < HS
    outs = []
    for k in range(first, last):
        at = slice((k - first) * PAIR, (k - first + 1) * PAIR)
        mine = numer[at] + inside[pair_rows(k), :]
        square = mine * mine
        one = jnp.sum(jnp.where(low, square, 0.0), axis=-1, keepdims=True)
        two = jnp.sum(jnp.where(low, 0.0, square), axis=-1, keepdims=True)
        mean = jnp.where(low, one, two) * (1.0 / HS)
        outs.append((mine * lax.rsqrt(mean + 1e-05) * gain[...]).astype(BF))
    return outs


def apply_kernel(*refs):
    phi, states, inside, gain, outs, turned = refs[0], refs[1:5], refs[5], refs[6], refs[7:10], refs[10]
    state = refs[11]
    z = lax.axis_index("z")
    for k in range(4):
        row = pl.multiple_of(flip(z, k) * PIECE, 8)
        state[pl.ds(row, PIECE), :] = states[k][...].astype(F32)
    turned[...] = state[...].T.astype(BF)
    for out, value in zip(outs, attend(turned[...], phi, inside, gain, 1, 4)):
        out[...] = value


def own_kernel(phi, turned, inside, gain, out):
    out[...] = attend(turned[...], phi, inside, gain, 0, 1)[0]


def merge_kernel(*refs):
    parts, out = refs[:4], refs[4]
    row = pl.multiple_of((1 - lax.axis_index("c")) * ROWS, ROWS)
    for k in range(4):
        col = pl.multiple_of(flip(lax.axis_index("y"), k) * 128, 128)
        out[:, pl.ds(col, 128)] = parts[k][pl.ds(row, ROWS), :]


FB = 2048


def mlp_kernel(*refs):
    parts, other, tok, gain, wo, wi, wf = refs[:4], *refs[4:10]
    att, res = refs[10:12]
    y, c = lax.axis_index("y"), lax.axis_index("c")
    row = pl.multiple_of(c * ROWS, ROWS)
    for k in range(4):
        col = pl.multiple_of((2 * flip(y, k) + c) * 128, 128)
        att[:, pl.ds(col, 128)] = parts[k][pl.ds(row, ROWS), :]
        col = pl.multiple_of((2 * k + 1 - c) * 128, 128)
        att[:, pl.ds(col, 128)] = other[:, k * 128 : (k + 1) * 128]
    stream = tok[...].astype(F32) + jnp.dot(att[...], wo[...], preferred_element_type=F32)
    stream = stream.astype(BF).astype(F32)
    normed = rms(stream, gain[...]).astype(BF)
    acc = stream
    for j in range(FF // FB):
        at = slice(j * FB, (j + 1) * FB)
        u = jnp.dot(normed, wi[:, at], preferred_element_type=F32)
        hidden = 0.5 * u * (1.0 + jnp.tanh(0.7978845608028654 * (u + 0.044715 * u * u * u)))
        acc = acc + jnp.dot(hidden.astype(BF), wf[at, :], preferred_element_type=F32)
    res[...] = acc.astype(BF)


def call(kernel, outs, scratch, specs, limit, name, flops=0, moved=0):
    return pl.pallas_call(
        kernel,
        out_shape=outs,
        in_specs=specs,
        out_specs=jax.tree.map(lambda _: VM, outs),
        scratch_shapes=scratch,
        compiler_params=pltpu.CompilerParams(vmem_limit_bytes=limit * MIB),
        cost_estimate=pl.CostEstimate(flops=flops, bytes_accessed=moved, transcendentals=0),
        name=name,
    )


def arr(*shape, dtype=BF):
    return jax.ShapeDtypeStruct(shape, dtype)


def fixed(array):
    return pltpu.with_memory_space_constraint(array, pltpu.HBM)


ORDER = (2, 3, 1)


def exchange(parts, axis):
    moved = {k: lax.ppermute(parts[k], axis, xor_pairs(4, k)) for k in ORDER}
    return [parts[0]] + [moved[k] for k in range(1, 4)]


def body(tokens, attn_gain, w_query, w_key, w_value, head_gain, w_output, mlp_gain, w_in, w_out):
    swapped = lax.ppermute(tokens, "c", xor_pairs(2, 1))
    own, gain, wkv = call(
        load_kernel,
        [arr(ROWS, D), arr(1, D, dtype=F32), arr(4, D, 256)],
        [
            pltpu.VMEM((ROWS, D), BF),
            pltpu.SemaphoreType.DMA((4, 2)),
            pltpu.SemaphoreType.DMA((2,)),
        ],
        [HBM] * 4,
        4,
        "load",
        flops=128 * 1024 * 1024,
        moved=4 * MIB,
    )(fixed(tokens), fixed(attn_gain.reshape(1, D)), fixed(w_key), fixed(w_value))
    *pairs, normed = call(
        kv_kernel,
        [arr(PAIR, 256)] * 4 + [arr(PAIR, D)],
        [],
        [VM] * 4,
        6,
        "kv",
        flops=2 * 256 * 1024 * 1024,
        moved=3 * MIB,
    )(own, swapped, gain, wkv)
    pairs = exchange(pairs, "y")
    queries = call(
        q_kernel,
        [arr(PAIR, 128)] * 4,
        [],
        [VM] * 2,
        4,
        "q",
        flops=2 * 256 * 1024 * 512,
        moved=4 * MIB,
    )(normed, w_query)
    pieces = call(
        state_kernel,
        [arr(PIECE, 128)] * 4,
        [
            pltpu.VMEM((2, 2 * HS, LEN), F32),
            pltpu.VMEM((2 * LEN, 128), BF),
            pltpu.VMEM((NF, 2 * LEN), BF),
            pltpu.VMEM((NF, 128), F32),
        ],
        [VM] * 4,
        20,
        "state",
        flops=2 * NF * 2 * LEN * 256,
        moved=2 * MIB,
    )(*pairs)
    pieces, queries = lax.optimization_barrier((pieces, queries))
    pieces = exchange(pieces, "z")
    queries = exchange(queries, "y")
    inside = call(
        inside_kernel,
        arr(LEN, 128, dtype=F32),
        [pltpu.VMEM((LEN, 128), BF)] * 3,
        [VM] * 8,
        16,
        "inside",
        flops=2 * 1024 * 1024 * 256 * 2,
        moved=2 * MIB,
    )(*pairs, *queries)

    total = call(total_kernel, arr(PIECE, 128), [], [VM] * 4, 4, "total", moved=MIB)(*pieces)
    moved = {k: lax.ppermute(total, "x", xor_pairs(4, k)) for k in ORDER}
    totals = [total] + [moved[k] for k in range(1, 4)]
    phi = call(
        features_kernel,
        arr(NF, 2 * LEN),
        [pltpu.VMEM((2, 2 * HS, LEN), F32)],
        [VM] * 4,
        6,
        "features",
        flops=NF * 2 * LEN * 128,
        moved=9 * MIB,
    )(*queries)
    states = call(
        combine_kernel, [arr(PIECE, 128)] * 4, [], [VM] * 8 + [ANY] * 2, 8, "combine", moved=MIB
    )(*pieces, *totals, phi, inside)
    states = exchange(states, "z")

    scale = head_gain.reshape(1, 128)
    *parts, turned = call(
        apply_kernel,
        [arr(PAIR, 128)] * 3 + [arr(128, NF)],
        [pltpu.VMEM((NF, 128), F32)],
        [VM] * 7,
        12,
        "apply",
        flops=2 * NF * 2 * LEN * 192,
        moved=2 * MIB,
    )(phi, *states, inside, scale)
    moved = {k: lax.ppermute(parts[k - 1], "y", xor_pairs(4, k)) for k in ORDER}
    mine = call(
        own_kernel,
        arr(PAIR, 128),
        [],
        [VM] * 4,
        8,
        "own",
        flops=2 * NF * 2 * LEN * 64,
        moved=2 * MIB,
    )(phi, turned, inside, scale)
    parts = [mine] + [moved[k] for k in range(1, 4)]
    other = call(merge_kernel, arr(ROWS, 512), [], [VM] * 4, 4, "merge")(*parts)
    other = lax.ppermute(other, "c", xor_pairs(2, 1))

    return call(
        mlp_kernel,
        [arr(ROWS, D)] * 2,
        [],
        [VM] * 10,
        8,
        "mlp",
        flops=2 * 128 * 1024 * 9216,
        moved=18 * MIB,
    )(*parts, other, tokens, mlp_gain.reshape(1, D), w_output, w_in, w_out)


def solution(mesh):
    finer = Mesh(mesh.devices.reshape(4, 4, 4, 2), SPLIT)
    placed = (P(SPLIT, None), P(), P(), P(), P(), P(BA), P(), P(), P(), P())
    return jax.shard_map(
        body,
        mesh=finer,
        in_specs=placed,
        out_specs=(P(SPLIT, None), P(SPLIT, None)),
        check_vma=False,
    )
```

```python
import jax
import jax.numpy as jnp
from jax import lax
from jax.experimental import pallas as pl
from jax.experimental.pallas import tpu as pltpu
from jax.sharding import Mesh
from jax.sharding import PartitionSpec as P

D = 1024
FF = 4096
HS = 64
NF = HS * (HS + 1) // 2
PIECE = NF // 4
ROWS = 128
PAIR = 2 * ROWS
LEN = 1024
F32 = jnp.float32
BF = jnp.bfloat16
SPLIT = ("x", "z", "y", "c")
BA = ("y", "c")
MIB = 1 << 20


VM = pl.BlockSpec(memory_space=pltpu.VMEM)
HBM = pl.BlockSpec(memory_space=pltpu.HBM)
ANY = pl.BlockSpec(memory_space=pl.ANY)


CROSS = 2


def hop(array, axis, k):
    over = 1 if k & CROSS else 0
    pairs = [(2 * i + c, 2 * (i ^ k) + (c ^ over)) for i in range(4) for c in range(2)]
    return lax.ppermute(array, (axis, "c"), pairs)


def other_core(array):
    return lax.ppermute(array, "c", [(0, 1), (1, 0)])


def crossed():
    bits = lax.axis_index("x") // CROSS + lax.axis_index("y") // CROSS + lax.axis_index("z") // CROSS
    return lax.rem(bits, 2)


def parity():
    return lax.rem(lax.axis_index("c") + crossed(), 2)


def flip(index, k):
    return jnp.bitwise_xor(index, k) if k else index


def rms(matrix, gain):
    return matrix * lax.rsqrt(jnp.mean(matrix * matrix, axis=-1, keepdims=True) + 1e-05) * gain


def columns(k):
    return pl.multiple_of((2 * flip(lax.axis_index("y"), k) + parity()) * 128, 128)


def load_kernel(tok, gain, wk, wv, normed, gout, wout, tbuf, sems, tsems):
    first = [
        pltpu.make_async_copy(gain, gout, tsems.at[0]),
        pltpu.make_async_copy(tok, tbuf, tsems.at[1]),
    ]
    for copy in first:
        copy.start()
    copies = []
    for k in range(4):
        for j, w in enumerate((wk, wv)):
            copy = pltpu.make_async_copy(
                w.at[:, pl.ds(columns(k), 128)],
                wout.at[k, :, j * 128 : (j + 1) * 128],
                sems.at[k, j],
            )
            copy.start()
            copies.append(copy)
    for copy in first:
        copy.wait()
    normed[...] = rms(tbuf[...].astype(F32), gout[...]).astype(BF)
    for copy in copies:
        copy.wait()


def kv_kernel(own, other, gain, wkv, after, *rest):
    outs, normed = rest[:4], rest[4]
    c = lax.axis_index("c")
    normed[pl.ds(pl.multiple_of(c * ROWS, ROWS), ROWS), :] = own[...]
    at = pl.ds(pl.multiple_of((1 - c) * ROWS, ROWS), ROWS)
    normed[at, :] = rms(other[...].astype(F32), gain[...]).astype(BF)
    for k in (1, 3, 2, 0):
        outs[k][...] = jnp.dot(normed[...], wkv[k], preferred_element_type=F32).astype(BF)


def q_kernel(normed, wq, *outs):
    for k in range(4):
        outs[k][...] = jnp.dot(
            normed[...], wq[:, pl.ds(columns(k), 128)], preferred_element_type=F32
        ).astype(BF)


def fill_pairs(ext, h, phi, col, weighted, first=0, last=33):
    for d in range(first, last):
        rows = HS if d < 32 else 32
        left = ext[h, 0:rows, :]
        if weighted and d:
            left = left + left
        phi[d * HS : d * HS + rows, col : col + LEN] = (left * ext[h, d : d + rows, :]).astype(BF)


def state_kernel(*refs):
    chunks, outs = refs[:4], refs[4:8]
    ext, vz, phi, state = refs[8:]
    lane = lax.broadcasted_iota(jnp.int32, (PAIR, 128), 1)
    zero = jnp.zeros((PAIR, 128), BF)
    for k in range(4):
        at = slice(k * PAIR, (k + 1) * PAIR)
        turned = chunks[k][:, 0:128].astype(F32).T
        value = chunks[k][:, 128:256]
        for h in range(2):
            part = turned[h * HS : (h + 1) * HS]
            ext[h, 0:HS, at] = part
            ext[h, HS : 2 * HS, at] = part
            mine = (lane >= HS) if h else (lane < HS)
            vz[h * LEN + k * PAIR : h * LEN + (k + 1) * PAIR, :] = jnp.where(mine, value, zero)
    for first, last in ((0, 8), (8, 16), (16, 24), (24, 33)):
        for h in range(2):
            fill_pairs(ext, h, phi, h * LEN, True, first, last)
        at = slice(first * HS, min(last * HS, NF))
        state[at, :] = jnp.dot(phi[at, :], vz[...], preferred_element_type=F32)
    me = lax.axis_index("z")
    for k in range(4):
        row = pl.multiple_of(flip(me, k) * PIECE, 8)
        outs[k][...] = state[pl.ds(row, PIECE), :].astype(BF)


def pair_rows(k):
    return pl.ds(pl.multiple_of(flip(lax.axis_index("y"), k) * PAIR, PAIR), PAIR)


def inside_kernel(*refs):
    pairs, queries, out = refs[:4], refs[4:8], refs[8]
    q, kk, v = refs[9:]
    for k in range(4):
        at = pair_rows(k)
        q[at, :] = queries[k][...]
        kk[at, :] = pairs[k][:, 0:128]
        v[at, :] = pairs[k][:, 128:256]
    T = 256
    lane_q = lax.broadcasted_iota(jnp.int32, (T, 128), 1)
    lane_v = lax.broadcasted_iota(jnp.int32, (LEN, 128), 1)
    causal = lax.broadcasted_iota(jnp.int32, (T, T), 0) >= lax.broadcasted_iota(
        jnp.int32, (T, T), 1
    )
    nt = (((1,), (1,)), ((), ()))
    vh = [jnp.where((lane_v >= HS) if h else (lane_v < HS), v[...], jnp.zeros((), BF)) for h in range(2)]
    for i in range(LEN // T):
        rows = slice(i * T, (i + 1) * T)
        total = None
        for h in range(2):
            qh = jnp.where((lane_q >= HS) if h else (lane_q < HS), q[rows, :], jnp.zeros((), BF))
            last = lax.dot_general(qh, kk[rows, :], nt, preferred_element_type=F32)
            last = jnp.where(causal, last * last, 0.0).astype(BF)
            add = jnp.dot(last, vh[h][rows], preferred_element_type=F32)
            total = add if total is None else total + add
            if i:
                full = lax.dot_general(qh, kk[0 : i * T, :], nt, preferred_element_type=F32)
                full = (full * full).astype(BF)
                total = total + jnp.dot(full, vh[h][0 : i * T], preferred_element_type=F32)
        out[rows, :] = total


def total_kernel(*refs):
    pieces, out = refs[:4], refs[4]
    out[...] = sum(p[...].astype(F32) for p in pieces).astype(BF)


def combine_kernel(*refs):
    pieces, totals, outs = refs[:4], refs[4:8], refs[10:14]
    x, z = lax.axis_index("x"), lax.axis_index("z")
    base = jnp.zeros((PIECE, 128), F32)
    for k in range(1, 4):
        base = base + jnp.where(flip(x, k) < x, totals[k][...].astype(F32), 0.0)
    for k in range(4):
        acc = base
        for j in range(4):
            if j != k:
                acc = acc + jnp.where(flip(z, j) < flip(z, k), pieces[j][...].astype(F32), 0.0)
        outs[k][...] = acc.astype(BF)


def features_kernel(*refs):
    queries, phi, ext = refs[:4], refs[4], refs[5]
    for k in range(4):
        at = slice(k * PAIR, (k + 1) * PAIR)
        turned = queries[k][...].astype(F32).T
        for h in range(2):
            part = turned[h * HS : (h + 1) * HS]
            ext[h, 0:HS, at] = part
            ext[h, HS : 2 * HS, at] = part
    for h in range(2):
        fill_pairs(ext, h, phi, h * LEN, False)


def attend(turned, phi, inside, gains, first, last):
    gain = jnp.where(crossed() == 1, gains[1][...], gains[0][...])
    halves = [
        jnp.dot(
            turned[h * HS : (h + 1) * HS],
            phi[:, h * LEN + first * PAIR : h * LEN + last * PAIR],
            preferred_element_type=F32,
        )
        for h in range(2)
    ]
    numer = jnp.concatenate(halves, axis=0).T
    low = lax.broadcasted_iota(jnp.int32, (PAIR, 128), 1) < HS
    outs = []
    for k in range(first, last):
        at = slice((k - first) * PAIR, (k - first + 1) * PAIR)
        mine = numer[at] + inside[pair_rows(k), :]
        square = mine * mine
        one = jnp.sum(jnp.where(low, square, 0.0), axis=-1, keepdims=True)
        two = jnp.sum(jnp.where(low, 0.0, square), axis=-1, keepdims=True)
        mean = jnp.where(low, one, two) * (1.0 / HS)
        outs.append((mine * lax.rsqrt(mean + 1e-05) * gain).astype(BF))
    return outs


def apply_kernel(*refs):
    phi, states, inside, gains = refs[0], refs[1:5], refs[5], refs[6:8]
    outs, turned, state = refs[8:11], refs[11], refs[12]
    z = lax.axis_index("z")
    for k in range(4):
        row = pl.multiple_of(flip(z, k) * PIECE, 8)
        state[pl.ds(row, PIECE), :] = states[k][...].astype(F32)
    turned[...] = state[...].T.astype(BF)
    for out, value in zip(outs, attend(turned[...], phi, inside, gains, 1, 4)):
        out[...] = value


def own_kernel(phi, turned, inside, gain, gain_other, out):
    out[...] = attend(turned[...], phi, inside, (gain, gain_other), 0, 1)[0]


def merge_kernel(*refs):
    parts, out = refs[:4], refs[4]
    row = pl.multiple_of((1 - lax.axis_index("c")) * ROWS, ROWS)
    for k in range(4):
        col = pl.multiple_of(flip(lax.axis_index("y"), k) * 128, 128)
        out[:, pl.ds(col, 128)] = parts[k][pl.ds(row, ROWS), :]


FB = 2048


def mlp_kernel(*refs):
    parts, other, tok, gain, wo, wi, wf = refs[:4], *refs[4:10]
    att, res = refs[10:12]
    row = pl.multiple_of(lax.axis_index("c") * ROWS, ROWS)
    for k in range(4):
        att[:, pl.ds(columns(k), 128)] = parts[k][pl.ds(row, ROWS), :]
        col = pl.multiple_of((2 * k + 1 - parity()) * 128, 128)
        att[:, pl.ds(col, 128)] = other[:, k * 128 : (k + 1) * 128]
    stream = tok[...].astype(F32) + jnp.dot(att[...], wo[...], preferred_element_type=F32)
    stream = stream.astype(BF).astype(F32)
    normed = rms(stream, gain[...]).astype(BF)
    acc = stream
    for j in range(FF // FB):
        at = slice(j * FB, (j + 1) * FB)
        u = jnp.dot(normed, wi[:, at], preferred_element_type=F32)
        hidden = 0.5 * u * (1.0 + jnp.tanh(0.7978845608028654 * (u + 0.044715 * u * u * u)))
        acc = acc + jnp.dot(hidden.astype(BF), wf[at, :], preferred_element_type=F32)
    res[...] = acc.astype(BF)


def call(kernel, outs, scratch, specs, limit, name, flops=0, moved=0):
    return pl.pallas_call(
        kernel,
        out_shape=outs,
        in_specs=specs,
        out_specs=jax.tree.map(lambda _: VM, outs),
        scratch_shapes=scratch,
        compiler_params=pltpu.CompilerParams(vmem_limit_bytes=limit * MIB),
        cost_estimate=pl.CostEstimate(flops=flops, bytes_accessed=moved, transcendentals=0),
        name=name,
    )


def arr(*shape, dtype=BF):
    return jax.ShapeDtypeStruct(shape, dtype)


def fixed(array):
    return pltpu.with_memory_space_constraint(array, pltpu.HBM)


ORDER = (2, 3, 1)


def exchange(parts, axis):
    moved = {k: hop(parts[k], axis, k) for k in ORDER}
    return [parts[0]] + [moved[k] for k in range(1, 4)]


def body(tokens, attn_gain, w_query, w_key, w_value, head_gain, w_output, mlp_gain, w_in, w_out):
    swapped = other_core(tokens)
    gain_here = head_gain.reshape(1, 128)
    gain_there = other_core(gain_here)
    own, gain, wkv = call(
        load_kernel,
        [arr(ROWS, D), arr(1, D, dtype=F32), arr(4, D, 256)],
        [
            pltpu.VMEM((ROWS, D), BF),
            pltpu.SemaphoreType.DMA((4, 2)),
            pltpu.SemaphoreType.DMA((2,)),
        ],
        [HBM] * 4,
        4,
        "load",
        flops=128 * 1024 * 1024,
        moved=4 * MIB,
    )(fixed(tokens), fixed(attn_gain.reshape(1, D)), fixed(w_key), fixed(w_value))
    *pairs, normed = call(
        kv_kernel,
        [arr(PAIR, 256)] * 4 + [arr(PAIR, D)],
        [],
        [VM] * 4 + [ANY],
        6,
        "kv",
        flops=2 * 256 * 1024 * 1024,
        moved=3 * MIB,
    )(own, swapped, gain, wkv, gain_there)
    pairs = exchange(pairs, "y")
    queries = call(
        q_kernel,
        [arr(PAIR, 128)] * 4,
        [],
        [VM] * 2,
        4,
        "q",
        flops=2 * 256 * 1024 * 512,
        moved=4 * MIB,
    )(normed, w_query)
    pieces = call(
        state_kernel,
        [arr(PIECE, 128)] * 4,
        [
            pltpu.VMEM((2, 2 * HS, LEN), F32),
            pltpu.VMEM((2 * LEN, 128), BF),
            pltpu.VMEM((NF, 2 * LEN), BF),
            pltpu.VMEM((NF, 128), F32),
        ],
        [VM] * 4,
        20,
        "state",
        flops=2 * NF * 2 * LEN * 256,
        moved=2 * MIB,
    )(*pairs)
    pieces, queries = lax.optimization_barrier((pieces, queries))
    pieces = exchange(pieces, "z")
    queries = exchange(queries, "y")
    inside = call(
        inside_kernel,
        arr(LEN, 128, dtype=F32),
        [pltpu.VMEM((LEN, 128), BF)] * 3,
        [VM] * 8,
        16,
        "inside",
        flops=2 * 1024 * 1024 * 256 * 2,
        moved=2 * MIB,
    )(*pairs, *queries)

    total = call(total_kernel, arr(PIECE, 128), [], [VM] * 4, 4, "total", moved=MIB)(*pieces)
    moved = {k: hop(total, "x", k) for k in ORDER}
    totals = [total] + [moved[k] for k in range(1, 4)]
    phi = call(
        features_kernel,
        arr(NF, 2 * LEN),
        [pltpu.VMEM((2, 2 * HS, LEN), F32)],
        [VM] * 4,
        6,
        "features",
        flops=NF * 2 * LEN * 128,
        moved=9 * MIB,
    )(*queries)
    states = call(
        combine_kernel, [arr(PIECE, 128)] * 4, [], [VM] * 8 + [ANY] * 2, 8, "combine", moved=MIB
    )(*pieces, *totals, phi, inside)
    states = exchange(states, "z")

    *parts, turned = call(
        apply_kernel,
        [arr(PAIR, 128)] * 3 + [arr(128, NF)],
        [pltpu.VMEM((NF, 128), F32)],
        [VM] * 8,
        12,
        "apply",
        flops=2 * NF * 2 * LEN * 192,
        moved=2 * MIB,
    )(phi, *states, inside, gain_here, gain_there)
    moved = {k: hop(parts[k - 1], "y", k) for k in ORDER}
    mine = call(
        own_kernel,
        arr(PAIR, 128),
        [],
        [VM] * 5,
        8,
        "own",
        flops=2 * NF * 2 * LEN * 64,
        moved=2 * MIB,
    )(phi, turned, inside, gain_here, gain_there)
    parts = [mine] + [moved[k] for k in range(1, 4)]
    other = call(merge_kernel, arr(ROWS, 512), [], [VM] * 4, 4, "merge")(*parts)
    other = other_core(other)

    return call(
        mlp_kernel,
        [arr(ROWS, D)] * 2,
        [],
        [VM] * 10,
        8,
        "mlp",
        flops=2 * 128 * 1024 * 9216,
        moved=18 * MIB,
    )(*parts, other, tokens, mlp_gain.reshape(1, D), w_output, w_in, w_out)


def solution(mesh):
    finer = Mesh(mesh.devices.reshape(4, 4, 4, 2), SPLIT)
    placed = (P(SPLIT, None), P(), P(), P(), P(), P(BA), P(), P(), P(), P())
    return jax.shard_map(
        body,
        mesh=finer,
        in_specs=placed,
        out_specs=(P(SPLIT, None), P(SPLIT, None)),
        check_vma=False,
    )
```

```python
import jax
import jax.numpy as jnp
from jax import lax
from jax.experimental import pallas as pl
from jax.experimental.pallas import tpu as pltpu
from jax.sharding import Mesh
from jax.sharding import PartitionSpec as P

D = 1024
FF = 4096
HS = 64
NF = HS * (HS + 1) // 2
PIECE = NF // 4
ROWS = 128
PAIR = 2 * ROWS
LEN = 1024
F32 = jnp.float32
BF = jnp.bfloat16
SPLIT = ("x", "z", "y", "c")
BA = ("y", "c")
MIB = 1 << 20


VM = pl.BlockSpec(memory_space=pltpu.VMEM)
HBM = pl.BlockSpec(memory_space=pltpu.HBM)
ANY = pl.BlockSpec(memory_space=pl.ANY)


def xor_pairs(n, k):
    return [(i, i ^ k) for i in range(n)]


def flip(index, k):
    return jnp.bitwise_xor(index, k) if k else index


def rms(matrix, gain):
    return matrix * lax.rsqrt(jnp.mean(matrix * matrix, axis=-1, keepdims=True) + 1e-05) * gain


def columns(k):
    return pl.multiple_of((2 * flip(lax.axis_index("y"), k) + lax.axis_index("c")) * 128, 128)


def load_kernel(tok, gain, wk, wv, normed, gout, wout, tbuf, sems, tsems):
    first = [
        pltpu.make_async_copy(gain, gout, tsems.at[0]),
        pltpu.make_async_copy(tok, tbuf, tsems.at[1]),
    ]
    for copy in first:
        copy.start()
    copies = []
    for k in range(1, 4):
        for j, w in enumerate((wk, wv)):
            copy = pltpu.make_async_copy(
                w.at[:, pl.ds(columns(k), 128)],
                wout.at[k - 1, :, j * 128 : (j + 1) * 128],
                sems.at[k - 1, j],
            )
            copy.start()
            copies.append(copy)
    for copy in first:
        copy.wait()
    normed[...] = rms(tbuf[...].astype(F32), gout[...]).astype(BF)
    for copy in copies:
        copy.wait()


def kv_kernel(own, other, gain, wkv, *rest):
    outs, normed = rest[:3], rest[3]
    c = lax.axis_index("c")
    normed[pl.ds(pl.multiple_of(c * ROWS, ROWS), ROWS), :] = own[...]
    at = pl.ds(pl.multiple_of((1 - c) * ROWS, ROWS), ROWS)
    normed[at, :] = rms(other[...].astype(F32), gain[...]).astype(BF)
    for k in range(3):
        outs[k][...] = jnp.dot(normed[...], wkv[k], preferred_element_type=F32).astype(BF)


def q_kernel(normed, wq, wk, wv, *rest):
    outs, own, wbuf, sems = rest[:4], rest[4], rest[5], rest[6]
    copies = []
    for j, w in enumerate((wk, wv)):
        copy = pltpu.make_async_copy(
            w.at[:, pl.ds(columns(0), 128)], wbuf.at[:, j * 128 : (j + 1) * 128], sems.at[j]
        )
        copy.start()
        copies.append(copy)
    for k in range(4):
        outs[k][...] = jnp.dot(
            normed[...], wq[:, pl.ds(columns(k), 128)], preferred_element_type=F32
        ).astype(BF)
    for copy in copies:
        copy.wait()
    own[...] = jnp.dot(normed[...], wbuf[...], preferred_element_type=F32).astype(BF)


def fill_pairs(ext, h, phi, col, weighted, first=0, last=33):
    for d in range(first, last):
        rows = HS if d < 32 else 32
        left = ext[h, 0:rows, :]
        if weighted and d:
            left = left + left
        phi[d * HS : d * HS + rows, col : col + LEN] = (left * ext[h, d : d + rows, :]).astype(BF)


def state_kernel(*refs):
    chunks, outs = refs[:4], refs[4:8]
    ext, vz, phi, state = refs[8:]
    lane = lax.broadcasted_iota(jnp.int32, (PAIR, 128), 1)
    zero = jnp.zeros((PAIR, 128), BF)
    for k in range(4):
        at = slice(k * PAIR, (k + 1) * PAIR)
        turned = chunks[k][:, 0:128].astype(F32).T
        value = chunks[k][:, 128:256]
        for h in range(2):
            part = turned[h * HS : (h + 1) * HS]
            ext[h, 0:HS, at] = part
            ext[h, HS : 2 * HS, at] = part
            mine = (lane >= HS) if h else (lane < HS)
            vz[h * LEN + k * PAIR : h * LEN + (k + 1) * PAIR, :] = jnp.where(mine, value, zero)
    for first, last in ((0, 8), (8, 16), (16, 24), (24, 33)):
        for h in range(2):
            fill_pairs(ext, h, phi, h * LEN, True, first, last)
        at = slice(first * HS, min(last * HS, NF))
        state[at, :] = jnp.dot(phi[at, :], vz[...], preferred_element_type=F32)
    me = lax.axis_index("z")
    for k in range(4):
        row = pl.multiple_of(flip(me, k) * PIECE, 8)
        outs[k][...] = state[pl.ds(row, PIECE), :].astype(BF)


def pair_rows(k):
    return pl.ds(pl.multiple_of(flip(lax.axis_index("y"), k) * PAIR, PAIR), PAIR)


def inside_kernel(*refs):
    pairs, queries, out = refs[:4], refs[4:8], refs[8]
    q, kk, v = refs[9:]
    for k in range(4):
        at = pair_rows(k)
        q[at, :] = queries[k][...]
        kk[at, :] = pairs[k][:, 0:128]
        v[at, :] = pairs[k][:, 128:256]
    T = 256
    lane_q = lax.broadcasted_iota(jnp.int32, (T, 128), 1)
    lane_v = lax.broadcasted_iota(jnp.int32, (LEN, 128), 1)
    causal = lax.broadcasted_iota(jnp.int32, (T, T), 0) >= lax.broadcasted_iota(
        jnp.int32, (T, T), 1
    )
    nt = (((1,), (1,)), ((), ()))
    vh = [jnp.where((lane_v >= HS) if h else (lane_v < HS), v[...], jnp.zeros((), BF)) for h in range(2)]
    for i in range(LEN // T):
        rows = slice(i * T, (i + 1) * T)
        total = None
        for h in range(2):
            qh = jnp.where((lane_q >= HS) if h else (lane_q < HS), q[rows, :], jnp.zeros((), BF))
            last = lax.dot_general(qh, kk[rows, :], nt, preferred_element_type=F32)
            last = jnp.where(causal, last * last, 0.0).astype(BF)
            add = jnp.dot(last, vh[h][rows], preferred_element_type=F32)
            total = add if total is None else total + add
            if i:
                full = lax.dot_general(qh, kk[0 : i * T, :], nt, preferred_element_type=F32)
                full = (full * full).astype(BF)
                total = total + jnp.dot(full, vh[h][0 : i * T], preferred_element_type=F32)
        out[rows, :] = total


def total_kernel(*refs):
    pieces, out = refs[:4], refs[4]
    out[...] = sum(p[...].astype(F32) for p in pieces).astype(BF)


def combine_kernel(*refs):
    pieces, totals, outs = refs[:4], refs[4:8], refs[10:14]
    x, z = lax.axis_index("x"), lax.axis_index("z")
    base = jnp.zeros((PIECE, 128), F32)
    for k in range(1, 4):
        base = base + jnp.where(flip(x, k) < x, totals[k][...].astype(F32), 0.0)
    for k in range(4):
        acc = base
        for j in range(4):
            if j != k:
                acc = acc + jnp.where(flip(z, j) < flip(z, k), pieces[j][...].astype(F32), 0.0)
        outs[k][...] = acc.astype(BF)


def features_kernel(*refs):
    queries, phi, ext = refs[:4], refs[4], refs[5]
    for k in range(4):
        at = slice(k * PAIR, (k + 1) * PAIR)
        turned = queries[k][...].astype(F32).T
        for h in range(2):
            part = turned[h * HS : (h + 1) * HS]
            ext[h, 0:HS, at] = part
            ext[h, HS : 2 * HS, at] = part
    for h in range(2):
        fill_pairs(ext, h, phi, h * LEN, False)


def attend(turned, phi, inside, gain, first, last):
    halves = [
        jnp.dot(
            turned[h * HS : (h + 1) * HS],
            phi[:, h * LEN + first * PAIR : h * LEN + last * PAIR],
            preferred_element_type=F32,
        )
        for h in range(2)
    ]
    numer = jnp.concatenate(halves, axis=0).T
    low = lax.broadcasted_iota(jnp.int32, (PAIR, 128), 1) < HS
    outs = []
    for k in range(first, last):
        at = slice((k - first) * PAIR, (k - first + 1) * PAIR)
        mine = numer[at] + inside[pair_rows(k), :]
        square = mine * mine
        one = jnp.sum(jnp.where(low, square, 0.0), axis=-1, keepdims=True)
        two = jnp.sum(jnp.where(low, 0.0, square), axis=-1, keepdims=True)
        mean = jnp.where(low, one, two) * (1.0 / HS)
        outs.append((mine * lax.rsqrt(mean + 1e-05) * gain[...]).astype(BF))
    return outs


def apply_kernel(*refs):
    phi, states, inside, gain, outs, turned = refs[0], refs[1:5], refs[5], refs[6], refs[7:10], refs[10]
    state = refs[11]
    z = lax.axis_index("z")
    for k in range(4):
        row = pl.multiple_of(flip(z, k) * PIECE, 8)
        state[pl.ds(row, PIECE), :] = states[k][...].astype(F32)
    turned[...] = state[...].T.astype(BF)
    for out, value in zip(outs, attend(turned[...], phi, inside, gain, 1, 4)):
        out[...] = value


def own_kernel(phi, turned, inside, gain, out):
    out[...] = attend(turned[...], phi, inside, gain, 0, 1)[0]


def merge_kernel(*refs):
    parts, out = refs[:4], refs[4]
    row = pl.multiple_of((1 - lax.axis_index("c")) * ROWS, ROWS)
    for k in range(4):
        col = pl.multiple_of(flip(lax.axis_index("y"), k) * 128, 128)
        out[:, pl.ds(col, 128)] = parts[k][pl.ds(row, ROWS), :]


FB = 2048


def mlp_kernel(*refs):
    parts, other, tok, gain, wo, wi, wf = refs[:4], *refs[4:10]
    att, res = refs[10:12]
    y, c = lax.axis_index("y"), lax.axis_index("c")
    row = pl.multiple_of(c * ROWS, ROWS)
    for k in range(4):
        col = pl.multiple_of((2 * flip(y, k) + c) * 128, 128)
        att[:, pl.ds(col, 128)] = parts[k][pl.ds(row, ROWS), :]
        col = pl.multiple_of((2 * k + 1 - c) * 128, 128)
        att[:, pl.ds(col, 128)] = other[:, k * 128 : (k + 1) * 128]
    stream = tok[...].astype(F32) + jnp.dot(att[...], wo[...], preferred_element_type=F32)
    stream = stream.astype(BF).astype(F32)
    normed = rms(stream, gain[...]).astype(BF)
    acc = stream
    for j in range(FF // FB):
        at = slice(j * FB, (j + 1) * FB)
        u = jnp.dot(normed, wi[:, at], preferred_element_type=F32)
        hidden = 0.5 * u * (1.0 + jnp.tanh(0.7978845608028654 * (u + 0.044715 * u * u * u)))
        acc = acc + jnp.dot(hidden.astype(BF), wf[at, :], preferred_element_type=F32)
    res[...] = acc.astype(BF)


def call(kernel, outs, scratch, specs, limit, name, flops=0, moved=0):
    return pl.pallas_call(
        kernel,
        out_shape=outs,
        in_specs=specs,
        out_specs=jax.tree.map(lambda _: VM, outs),
        scratch_shapes=scratch,
        compiler_params=pltpu.CompilerParams(vmem_limit_bytes=limit * MIB),
        cost_estimate=pl.CostEstimate(flops=flops, bytes_accessed=moved, transcendentals=0),
        name=name,
    )


def arr(*shape, dtype=BF):
    return jax.ShapeDtypeStruct(shape, dtype)


def fixed(array):
    return pltpu.with_memory_space_constraint(array, pltpu.HBM)


ORDER = (2, 3, 1)


def exchange(parts, axis):
    moved = {k: lax.ppermute(parts[k], axis, xor_pairs(4, k)) for k in ORDER}
    return [parts[0]] + [moved[k] for k in range(1, 4)]


def body(tokens, attn_gain, w_query, w_key, w_value, head_gain, w_output, mlp_gain, w_in, w_out):
    swapped = lax.ppermute(tokens, "c", xor_pairs(2, 1))
    own, gain, wkv = call(
        load_kernel,
        [arr(ROWS, D), arr(1, D, dtype=F32), arr(3, D, 256)],
        [
            pltpu.VMEM((ROWS, D), BF),
            pltpu.SemaphoreType.DMA((3, 2)),
            pltpu.SemaphoreType.DMA((2,)),
        ],
        [HBM] * 4,
        4,
        "load",
        flops=128 * 1024 * 1024,
        moved=4 * MIB,
    )(fixed(tokens), fixed(attn_gain.reshape(1, D)), fixed(w_key), fixed(w_value))
    *pairs, normed = call(
        kv_kernel,
        [arr(PAIR, 256)] * 3 + [arr(PAIR, D)],
        [],
        [VM] * 4,
        6,
        "kv",
        flops=2 * 256 * 1024 * 1024,
        moved=3 * MIB,
    )(own, swapped, gain, wkv)
    pairs = exchange([None, *pairs], "y")
    *queries, pairs[0] = call(
        q_kernel,
        [arr(PAIR, 128)] * 4 + [arr(PAIR, 256)],
        [pltpu.VMEM((D, 256), BF), pltpu.SemaphoreType.DMA((2,))],
        [VM] * 2 + [HBM] * 2,
        6,
        "q",
        flops=2 * 256 * 1024 * 512,
        moved=4 * MIB,
    )(normed, w_query, fixed(w_key), fixed(w_value))
    pieces = call(
        state_kernel,
        [arr(PIECE, 128)] * 4,
        [
            pltpu.VMEM((2, 2 * HS, LEN), F32),
            pltpu.VMEM((2 * LEN, 128), BF),
            pltpu.VMEM((NF, 2 * LEN), BF),
            pltpu.VMEM((NF, 128), F32),
        ],
        [VM] * 4,
        20,
        "state",
        flops=2 * NF * 2 * LEN * 256,
        moved=2 * MIB,
    )(*pairs)
    pieces, queries = lax.optimization_barrier((pieces, queries))
    pieces = exchange(pieces, "z")
    queries = exchange(queries, "y")
    inside = call(
        inside_kernel,
        arr(LEN, 128, dtype=F32),
        [pltpu.VMEM((LEN, 128), BF)] * 3,
        [VM] * 8,
        16,
        "inside",
        flops=2 * 1024 * 1024 * 256 * 2,
        moved=2 * MIB,
    )(*pairs, *queries)

    total = call(total_kernel, arr(PIECE, 128), [], [VM] * 4, 4, "total", moved=MIB)(*pieces)
    later = {k: [(i, j) for i, j in xor_pairs(4, k) if i < j] for k in ORDER}
    moved = {k: lax.ppermute(total, "x", later[k]) for k in ORDER}
    totals = [total] + [moved[k] for k in range(1, 4)]
    phi = call(
        features_kernel,
        arr(NF, 2 * LEN),
        [pltpu.VMEM((2, 2 * HS, LEN), F32)],
        [VM] * 4,
        6,
        "features",
        flops=NF * 2 * LEN * 128,
        moved=9 * MIB,
    )(*queries)
    states = call(
        combine_kernel, [arr(PIECE, 128)] * 4, [], [VM] * 8 + [ANY] * 2, 8, "combine", moved=MIB
    )(*pieces, *totals, phi, inside)
    states = exchange(states, "z")

    scale = head_gain.reshape(1, 128)
    *parts, turned = call(
        apply_kernel,
        [arr(PAIR, 128)] * 3 + [arr(128, NF)],
        [pltpu.VMEM((NF, 128), F32)],
        [VM] * 7,
        12,
        "apply",
        flops=2 * NF * 2 * LEN * 192,
        moved=2 * MIB,
    )(phi, *states, inside, scale)
    moved = {k: lax.ppermute(parts[k - 1], "y", xor_pairs(4, k)) for k in ORDER}
    mine = call(
        own_kernel,
        arr(PAIR, 128),
        [],
        [VM] * 4,
        8,
        "own",
        flops=2 * NF * 2 * LEN * 64,
        moved=2 * MIB,
    )(phi, turned, inside, scale)
    parts = [mine] + [moved[k] for k in range(1, 4)]
    other = call(merge_kernel, arr(ROWS, 512), [], [VM] * 4, 4, "merge")(*parts)
    other = lax.ppermute(other, "c", xor_pairs(2, 1))

    return call(
        mlp_kernel,
        [arr(ROWS, D)] * 2,
        [],
        [VM] * 10,
        8,
        "mlp",
        flops=2 * 128 * 1024 * 9216,
        moved=18 * MIB,
    )(*parts, other, tokens, mlp_gain.reshape(1, D), w_output, w_in, w_out)


def solution(mesh):
    finer = Mesh(mesh.devices.reshape(4, 4, 4, 2), SPLIT)
    placed = (P(SPLIT, None), P(), P(), P(), P(), P(BA), P(), P(), P(), P())
    return jax.shard_map(
        body,
        mesh=finer,
        in_specs=placed,
        out_specs=(P(SPLIT, None), P(SPLIT, None)),
        check_vma=False,
    )
```

```python
import jax
import jax.numpy as jnp
from jax import lax
from jax.experimental import pallas as pl
from jax.experimental.pallas import tpu as pltpu
from jax.sharding import Mesh
from jax.sharding import PartitionSpec as P

D = 1024
FF = 4096
HS = 64
NF = HS * (HS + 1) // 2
PIECE = NF // 4
ROWS = 128
PAIR = 2 * ROWS
LEN = 1024
F32 = jnp.float32
BF = jnp.bfloat16
SPLIT = ("x", "z", "y", "c")
BA = ("y", "c")
MIB = 1 << 20


VM = pl.BlockSpec(memory_space=pltpu.VMEM)
HBM = pl.BlockSpec(memory_space=pltpu.HBM)
ANY = pl.BlockSpec(memory_space=pl.ANY)


def xor_pairs(n, k):
    return [(i, i ^ k) for i in range(n)]


def flip(index, k):
    return jnp.bitwise_xor(index, k) if k else index


def rms(matrix, gain):
    return matrix * lax.rsqrt(jnp.mean(matrix * matrix, axis=-1, keepdims=True) + 1e-05) * gain


def columns(k):
    return pl.multiple_of((2 * flip(lax.axis_index("y"), k) + lax.axis_index("c")) * 128, 128)


def load_kernel(tok, gain, wk, wv, normed, gout, wout, tbuf, sems, tsems):
    first = [
        pltpu.make_async_copy(gain, gout, tsems.at[0]),
        pltpu.make_async_copy(tok, tbuf, tsems.at[1]),
    ]
    for copy in first:
        copy.start()
    copies = []
    for k in range(1, 4):
        for j, w in enumerate((wk, wv)):
            copy = pltpu.make_async_copy(
                w.at[:, pl.ds(columns(k), 128)],
                wout.at[k - 1, :, j * 128 : (j + 1) * 128],
                sems.at[k - 1, j],
            )
            copy.start()
            copies.append(copy)
    for copy in first:
        copy.wait()
    normed[...] = rms(tbuf[...].astype(F32), gout[...]).astype(BF)
    for copy in copies:
        copy.wait()


def kv_kernel(own, other, gain, wkv, *rest):
    outs, normed = rest[:3], rest[3]
    c = lax.axis_index("c")
    normed[pl.ds(pl.multiple_of(c * ROWS, ROWS), ROWS), :] = own[...]
    at = pl.ds(pl.multiple_of((1 - c) * ROWS, ROWS), ROWS)
    normed[at, :] = rms(other[...].astype(F32), gain[...]).astype(BF)
    for k in range(3):
        outs[k][...] = jnp.dot(normed[...], wkv[k], preferred_element_type=F32).astype(BF)


def q_kernel(normed, wq, wk, wv, *rest):
    outs, own, wbuf, sems = rest[:4], rest[4], rest[5], rest[6]
    copies = []
    for j, w in enumerate((wk, wv)):
        copy = pltpu.make_async_copy(
            w.at[:, pl.ds(columns(0), 128)], wbuf.at[:, j * 128 : (j + 1) * 128], sems.at[j]
        )
        copy.start()
        copies.append(copy)
    for k in range(4):
        outs[k][...] = jnp.dot(
            normed[...], wq[:, pl.ds(columns(k), 128)], preferred_element_type=F32
        ).astype(BF)
    for copy in copies:
        copy.wait()
    own[...] = jnp.dot(normed[...], wbuf[...], preferred_element_type=F32).astype(BF)


MAIN = 8 * HS


def fill_queries(ext, h, phi, col):
    for d in range(32):
        row = MAIN * (d % 4) + HS * (d // 4)
        phi[row : row + HS, col : col + LEN] = (ext[h, 0:HS, :] * ext[h, d : d + HS, :]).astype(BF)
    phi[4 * MAIN : NF, col : col + LEN] = (ext[h, 0:32, :] * ext[h, 32:HS, :]).astype(BF)


def key_piece(ext, vz, phi, turned, k):
    c = flip(lax.axis_index("z"), k)
    for h in range(2):
        col = slice(h * LEN, (h + 1) * LEN)
        turned[...] = pltpu.roll(ext[h], lax.rem(2 * HS - c, 2 * HS), 0)
        for j in range(8):
            left = ext[h, 0:HS, :]
            twice = left + left
            if j == 0:
                twice = jnp.where(c == 0, left, twice)
            phi[j * HS : (j + 1) * HS, col] = (twice * turned[4 * j : 4 * j + HS, :]).astype(BF)
        low = ext[h, pl.ds(pl.multiple_of(8 * c, 8), 8), :]
        high = ext[h, pl.ds(pl.multiple_of(8 * c + 32, 8), 8), :]
        phi[MAIN:PIECE, col] = ((low + low) * high).astype(BF)
    return jnp.dot(phi[...], vz[...], preferred_element_type=F32).astype(BF)


def state_kernel(*refs):
    chunks, outs = refs[:4], refs[4:6]
    ext, vz, phi, turned = refs[6:]
    lane = lax.broadcasted_iota(jnp.int32, (PAIR, 128), 1)
    zero = jnp.zeros((PAIR, 128), BF)
    for k in range(4):
        at = slice(k * PAIR, (k + 1) * PAIR)
        keys = chunks[k][:, 0:128].astype(F32).T
        value = chunks[k][:, 128:256]
        for h in range(2):
            part = keys[h * HS : (h + 1) * HS]
            ext[h, 0:HS, at] = part
            ext[h, HS : 2 * HS, at] = part
            mine = (lane >= HS) if h else (lane < HS)
            vz[h * LEN + k * PAIR : h * LEN + (k + 1) * PAIR, :] = jnp.where(mine, value, zero)
    for out, k in zip(outs, (1, 2)):
        out[...] = key_piece(ext, vz, phi, turned, k)


def third_kernel(ext, vz, out, phi, turned):
    out[...] = key_piece(ext, vz, phi, turned, 3)


def rest_kernel(ext, vz, after, out, phi, turned):
    out[...] = key_piece(ext, vz, phi, turned, 0)


def pair_rows(k):
    return pl.ds(pl.multiple_of(flip(lax.axis_index("y"), k) * PAIR, PAIR), PAIR)


def inside_kernel(*refs):
    pairs, queries, out = refs[:4], refs[4:8], refs[8]
    q, kk, v = refs[9:]
    for k in range(4):
        at = pair_rows(k)
        q[at, :] = queries[k][...]
        kk[at, :] = pairs[k][:, 0:128]
        v[at, :] = pairs[k][:, 128:256]
    T = 256
    lane_q = lax.broadcasted_iota(jnp.int32, (T, 128), 1)
    lane_v = lax.broadcasted_iota(jnp.int32, (LEN, 128), 1)
    causal = lax.broadcasted_iota(jnp.int32, (T, T), 0) >= lax.broadcasted_iota(
        jnp.int32, (T, T), 1
    )
    nt = (((1,), (1,)), ((), ()))
    vh = [jnp.where((lane_v >= HS) if h else (lane_v < HS), v[...], jnp.zeros((), BF)) for h in range(2)]
    for i in range(LEN // T):
        rows = slice(i * T, (i + 1) * T)
        total = None
        for h in range(2):
            qh = jnp.where((lane_q >= HS) if h else (lane_q < HS), q[rows, :], jnp.zeros((), BF))
            last = lax.dot_general(qh, kk[rows, :], nt, preferred_element_type=F32)
            last = jnp.where(causal, last * last, 0.0).astype(BF)
            add = jnp.dot(last, vh[h][rows], preferred_element_type=F32)
            total = add if total is None else total + add
            if i:
                full = lax.dot_general(qh, kk[0 : i * T, :], nt, preferred_element_type=F32)
                full = (full * full).astype(BF)
                total = total + jnp.dot(full, vh[h][0 : i * T], preferred_element_type=F32)
        out[rows, :] = total


def total_kernel(*refs):
    pieces, out = refs[:4], refs[4]
    out[...] = sum(p[...].astype(F32) for p in pieces).astype(BF)


def combine_kernel(*refs):
    pieces, totals, outs = refs[:4], refs[4:8], refs[10:14]
    x, z = lax.axis_index("x"), lax.axis_index("z")
    base = jnp.zeros((PIECE, 128), F32)
    for k in range(1, 4):
        base = base + jnp.where(flip(x, k) < x, totals[k][...].astype(F32), 0.0)
    for k in range(4):
        acc = base
        for j in range(4):
            if j != k:
                acc = acc + jnp.where(flip(z, j) < flip(z, k), pieces[j][...].astype(F32), 0.0)
        outs[k][...] = acc.astype(BF)


def features_kernel(*refs):
    queries, phi, ext = refs[:4], refs[4], refs[5]
    for k in range(4):
        at = slice(k * PAIR, (k + 1) * PAIR)
        turned = queries[k][...].astype(F32).T
        for h in range(2):
            part = turned[h * HS : (h + 1) * HS]
            ext[h, 0:HS, at] = part
            ext[h, HS : 2 * HS, at] = part
    for h in range(2):
        fill_queries(ext, h, phi, h * LEN)


def attend(turned, phi, inside, gain, first, last):
    halves = [
        jnp.dot(
            turned[h * HS : (h + 1) * HS],
            phi[:, h * LEN + first * PAIR : h * LEN + last * PAIR],
            preferred_element_type=F32,
        )
        for h in range(2)
    ]
    numer = jnp.concatenate(halves, axis=0).T
    low = lax.broadcasted_iota(jnp.int32, (PAIR, 128), 1) < HS
    outs = []
    for k in range(first, last):
        at = slice((k - first) * PAIR, (k - first + 1) * PAIR)
        mine = numer[at] + inside[pair_rows(k), :]
        square = mine * mine
        one = jnp.sum(jnp.where(low, square, 0.0), axis=-1, keepdims=True)
        two = jnp.sum(jnp.where(low, 0.0, square), axis=-1, keepdims=True)
        mean = jnp.where(low, one, two) * (1.0 / HS)
        outs.append((mine * lax.rsqrt(mean + 1e-05) * gain[...]).astype(BF))
    return outs


def apply_kernel(*refs):
    phi, states, inside, gain, outs, turned = refs[0], refs[1:5], refs[5], refs[6], refs[7:10], refs[10]
    state = refs[11]
    z = lax.axis_index("z")
    for k in range(4):
        c = flip(z, k)
        piece = states[k][...].astype(F32)
        state[pl.ds(pl.multiple_of(c * MAIN, MAIN), MAIN), :] = piece[0:MAIN]
        state[pl.ds(pl.multiple_of(4 * MAIN + 8 * c, 8), 8), :] = piece[MAIN:PIECE]
    turned[...] = state[...].T.astype(BF)
    for out, value in zip(outs, attend(turned[...], phi, inside, gain, 1, 4)):
        out[...] = value


def own_kernel(phi, turned, inside, gain, out):
    out[...] = attend(turned[...], phi, inside, gain, 0, 1)[0]


def merge_kernel(*refs):
    parts, out = refs[:4], refs[4]
    row = pl.multiple_of((1 - lax.axis_index("c")) * ROWS, ROWS)
    for k in range(4):
        col = pl.multiple_of(flip(lax.axis_index("y"), k) * 128, 128)
        out[:, pl.ds(col, 128)] = parts[k][pl.ds(row, ROWS), :]


FB = 2048


def mlp_kernel(*refs):
    parts, other, tok, gain, wo, wi, wf = refs[:4], *refs[4:10]
    att, res = refs[10:12]
    y, c = lax.axis_index("y"), lax.axis_index("c")
    row = pl.multiple_of(c * ROWS, ROWS)
    for k in range(4):
        col = pl.multiple_of((2 * flip(y, k) + c) * 128, 128)
        att[:, pl.ds(col, 128)] = parts[k][pl.ds(row, ROWS), :]
        col = pl.multiple_of((2 * k + 1 - c) * 128, 128)
        att[:, pl.ds(col, 128)] = other[:, k * 128 : (k + 1) * 128]
    stream = tok[...].astype(F32) + jnp.dot(att[...], wo[...], preferred_element_type=F32)
    stream = stream.astype(BF).astype(F32)
    normed = rms(stream, gain[...]).astype(BF)
    acc = stream
    for j in range(FF // FB):
        at = slice(j * FB, (j + 1) * FB)
        u = jnp.dot(normed, wi[:, at], preferred_element_type=F32)
        hidden = 0.5 * u * (1.0 + jnp.tanh(0.7978845608028654 * (u + 0.044715 * u * u * u)))
        acc = acc + jnp.dot(hidden.astype(BF), wf[at, :], preferred_element_type=F32)
    res[...] = acc.astype(BF)


def call(kernel, outs, scratch, specs, limit, flops=0, moved=0):
    return pl.pallas_call(
        kernel,
        out_shape=outs,
        in_specs=specs,
        out_specs=jax.tree.map(lambda _: VM, outs),
        scratch_shapes=scratch,
        compiler_params=pltpu.CompilerParams(vmem_limit_bytes=limit * MIB),
        cost_estimate=pl.CostEstimate(flops=flops, bytes_accessed=moved, transcendentals=0),
    )


def arr(*shape, dtype=BF):
    return jax.ShapeDtypeStruct(shape, dtype)


def fixed(array):
    return pltpu.with_memory_space_constraint(array, pltpu.HBM)


ORDER = (2, 3, 1)


def exchange(parts, axis):
    moved = {k: lax.ppermute(parts[k], axis, xor_pairs(4, k)) for k in ORDER}
    return [parts[0]] + [moved[k] for k in range(1, 4)]


def body(tokens, attn_gain, w_query, w_key, w_value, head_gain, w_output, mlp_gain, w_in, w_out):
    swapped = lax.ppermute(tokens, "c", xor_pairs(2, 1))
    own, gain, wkv = call(
        load_kernel,
        [arr(ROWS, D), arr(1, D, dtype=F32), arr(3, D, 256)],
        [
            pltpu.VMEM((ROWS, D), BF),
            pltpu.SemaphoreType.DMA((3, 2)),
            pltpu.SemaphoreType.DMA((2,)),
        ],
        [HBM] * 4,
        4,
        flops=128 * 1024 * 1024,
        moved=4 * MIB,
    )(fixed(tokens), fixed(attn_gain.reshape(1, D)), fixed(w_key), fixed(w_value))
    *pairs, normed = call(
        kv_kernel,
        [arr(PAIR, 256)] * 3 + [arr(PAIR, D)],
        [],
        [VM] * 4,
        6,
        flops=2 * 256 * 1024 * 1024,
        moved=3 * MIB,
    )(own, swapped, gain, wkv)
    pairs = exchange([None, *pairs], "y")
    *queries, pairs[0] = call(
        q_kernel,
        [arr(PAIR, 128)] * 4 + [arr(PAIR, 256)],
        [pltpu.VMEM((D, 256), BF), pltpu.SemaphoreType.DMA((2,))],
        [VM] * 2 + [HBM] * 2,
        6,
        flops=2 * 256 * 1024 * 512,
        moved=4 * MIB,
    )(normed, w_query, fixed(w_key), fixed(w_value))
    spare = [pltpu.VMEM((PIECE, 2 * LEN), BF), pltpu.VMEM((2 * HS, LEN), F32)]
    cost = 2 * PIECE * 2 * LEN * 256
    first, second, ext, vz = call(
        state_kernel,
        [arr(PIECE, 128)] * 2 + [arr(2, 2 * HS, LEN, dtype=F32), arr(2 * LEN, 128)],
        spare,
        [VM] * 4,
        8,
        flops=2 * cost,
        moved=2 * MIB,
    )(*pairs)
    third = call(third_kernel, arr(PIECE, 128), spare, [VM] * 2, 8, flops=cost, moved=MIB)(ext, vz)
    own = call(
        rest_kernel, arr(PIECE, 128), spare, [VM] * 2 + [ANY], 8, flops=cost, moved=MIB
    )(ext, vz, third)
    pieces = [own]
    for k, piece in ((1, first), (2, second), (3, third)):
        pieces.append(lax.ppermute(piece, "z", xor_pairs(4, k)))
    queries = lax.optimization_barrier((queries, third))[0]
    queries = exchange(queries, "y")
    inside = call(
        inside_kernel,
        arr(LEN, 128, dtype=F32),
        [pltpu.VMEM((LEN, 128), BF)] * 3,
        [VM] * 8,
        16,
        flops=2 * 1024 * 1024 * 256 * 2,
        moved=2 * MIB,
    )(*pairs, *queries)

    total = call(total_kernel, arr(PIECE, 128), [], [VM] * 4, 4, moved=MIB)(*pieces)
    moved = {k: lax.ppermute(total, "x", xor_pairs(4, k)) for k in ORDER}
    totals = [total] + [moved[k] for k in range(1, 4)]
    phi = call(
        features_kernel,
        arr(NF, 2 * LEN),
        [pltpu.VMEM((2, 2 * HS, LEN), F32)],
        [VM] * 4,
        6,
        flops=NF * 2 * LEN * 128,
        moved=9 * MIB,
    )(*queries)
    states = call(
        combine_kernel, [arr(PIECE, 128)] * 4, [], [VM] * 8 + [ANY] * 2, 8, moved=MIB
    )(*pieces, *totals, phi, inside)
    states = exchange(states, "z")

    scale = head_gain.reshape(1, 128)
    *parts, turned = call(
        apply_kernel,
        [arr(PAIR, 128)] * 3 + [arr(128, NF)],
        [pltpu.VMEM((NF, 128), F32)],
        [VM] * 7,
        12,
        flops=2 * NF * 2 * LEN * 192,
        moved=2 * MIB,
    )(phi, *states, inside, scale)
    moved = {k: lax.ppermute(parts[k - 1], "y", xor_pairs(4, k)) for k in ORDER}
    mine = call(
        own_kernel, arr(PAIR, 128), [], [VM] * 4, 8, flops=2 * NF * 2 * LEN * 64, moved=2 * MIB
    )(phi, turned, inside, scale)
    parts = [mine] + [moved[k] for k in range(1, 4)]
    other = call(merge_kernel, arr(ROWS, 512), [], [VM] * 4, 4)(*parts)
    other = lax.ppermute(other, "c", xor_pairs(2, 1))

    return call(
        mlp_kernel,
        [arr(ROWS, D)] * 2,
        [],
        [VM] * 10,
        8,
        flops=2 * 128 * 1024 * 9216,
        moved=18 * MIB,
    )(*parts, other, tokens, mlp_gain.reshape(1, D), w_output, w_in, w_out)


def solution(mesh):
    finer = Mesh(mesh.devices.reshape(4, 4, 4, 2), SPLIT)
    placed = (P(SPLIT, None), P(), P(), P(), P(), P(BA), P(), P(), P(), P())
    return jax.shard_map(
        body,
        mesh=finer,
        in_specs=placed,
        out_specs=(P(SPLIT, None), P(SPLIT, None)),
        check_vma=False,
    )
```

```python
import jax
import jax.numpy as jnp
from jax import lax
from jax.experimental import pallas as pl
from jax.experimental.pallas import tpu as pltpu
from jax.sharding import Mesh
from jax.sharding import PartitionSpec as P

D = 1024
FF = 4096
HS = 64
NF = HS * (HS + 1) // 2
PIECE = NF // 4
ROWS = 128
PAIR = 2 * ROWS
LEN = 1024
F32 = jnp.float32
BF = jnp.bfloat16
SPLIT = ("x", "z", "y", "c")
BA = ("y", "c")
MIB = 1 << 20


VM = pl.BlockSpec(memory_space=pltpu.VMEM)
HBM = pl.BlockSpec(memory_space=pltpu.HBM)
ANY = pl.BlockSpec(memory_space=pl.ANY)


def xor_pairs(n, k):
    return [(i, i ^ k) for i in range(n)]


def flip(index, k):
    return jnp.bitwise_xor(index, k) if k else index


def rms(matrix, gain):
    return matrix * lax.rsqrt(jnp.mean(matrix * matrix, axis=-1, keepdims=True) + 1e-05) * gain


def columns(k):
    return pl.multiple_of((2 * flip(lax.axis_index("y"), k) + lax.axis_index("c")) * 128, 128)


def load_kernel(tok, gain, wk, wv, normed, gout, wout, tbuf, sems, tsems):
    first = [
        pltpu.make_async_copy(gain, gout, tsems.at[0]),
        pltpu.make_async_copy(tok, tbuf, tsems.at[1]),
    ]
    for copy in first:
        copy.start()
    copies = []
    for k in range(1, 4):
        for j, w in enumerate((wk, wv)):
            copy = pltpu.make_async_copy(
                w.at[:, pl.ds(columns(k), 128)],
                wout.at[k - 1, :, j * 128 : (j + 1) * 128],
                sems.at[k - 1, j],
            )
            copy.start()
            copies.append(copy)
    for copy in first:
        copy.wait()
    normed[...] = rms(tbuf[...].astype(F32), gout[...]).astype(BF)
    for copy in copies:
        copy.wait()


def kv_kernel(own, other, gain, wkv, *rest):
    outs, normed = rest[:3], rest[3]
    c = lax.axis_index("c")
    normed[pl.ds(pl.multiple_of(c * ROWS, ROWS), ROWS), :] = own[...]
    at = pl.ds(pl.multiple_of((1 - c) * ROWS, ROWS), ROWS)
    normed[at, :] = rms(other[...].astype(F32), gain[...]).astype(BF)
    for k in range(3):
        outs[k][...] = jnp.dot(normed[...], wkv[k], preferred_element_type=F32).astype(BF)


def q_kernel(normed, wq, wk, wv, *rest):
    outs, own, wbuf, sems = rest[:4], rest[4], rest[5], rest[6]
    copies = []
    for j, w in enumerate((wk, wv)):
        copy = pltpu.make_async_copy(
            w.at[:, pl.ds(columns(0), 128)], wbuf.at[:, j * 128 : (j + 1) * 128], sems.at[j]
        )
        copy.start()
        copies.append(copy)
    for k in range(4):
        outs[k][...] = jnp.dot(
            normed[...], wq[:, pl.ds(columns(k), 128)], preferred_element_type=F32
        ).astype(BF)
    for copy in copies:
        copy.wait()
    own[...] = jnp.dot(normed[...], wbuf[...], preferred_element_type=F32).astype(BF)


MAIN = 8 * HS


def fill_queries(ext, h, phi, col):
    for d in range(32):
        phi[d * HS : (d + 1) * HS, col : col + LEN] = (
            ext[h, 0:HS, :] * ext[h, d : d + HS, :]
        ).astype(BF)
    phi[4 * MAIN : NF, col : col + LEN] = (ext[h, 0:32, :] * ext[h, 32:HS, :]).astype(BF)


def key_piece(ext, vz, phi, turned, k):
    c = flip(lax.axis_index("z"), k)
    total = None
    for h in range(2):
        turned[h] = ext[h, pl.ds(pl.multiple_of(8 * c, 8), HS + 8), :]
        for j in range(8):
            left = ext[h, 0:HS, :]
            twice = left + left
            if j == 0:
                twice = jnp.where(c == 0, left, twice)
            phi[h, j * HS : (j + 1) * HS, :] = (twice * turned[h, j : j + HS, :]).astype(BF)
        low = ext[h, pl.ds(pl.multiple_of(8 * c, 8), 8), :]
        high = ext[h, pl.ds(pl.multiple_of(8 * c + 32, 8), 8), :]
        phi[h, MAIN:PIECE, :] = ((low + low) * high).astype(BF)
        part = jnp.dot(phi[h], vz[h * LEN : (h + 1) * LEN], preferred_element_type=F32)
        total = part if total is None else total + part
    return total.astype(BF)


def state_kernel(*refs):
    chunks, outs = refs[:4], refs[4:6]
    ext, vz, phi, turned = refs[6:]
    lane = lax.broadcasted_iota(jnp.int32, (PAIR, 128), 1)
    zero = jnp.zeros((PAIR, 128), BF)
    for k in range(4):
        at = slice(k * PAIR, (k + 1) * PAIR)
        keys = chunks[k][:, 0:128].astype(F32).T
        value = chunks[k][:, 128:256]
        for h in range(2):
            part = keys[h * HS : (h + 1) * HS]
            ext[h, 0:HS, at] = part
            ext[h, HS : 2 * HS, at] = part
            mine = (lane >= HS) if h else (lane < HS)
            vz[h * LEN + k * PAIR : h * LEN + (k + 1) * PAIR, :] = jnp.where(mine, value, zero)
    for i, (out, k) in enumerate(zip(outs, (1, 2))):
        out[...] = key_piece(ext, vz, phi.at[i], turned.at[i], k)


def third_kernel(ext, vz, out, phi, turned):
    out[...] = key_piece(ext, vz, phi, turned, 3)


def rest_kernel(ext, vz, after, out, phi, turned):
    out[...] = key_piece(ext, vz, phi, turned, 0)


def pair_rows(k):
    return pl.ds(pl.multiple_of(flip(lax.axis_index("y"), k) * PAIR, PAIR), PAIR)


def inside_kernel(*refs):
    pairs, queries, out = refs[:4], refs[4:8], refs[8]
    q, kk, v = refs[9:]
    for k in range(4):
        at = pair_rows(k)
        q[at, :] = queries[k][...]
        kk[at, :] = pairs[k][:, 0:128]
        v[at, :] = pairs[k][:, 128:256]
    T = 256
    lane_q = lax.broadcasted_iota(jnp.int32, (T, 128), 1)
    lane_v = lax.broadcasted_iota(jnp.int32, (LEN, 128), 1)
    causal = lax.broadcasted_iota(jnp.int32, (T, T), 0) >= lax.broadcasted_iota(
        jnp.int32, (T, T), 1
    )
    nt = (((1,), (1,)), ((), ()))
    vh = [jnp.where((lane_v >= HS) if h else (lane_v < HS), v[...], jnp.zeros((), BF)) for h in range(2)]
    for i in range(LEN // T):
        rows = slice(i * T, (i + 1) * T)
        total = None
        for h in range(2):
            qh = jnp.where((lane_q >= HS) if h else (lane_q < HS), q[rows, :], jnp.zeros((), BF))
            last = lax.dot_general(qh, kk[rows, :], nt, preferred_element_type=F32)
            last = jnp.where(causal, last * last, 0.0).astype(BF)
            add = jnp.dot(last, vh[h][rows], preferred_element_type=F32)
            total = add if total is None else total + add
            if i:
                full = lax.dot_general(qh, kk[0 : i * T, :], nt, preferred_element_type=F32)
                full = (full * full).astype(BF)
                total = total + jnp.dot(full, vh[h][0 : i * T], preferred_element_type=F32)
        out[rows, :] = total


def total_kernel(*refs):
    pieces, out = refs[:4], refs[4]
    out[...] = sum(p[...].astype(F32) for p in pieces).astype(BF)


def combine_kernel(*refs):
    pieces, totals, outs = refs[:4], refs[4:8], refs[10:14]
    x, z = lax.axis_index("x"), lax.axis_index("z")
    base = jnp.zeros((PIECE, 128), F32)
    for k in range(1, 4):
        base = base + jnp.where(flip(x, k) < x, totals[k][...].astype(F32), 0.0)
    for k in range(4):
        acc = base
        for j in range(4):
            if j != k:
                acc = acc + jnp.where(flip(z, j) < flip(z, k), pieces[j][...].astype(F32), 0.0)
        outs[k][...] = acc.astype(BF)


def features_kernel(*refs):
    queries, phi, ext = refs[:4], refs[4], refs[5]
    for k in range(4):
        at = slice(k * PAIR, (k + 1) * PAIR)
        turned = queries[k][...].astype(F32).T
        for h in range(2):
            part = turned[h * HS : (h + 1) * HS]
            ext[h, 0:HS, at] = part
            ext[h, HS : 2 * HS, at] = part
    for h in range(2):
        fill_queries(ext, h, phi, h * LEN)


def attend(turned, phi, inside, gain, first, last):
    halves = [
        jnp.dot(
            turned[h * HS : (h + 1) * HS],
            phi[:, h * LEN + first * PAIR : h * LEN + last * PAIR],
            preferred_element_type=F32,
        )
        for h in range(2)
    ]
    numer = jnp.concatenate(halves, axis=0).T
    low = lax.broadcasted_iota(jnp.int32, (PAIR, 128), 1) < HS
    outs = []
    for k in range(first, last):
        at = slice((k - first) * PAIR, (k - first + 1) * PAIR)
        mine = numer[at] + inside[pair_rows(k), :]
        square = mine * mine
        one = jnp.sum(jnp.where(low, square, 0.0), axis=-1, keepdims=True)
        two = jnp.sum(jnp.where(low, 0.0, square), axis=-1, keepdims=True)
        mean = jnp.where(low, one, two) * (1.0 / HS)
        outs.append((mine * lax.rsqrt(mean + 1e-05) * gain[...]).astype(BF))
    return outs


def apply_kernel(*refs):
    phi, states, inside, gain, outs, turned = refs[0], refs[1:5], refs[5], refs[6], refs[7:10], refs[10]
    state = refs[11]
    z = lax.axis_index("z")
    for k in range(4):
        c = flip(z, k)
        piece = states[k][...].astype(F32)
        state[pl.ds(pl.multiple_of(c * MAIN, MAIN), MAIN), :] = piece[0:MAIN]
        state[pl.ds(pl.multiple_of(4 * MAIN + 8 * c, 8), 8), :] = piece[MAIN:PIECE]
    turned[...] = state[...].T.astype(BF)
    for out, value in zip(outs, attend(turned[...], phi, inside, gain, 1, 4)):
        out[...] = value


def own_kernel(phi, turned, inside, gain, out):
    out[...] = attend(turned[...], phi, inside, gain, 0, 1)[0]


def merge_kernel(*refs):
    parts, out = refs[:4], refs[4]
    row = pl.multiple_of((1 - lax.axis_index("c")) * ROWS, ROWS)
    for k in range(4):
        col = pl.multiple_of(flip(lax.axis_index("y"), k) * 128, 128)
        out[:, pl.ds(col, 128)] = parts[k][pl.ds(row, ROWS), :]


FB = 2048


def mlp_kernel(*refs):
    parts, other, tok, gain, wo, wi, wf = refs[:4], *refs[4:10]
    att, res = refs[10:12]
    y, c = lax.axis_index("y"), lax.axis_index("c")
    row = pl.multiple_of(c * ROWS, ROWS)
    for k in range(4):
        col = 2 * flip(y, k) + ((1 - c) if k else c)
        att[:, pl.ds(pl.multiple_of(col * 128, 128), 128)] = parts[k][pl.ds(row, ROWS), :]
        col = 2 * k + jnp.where(y == k, 1 - c, c)
        att[:, pl.ds(pl.multiple_of(col * 128, 128), 128)] = other[:, k * 128 : (k + 1) * 128]
    stream = tok[...].astype(F32) + jnp.dot(att[...], wo[...], preferred_element_type=F32)
    stream = stream.astype(BF).astype(F32)
    normed = rms(stream, gain[...]).astype(BF)
    acc = stream
    for j in range(FF // FB):
        at = slice(j * FB, (j + 1) * FB)
        u = jnp.dot(normed, wi[:, at], preferred_element_type=F32)
        hidden = 0.5 * u * (1.0 + jnp.tanh(0.7978845608028654 * (u + 0.044715 * u * u * u)))
        acc = acc + jnp.dot(hidden.astype(BF), wf[at, :], preferred_element_type=F32)
    res[...] = acc.astype(BF)


def call(kernel, outs, scratch, specs, limit, flops=0, moved=0):
    return pl.pallas_call(
        kernel,
        out_shape=outs,
        in_specs=specs,
        out_specs=jax.tree.map(lambda _: VM, outs),
        scratch_shapes=scratch,
        compiler_params=pltpu.CompilerParams(vmem_limit_bytes=limit * MIB),
        cost_estimate=pl.CostEstimate(flops=flops, bytes_accessed=moved, transcendentals=0),
    )


def arr(*shape, dtype=BF):
    return jax.ShapeDtypeStruct(shape, dtype)


def fixed(array):
    return pltpu.with_memory_space_constraint(array, pltpu.HBM)


ORDER = (2, 3, 1)


def exchange(parts, axis):
    moved = {k: lax.ppermute(parts[k], axis, xor_pairs(4, k)) for k in ORDER}
    return [parts[0]] + [moved[k] for k in range(1, 4)]


def body(tokens, attn_gain, w_query, w_key, w_value, head_gain, w_output, mlp_gain, w_in, w_out):
    swapped = lax.ppermute(tokens, "c", xor_pairs(2, 1))
    own, gain, wkv = call(
        load_kernel,
        [arr(ROWS, D), arr(1, D, dtype=F32), arr(3, D, 256)],
        [
            pltpu.VMEM((ROWS, D), BF),
            pltpu.SemaphoreType.DMA((3, 2)),
            pltpu.SemaphoreType.DMA((2,)),
        ],
        [HBM] * 4,
        4,
        flops=128 * 1024 * 1024,
        moved=4 * MIB,
    )(fixed(tokens), fixed(attn_gain.reshape(1, D)), fixed(w_key), fixed(w_value))
    *pairs, normed = call(
        kv_kernel,
        [arr(PAIR, 256)] * 3 + [arr(PAIR, D)],
        [],
        [VM] * 4,
        6,
        flops=2 * 256 * 1024 * 1024,
        moved=3 * MIB,
    )(own, swapped, gain, wkv)
    pairs = exchange([None, *pairs], "y")
    *queries, pairs[0] = call(
        q_kernel,
        [arr(PAIR, 128)] * 4 + [arr(PAIR, 256)],
        [pltpu.VMEM((D, 256), BF), pltpu.SemaphoreType.DMA((2,))],
        [VM] * 2 + [HBM] * 2,
        6,
        flops=2 * 256 * 1024 * 512,
        moved=4 * MIB,
    )(normed, w_query, fixed(w_key), fixed(w_value))
    spare = [pltpu.VMEM((2, PIECE, LEN), BF), pltpu.VMEM((2, HS + 8, LEN), F32)]
    twice = [pltpu.VMEM((2, 2, PIECE, LEN), BF), pltpu.VMEM((2, 2, HS + 8, LEN), F32)]
    cost = 2 * PIECE * 2 * LEN * 256
    first, second, ext, vz = call(
        state_kernel,
        [arr(PIECE, 128)] * 2 + [arr(2, 2 * HS, LEN, dtype=F32), arr(2 * LEN, 128)],
        twice,
        [VM] * 4,
        12,
        flops=2 * cost,
        moved=2 * MIB,
    )(*pairs)
    third = call(third_kernel, arr(PIECE, 128), spare, [VM] * 2, 8, flops=cost, moved=MIB)(ext, vz)
    own = call(
        rest_kernel, arr(PIECE, 128), spare, [VM] * 2 + [ANY], 8, flops=cost, moved=MIB
    )(ext, vz, third)
    pieces = [own]
    for k, piece in ((1, first), (2, second), (3, third)):
        pieces.append(lax.ppermute(piece, "z", xor_pairs(4, k)))
    queries = lax.optimization_barrier((queries, third))[0]
    queries = exchange(queries, "y")
    inside = call(
        inside_kernel,
        arr(LEN, 128, dtype=F32),
        [pltpu.VMEM((LEN, 128), BF)] * 3,
        [VM] * 8,
        16,
        flops=2 * 1024 * 1024 * 256 * 2,
        moved=2 * MIB,
    )(*pairs, *queries)

    total = call(total_kernel, arr(PIECE, 128), [], [VM] * 4, 4, moved=MIB)(*pieces)
    moved = {k: lax.ppermute(total, "x", xor_pairs(4, k)) for k in ORDER}
    totals = [total] + [moved[k] for k in range(1, 4)]
    phi = call(
        features_kernel,
        arr(NF, 2 * LEN),
        [pltpu.VMEM((2, 2 * HS, LEN), F32)],
        [VM] * 4,
        6,
        flops=NF * 2 * LEN * 128,
        moved=9 * MIB,
    )(*queries)
    states = call(
        combine_kernel, [arr(PIECE, 128)] * 4, [], [VM] * 8 + [ANY] * 2, 8, moved=MIB
    )(*pieces, *totals, phi, inside)
    states = exchange(states, "z")

    scale = head_gain.reshape(1, 128)
    *parts, turned = call(
        apply_kernel,
        [arr(PAIR, 128)] * 3 + [arr(128, NF)],
        [pltpu.VMEM((NF, 128), F32)],
        [VM] * 7,
        12,
        flops=2 * NF * 2 * LEN * 192,
        moved=2 * MIB,
    )(phi, *states, inside, scale)
    swaps = {k: [(i, i ^ (2 * k + 1)) for i in range(8)] for k in ORDER}
    moved = {k: lax.ppermute(parts[k - 1], ("y", "c"), swaps[k]) for k in ORDER}
    mine = call(
        own_kernel, arr(PAIR, 128), [], [VM] * 4, 8, flops=2 * NF * 2 * LEN * 64, moved=2 * MIB
    )(phi, turned, inside, scale)
    parts = [mine] + [moved[k] for k in range(1, 4)]
    other = call(merge_kernel, arr(ROWS, 512), [], [VM] * 4, 4)(*parts)
    other = lax.ppermute(other, "c", xor_pairs(2, 1))

    return call(
        mlp_kernel,
        [arr(ROWS, D)] * 2,
        [],
        [VM] * 10,
        8,
        flops=2 * 128 * 1024 * 9216,
        moved=18 * MIB,
    )(*parts, other, tokens, mlp_gain.reshape(1, D), w_output, w_in, w_out)


def solution(mesh):
    finer = Mesh(mesh.devices.reshape(4, 4, 4, 2), SPLIT)
    placed = (P(SPLIT, None), P(), P(), P(), P(), P(BA), P(), P(), P(), P())
    return jax.shard_map(
        body,
        mesh=finer,
        in_specs=placed,
        out_specs=(P(SPLIT, None), P(SPLIT, None)),
        check_vma=False,
    )
```

```python
import jax
import jax.numpy as jnp
from jax import lax
from jax.experimental import pallas as pl
from jax.experimental.pallas import tpu as pltpu
from jax.sharding import Mesh
from jax.sharding import PartitionSpec as P

D = 1024
FF = 4096
HS = 64
NF = HS * (HS + 1) // 2
PIECE = NF // 4
ROWS = 128
PAIR = 2 * ROWS
LEN = 1024
F32 = jnp.float32
BF = jnp.bfloat16
SPLIT = ("x", "z", "y", "c")
BA = ("y", "c")
MIB = 1 << 20


VM = pl.BlockSpec(memory_space=pltpu.VMEM)
HBM = pl.BlockSpec(memory_space=pltpu.HBM)
ANY = pl.BlockSpec(memory_space=pl.ANY)


def xor_pairs(n, k):
    return [(i, i ^ k) for i in range(n)]


def flip(index, k):
    return jnp.bitwise_xor(index, k) if k else index


def rms(matrix, gain):
    return matrix * lax.rsqrt(jnp.mean(matrix * matrix, axis=-1, keepdims=True) + 1e-05) * gain


def columns(k):
    return pl.multiple_of((2 * flip(lax.axis_index("y"), k) + lax.axis_index("c")) * 128, 128)


def load_kernel(tok, gain, wk, wv, normed, gout, wout, tbuf, sems, tsems):
    first = [
        pltpu.make_async_copy(gain, gout, tsems.at[0]),
        pltpu.make_async_copy(tok, tbuf, tsems.at[1]),
    ]
    for copy in first:
        copy.start()
    copies = []
    for k in range(1, 4):
        for j, w in enumerate((wk, wv)):
            copy = pltpu.make_async_copy(
                w.at[:, pl.ds(columns(k), 128)],
                wout.at[k - 1, :, j * 128 : (j + 1) * 128],
                sems.at[k - 1, j],
            )
            copy.start()
            copies.append(copy)
    for copy in first:
        copy.wait()
    normed[...] = rms(tbuf[...].astype(F32), gout[...]).astype(BF)
    for copy in copies:
        copy.wait()


def kv_kernel(own, other, gain, wkv, *rest):
    outs, normed = rest[:3], rest[3]
    c = lax.axis_index("c")
    normed[pl.ds(pl.multiple_of(c * ROWS, ROWS), ROWS), :] = own[...]
    at = pl.ds(pl.multiple_of((1 - c) * ROWS, ROWS), ROWS)
    normed[at, :] = rms(other[...].astype(F32), gain[...]).astype(BF)
    for k in range(3):
        outs[k][...] = jnp.dot(normed[...], wkv[k], preferred_element_type=F32).astype(BF)


def q_kernel(normed, wq, wk, wv, *rest):
    outs, own, wbuf, sems = rest[:4], rest[4], rest[5], rest[6]
    copies = []
    for j, w in enumerate((wk, wv)):
        copy = pltpu.make_async_copy(
            w.at[:, pl.ds(columns(0), 128)], wbuf.at[:, j * 128 : (j + 1) * 128], sems.at[j]
        )
        copy.start()
        copies.append(copy)
    for k in range(4):
        outs[k][...] = jnp.dot(
            normed[...], wq[:, pl.ds(columns(k), 128)], preferred_element_type=F32
        ).astype(BF)
    for copy in copies:
        copy.wait()
    own[...] = jnp.dot(normed[...], wbuf[...], preferred_element_type=F32).astype(BF)


MAIN = 8 * HS


def fill_queries(ext, h, phi, col):
    for d in range(32):
        phi[d * HS : (d + 1) * HS, col : col + LEN] = (
            ext[h, 0:HS, :] * ext[h, d : d + HS, :]
        ).astype(BF)
    phi[4 * MAIN : NF, col : col + LEN] = (ext[h, 0:32, :] * ext[h, 32:HS, :]).astype(BF)


def key_piece(ext, vz, phi, turned, k):
    c = flip(lax.axis_index("z"), k)
    total = None
    for h in range(2):
        turned[h] = ext[h, pl.ds(pl.multiple_of(8 * c, 8), HS + 8), :]
        for j in range(8):
            left = ext[h, 0:HS, :]
            twice = left + left
            if j == 0:
                twice = jnp.where(c == 0, left, twice)
            phi[h, j * HS : (j + 1) * HS, :] = (twice * turned[h, j : j + HS, :]).astype(BF)
        low = ext[h, pl.ds(pl.multiple_of(8 * c, 8), 8), :]
        high = ext[h, pl.ds(pl.multiple_of(8 * c + 32, 8), 8), :]
        phi[h, MAIN:PIECE, :] = ((low + low) * high).astype(BF)
        part = jnp.dot(phi[h], vz[h * LEN : (h + 1) * LEN], preferred_element_type=F32)
        total = part if total is None else total + part
    return total.astype(BF)


def state_kernel(*refs):
    chunks, outs = refs[:4], refs[4:6]
    ext, vz, phi, turned = refs[6:]
    lane = lax.broadcasted_iota(jnp.int32, (PAIR, 128), 1)
    zero = jnp.zeros((PAIR, 128), BF)
    for k in range(4):
        at = slice(k * PAIR, (k + 1) * PAIR)
        keys = chunks[k][:, 0:128].astype(F32).T
        value = chunks[k][:, 128:256]
        for h in range(2):
            part = keys[h * HS : (h + 1) * HS]
            ext[h, 0:HS, at] = part
            ext[h, HS : 2 * HS, at] = part
            mine = (lane >= HS) if h else (lane < HS)
            vz[h * LEN + k * PAIR : h * LEN + (k + 1) * PAIR, :] = jnp.where(mine, value, zero)
    for i, (out, k) in enumerate(zip(outs, (1, 2))):
        out[...] = key_piece(ext, vz, phi.at[i], turned.at[i], k)


def third_kernel(ext, vz, out, phi, turned):
    out[...] = key_piece(ext, vz, phi, turned, 3)


def rest_kernel(ext, vz, after, out, phi, turned):
    out[...] = key_piece(ext, vz, phi, turned, 0)


def pair_rows(k):
    return pl.ds(pl.multiple_of(flip(lax.axis_index("y"), k) * PAIR, PAIR), PAIR)


def inside_kernel(*refs):
    pairs, queries, out = refs[:4], refs[4:8], refs[8]
    q, kk, v = refs[9:]
    for k in range(4):
        at = pair_rows(k)
        q[at, :] = queries[k][...]
        kk[at, :] = pairs[k][:, 0:128]
        v[at, :] = pairs[k][:, 128:256]
    T = 256
    lane_q = lax.broadcasted_iota(jnp.int32, (T, 128), 1)
    lane_v = lax.broadcasted_iota(jnp.int32, (LEN, 128), 1)
    causal = lax.broadcasted_iota(jnp.int32, (T, T), 0) >= lax.broadcasted_iota(
        jnp.int32, (T, T), 1
    )
    nt = (((1,), (1,)), ((), ()))
    vh = [jnp.where((lane_v >= HS) if h else (lane_v < HS), v[...], jnp.zeros((), BF)) for h in range(2)]
    for i in range(LEN // T):
        rows = slice(i * T, (i + 1) * T)
        total = None
        for h in range(2):
            qh = jnp.where((lane_q >= HS) if h else (lane_q < HS), q[rows, :], jnp.zeros((), BF))
            last = lax.dot_general(qh, kk[rows, :], nt, preferred_element_type=F32)
            last = jnp.where(causal, last * last, 0.0).astype(BF)
            add = jnp.dot(last, vh[h][rows], preferred_element_type=F32)
            total = add if total is None else total + add
            if i:
                full = lax.dot_general(qh, kk[0 : i * T, :], nt, preferred_element_type=F32)
                full = (full * full).astype(BF)
                total = total + jnp.dot(full, vh[h][0 : i * T], preferred_element_type=F32)
        out[rows, :] = total


def total_kernel(*refs):
    pieces, out = refs[:4], refs[4]
    out[...] = sum(p[...].astype(F32) for p in pieces).astype(BF)


def combine_kernel(*refs):
    pieces, totals, outs = refs[:4], refs[4:8], refs[10:14]
    x, z = lax.axis_index("x"), lax.axis_index("z")
    base = jnp.zeros((PIECE, 128), F32)
    for k in range(1, 4):
        base = base + jnp.where(flip(x, k) < x, totals[k][...].astype(F32), 0.0)
    for k in range(4):
        acc = base
        for j in range(4):
            if j != k:
                acc = acc + jnp.where(flip(z, j) < flip(z, k), pieces[j][...].astype(F32), 0.0)
        outs[k][...] = acc.astype(BF)


def features_kernel(*refs):
    queries, phi, ext = refs[:4], refs[4], refs[5]
    for k in range(4):
        at = slice(k * PAIR, (k + 1) * PAIR)
        turned = queries[k][...].astype(F32).T
        for h in range(2):
            part = turned[h * HS : (h + 1) * HS]
            ext[h, 0:HS, at] = part
            ext[h, HS : 2 * HS, at] = part
    for h in range(2):
        fill_queries(ext, h, phi, h * LEN)


def attend(turned, phi, inside, gain, first, last):
    halves = [
        jnp.dot(
            turned[h * HS : (h + 1) * HS],
            phi[:, h * LEN + first * PAIR : h * LEN + last * PAIR],
            preferred_element_type=F32,
        )
        for h in range(2)
    ]
    numer = jnp.concatenate(halves, axis=0).T
    low = lax.broadcasted_iota(jnp.int32, (PAIR, 128), 1) < HS
    outs = []
    for k in range(first, last):
        at = slice((k - first) * PAIR, (k - first + 1) * PAIR)
        mine = numer[at] + inside[pair_rows(k), :]
        square = mine * mine
        one = jnp.sum(jnp.where(low, square, 0.0), axis=-1, keepdims=True)
        two = jnp.sum(jnp.where(low, 0.0, square), axis=-1, keepdims=True)
        mean = jnp.where(low, one, two) * (1.0 / HS)
        outs.append((mine * lax.rsqrt(mean + 1e-05) * gain[...]).astype(BF))
    return outs


def apply_kernel(*refs):
    phi, states, inside, gain, outs, turned = refs[0], refs[1:5], refs[5], refs[6], refs[7:10], refs[10]
    state = refs[11]
    z = lax.axis_index("z")
    for k in range(4):
        c = flip(z, k)
        piece = states[k][...].astype(F32)
        state[pl.ds(pl.multiple_of(c * MAIN, MAIN), MAIN), :] = piece[0:MAIN]
        state[pl.ds(pl.multiple_of(4 * MAIN + 8 * c, 8), 8), :] = piece[MAIN:PIECE]
    turned[...] = state[...].T.astype(BF)
    for out, value in zip(outs, attend(turned[...], phi, inside, gain, 1, 4)):
        out[...] = value


def own_kernel(phi, turned, inside, gain, out):
    out[...] = attend(turned[...], phi, inside, gain, 0, 1)[0]


def merge_kernel(*refs):
    parts, out = refs[:4], refs[4]
    row = pl.multiple_of((1 - lax.axis_index("c")) * ROWS, ROWS)
    for k in range(4):
        col = pl.multiple_of(flip(lax.axis_index("y"), k) * 128, 128)
        out[:, pl.ds(col, 128)] = parts[k][pl.ds(row, ROWS), :]


FB = 2048


def mlp_kernel(*refs):
    parts, other, tok, gain, wo, wi, wf = refs[:4], *refs[4:10]
    att, res = refs[10:12]
    y, c = lax.axis_index("y"), lax.axis_index("c")
    row = pl.multiple_of(c * ROWS, ROWS)
    for k in range(4):
        col = 2 * flip(y, k) + ((1 - c) if k else c)
        att[:, pl.ds(pl.multiple_of(col * 128, 128), 128)] = parts[k][pl.ds(row, ROWS), :]
        col = 2 * k + jnp.where(y == k, 1 - c, c)
        att[:, pl.ds(pl.multiple_of(col * 128, 128), 128)] = other[:, k * 128 : (k + 1) * 128]
    stream = tok[...].astype(F32) + jnp.dot(att[...], wo[...], preferred_element_type=F32)
    stream = stream.astype(BF).astype(F32)
    normed = rms(stream, gain[...]).astype(BF)
    acc = stream
    for j in range(FF // FB):
        at = slice(j * FB, (j + 1) * FB)
        u = jnp.dot(normed, wi[:, at], preferred_element_type=F32)
        hidden = 0.5 * u * (1.0 + jnp.tanh(0.7978845608028654 * (u + 0.044715 * u * u * u)))
        acc = acc + jnp.dot(hidden.astype(BF), wf[at, :], preferred_element_type=F32)
    res[...] = acc.astype(BF)


def call(kernel, outs, scratch, specs, limit, flops=0, moved=0):
    return pl.pallas_call(
        kernel,
        out_shape=outs,
        in_specs=specs,
        out_specs=jax.tree.map(lambda _: VM, outs),
        scratch_shapes=scratch,
        compiler_params=pltpu.CompilerParams(vmem_limit_bytes=limit * MIB),
        cost_estimate=pl.CostEstimate(flops=flops, bytes_accessed=moved, transcendentals=0),
    )


def arr(*shape, dtype=BF):
    return jax.ShapeDtypeStruct(shape, dtype)


def fixed(array):
    return pltpu.with_memory_space_constraint(array, pltpu.HBM)


def exchange(parts, axes, pairs):
    moved = [parts[0]]
    for k in range(1, 4):
        moved.append(lax.ppermute(parts[k], axes, pairs[k]))
    return moved


ALONG = {k: xor_pairs(4, k) for k in range(1, 4)}
SWAPS = {k: [(i, i ^ (2 * k + 1)) for i in range(8)] for k in range(1, 4)}


def body(tokens, attn_gain, w_query, w_key, w_value, head_gain, w_output, mlp_gain, w_in, w_out):
    swapped = lax.ppermute(tokens, "c", xor_pairs(2, 1))
    own, gain, wkv = call(
        load_kernel,
        [arr(ROWS, D), arr(1, D, dtype=F32), arr(3, D, 256)],
        [
            pltpu.VMEM((ROWS, D), BF),
            pltpu.SemaphoreType.DMA((3, 2)),
            pltpu.SemaphoreType.DMA((2,)),
        ],
        [HBM] * 4,
        4,
        flops=128 * 1024 * 1024,
        moved=4 * MIB,
    )(fixed(tokens), fixed(attn_gain.reshape(1, D)), fixed(w_key), fixed(w_value))
    *pairs, normed = call(
        kv_kernel,
        [arr(PAIR, 256)] * 3 + [arr(PAIR, D)],
        [],
        [VM] * 4,
        6,
        flops=2 * 256 * 1024 * 1024,
        moved=3 * MIB,
    )(own, swapped, gain, wkv)
    pairs = exchange([None, *pairs], "y", ALONG)
    *queries, pairs[0] = call(
        q_kernel,
        [arr(PAIR, 128)] * 4 + [arr(PAIR, 256)],
        [pltpu.VMEM((D, 256), BF), pltpu.SemaphoreType.DMA((2,))],
        [VM] * 2 + [HBM] * 2,
        6,
        flops=2 * 256 * 1024 * 512,
        moved=4 * MIB,
    )(normed, w_query, fixed(w_key), fixed(w_value))
    spare = [pltpu.VMEM((2, PIECE, LEN), BF), pltpu.VMEM((2, HS + 8, LEN), F32)]
    twice = [pltpu.VMEM((2, 2, PIECE, LEN), BF), pltpu.VMEM((2, 2, HS + 8, LEN), F32)]
    cost = 2 * PIECE * 2 * LEN * 256
    first, second, ext, vz = call(
        state_kernel,
        [arr(PIECE, 128)] * 2 + [arr(2, 2 * HS, LEN, dtype=F32), arr(2 * LEN, 128)],
        twice,
        [VM] * 4,
        12,
        flops=2 * cost,
        moved=2 * MIB,
    )(*pairs)
    third = call(third_kernel, arr(PIECE, 128), spare, [VM] * 2, 8, flops=cost, moved=MIB)(ext, vz)
    own = call(
        rest_kernel, arr(PIECE, 128), spare, [VM] * 2 + [ANY], 8, flops=cost, moved=MIB
    )(ext, vz, third)
    pieces = exchange([own, first, second, third], "z", ALONG)
    queries = lax.optimization_barrier((queries, third))[0]
    queries = exchange(queries, "y", ALONG)
    inside = call(
        inside_kernel,
        arr(LEN, 128, dtype=F32),
        [pltpu.VMEM((LEN, 128), BF)] * 3,
        [VM] * 8,
        16,
        flops=2 * 1024 * 1024 * 256 * 2,
        moved=2 * MIB,
    )(*pairs, *queries)

    total = call(total_kernel, arr(PIECE, 128), [], [VM] * 4, 4, moved=MIB)(*pieces)
    totals = exchange([total] * 4, "x", ALONG)
    phi = call(
        features_kernel,
        arr(NF, 2 * LEN),
        [pltpu.VMEM((2, 2 * HS, LEN), F32)],
        [VM] * 4,
        6,
        flops=NF * 2 * LEN * 128,
        moved=9 * MIB,
    )(*queries)
    states = call(
        combine_kernel, [arr(PIECE, 128)] * 4, [], [VM] * 8 + [ANY] * 2, 8, moved=MIB
    )(*pieces, *totals, phi, inside)
    states = exchange(states, "z", ALONG)

    scale = head_gain.reshape(1, 128)
    *parts, turned = call(
        apply_kernel,
        [arr(PAIR, 128)] * 3 + [arr(128, NF)],
        [pltpu.VMEM((NF, 128), F32)],
        [VM] * 7,
        12,
        flops=2 * NF * 2 * LEN * 192,
        moved=2 * MIB,
    )(phi, *states, inside, scale)
    home = exchange([None, *parts], ("y", "c"), SWAPS)
    mine = call(
        own_kernel, arr(PAIR, 128), [], [VM] * 4, 8, flops=2 * NF * 2 * LEN * 64, moved=2 * MIB
    )(phi, turned, inside, scale)
    parts = [mine, *home[1:]]
    other = call(merge_kernel, arr(ROWS, 512), [], [VM] * 4, 4)(*parts)
    other = lax.ppermute(other, "c", xor_pairs(2, 1))

    return call(
        mlp_kernel,
        [arr(ROWS, D)] * 2,
        [],
        [VM] * 10,
        8,
        flops=2 * 128 * 1024 * 9216,
        moved=18 * MIB,
    )(*parts, other, tokens, mlp_gain.reshape(1, D), w_output, w_in, w_out)


def solution(mesh):
    finer = Mesh(mesh.devices.reshape(4, 4, 4, 2), SPLIT)
    placed = (P(SPLIT, None), P(), P(), P(), P(), P(BA), P(), P(), P(), P())
    return jax.shard_map(
        body,
        mesh=finer,
        in_specs=placed,
        out_specs=(P(SPLIT, None), P(SPLIT, None)),
        check_vma=False,
    )
```

```python
import jax
import jax.numpy as jnp
from jax import lax
from jax.experimental import pallas as pl
from jax.experimental.pallas import tpu as pltpu
from jax.sharding import Mesh
from jax.sharding import PartitionSpec as P

D = 1024
FF = 4096
HS = 64
NF = HS * (HS + 1) // 2
PIECE = NF // 4
ROWS = 128
PAIR = 2 * ROWS
LEN = 1024
F32 = jnp.float32
BF = jnp.bfloat16
SPLIT = ("x", "z", "y", "c")
BA = ("y", "c")
MIB = 1 << 20


VM = pl.BlockSpec(memory_space=pltpu.VMEM)
HBM = pl.BlockSpec(memory_space=pltpu.HBM)
ANY = pl.BlockSpec(memory_space=pl.ANY)


def xor_pairs(n, k):
    return [(i, i ^ k) for i in range(n)]


def flip(index, k):
    return jnp.bitwise_xor(index, k) if k else index


def rms(matrix, gain):
    return matrix * lax.rsqrt(jnp.mean(matrix * matrix, axis=-1, keepdims=True) + 1e-05) * gain


def columns(k):
    return pl.multiple_of((2 * flip(lax.axis_index("y"), k) + lax.axis_index("c")) * 128, 128)


def load_kernel(tok, gain, wk, wv, normed, gout, wout, tbuf, sems, tsems):
    first = [
        pltpu.make_async_copy(gain, gout, tsems.at[0]),
        pltpu.make_async_copy(tok, tbuf, tsems.at[1]),
    ]
    for copy in first:
        copy.start()
    copies = []
    for k in range(1, 4):
        for j, w in enumerate((wk, wv)):
            copy = pltpu.make_async_copy(
                w.at[:, pl.ds(columns(k), 128)],
                wout.at[k - 1, :, j * 128 : (j + 1) * 128],
                sems.at[k - 1, j],
            )
            copy.start()
            copies.append(copy)
    for copy in first:
        copy.wait()
    normed[...] = rms(tbuf[...].astype(F32), gout[...]).astype(BF)
    for copy in copies:
        copy.wait()


def kv_kernel(own, other, gain, wkv, *rest):
    outs, normed = rest[:3], rest[3]
    c = lax.axis_index("c")
    normed[pl.ds(pl.multiple_of(c * ROWS, ROWS), ROWS), :] = own[...]
    at = pl.ds(pl.multiple_of((1 - c) * ROWS, ROWS), ROWS)
    normed[at, :] = rms(other[...].astype(F32), gain[...]).astype(BF)
    for k in range(3):
        outs[k][...] = jnp.dot(normed[...], wkv[k], preferred_element_type=F32).astype(BF)


def q_kernel(normed, wq, wk, wv, *rest):
    outs, own, wbuf, sems = rest[:4], rest[4], rest[5], rest[6]
    copies = []
    for j, w in enumerate((wk, wv)):
        copy = pltpu.make_async_copy(
            w.at[:, pl.ds(columns(0), 128)], wbuf.at[:, j * 128 : (j + 1) * 128], sems.at[j]
        )
        copy.start()
        copies.append(copy)
    for k in range(4):
        outs[k][...] = jnp.dot(
            normed[...], wq[:, pl.ds(columns(k), 128)], preferred_element_type=F32
        ).astype(BF)
    for copy in copies:
        copy.wait()
    own[...] = jnp.dot(normed[...], wbuf[...], preferred_element_type=F32).astype(BF)


MAIN = 8 * HS


def fill_queries(ext, h, phi, col):
    for d in range(32):
        phi[d * HS : (d + 1) * HS, col : col + LEN] = (
            ext[h, 0:HS, :] * ext[h, d : d + HS, :]
        ).astype(BF)
    phi[4 * MAIN : NF, col : col + LEN] = (ext[h, 0:32, :] * ext[h, 32:HS, :]).astype(BF)


def key_piece(ext, vz, phi, turned, k):
    c = flip(lax.axis_index("z"), k)
    total = None
    for h in range(2):
        turned[h] = ext[h, pl.ds(pl.multiple_of(8 * c, 8), HS + 8), :]
        for j in range(8):
            left = ext[h, 0:HS, :]
            twice = left + left
            if j == 0:
                twice = jnp.where(c == 0, left, twice)
            phi[h, j * HS : (j + 1) * HS, :] = (twice * turned[h, j : j + HS, :]).astype(BF)
        low = ext[h, pl.ds(pl.multiple_of(8 * c, 8), 8), :]
        high = ext[h, pl.ds(pl.multiple_of(8 * c + 32, 8), 8), :]
        phi[h, MAIN:PIECE, :] = ((low + low) * high).astype(BF)
        part = jnp.dot(phi[h], vz[h * LEN : (h + 1) * LEN], preferred_element_type=F32)
        total = part if total is None else total + part
    return total.astype(BF)


def state_kernel(*refs):
    chunks, outs = refs[:4], refs[4:6]
    ext, vz, phi, turned = refs[6:]
    lane = lax.broadcasted_iota(jnp.int32, (PAIR, 128), 1)
    zero = jnp.zeros((PAIR, 128), BF)
    for k in range(4):
        at = slice(k * PAIR, (k + 1) * PAIR)
        keys = chunks[k][:, 0:128].astype(F32).T
        value = chunks[k][:, 128:256]
        for h in range(2):
            part = keys[h * HS : (h + 1) * HS]
            ext[h, 0:HS, at] = part
            ext[h, HS : 2 * HS, at] = part
            mine = (lane >= HS) if h else (lane < HS)
            vz[h * LEN + k * PAIR : h * LEN + (k + 1) * PAIR, :] = jnp.where(mine, value, zero)
    for i, (out, k) in enumerate(zip(outs, (2, 3))):
        out[...] = key_piece(ext, vz, phi.at[i], turned.at[i], k)


def third_kernel(ext, vz, out, phi, turned):
    out[...] = key_piece(ext, vz, phi, turned, 1)


def rest_kernel(ext, vz, after, out, phi, turned):
    out[...] = key_piece(ext, vz, phi, turned, 0)


def pair_rows(k):
    return pl.ds(pl.multiple_of(flip(lax.axis_index("y"), k) * PAIR, PAIR), PAIR)


def inside_kernel(*refs):
    pairs, queries, out = refs[:4], refs[4:8], refs[8]
    q, kk, v = refs[9:]
    for k in range(4):
        at = pair_rows(k)
        q[at, :] = queries[k][...]
        kk[at, :] = pairs[k][:, 0:128]
        v[at, :] = pairs[k][:, 128:256]
    T = 256
    lane_q = lax.broadcasted_iota(jnp.int32, (T, 128), 1)
    lane_v = lax.broadcasted_iota(jnp.int32, (LEN, 128), 1)
    causal = lax.broadcasted_iota(jnp.int32, (T, T), 0) >= lax.broadcasted_iota(
        jnp.int32, (T, T), 1
    )
    nt = (((1,), (1,)), ((), ()))
    vh = [jnp.where((lane_v >= HS) if h else (lane_v < HS), v[...], jnp.zeros((), BF)) for h in range(2)]
    for i in range(LEN // T):
        rows = slice(i * T, (i + 1) * T)
        total = None
        for h in range(2):
            qh = jnp.where((lane_q >= HS) if h else (lane_q < HS), q[rows, :], jnp.zeros((), BF))
            last = lax.dot_general(qh, kk[rows, :], nt, preferred_element_type=F32)
            last = jnp.where(causal, last * last, 0.0).astype(BF)
            add = jnp.dot(last, vh[h][rows], preferred_element_type=F32)
            total = add if total is None else total + add
            if i:
                full = lax.dot_general(qh, kk[0 : i * T, :], nt, preferred_element_type=F32)
                full = (full * full).astype(BF)
                total = total + jnp.dot(full, vh[h][0 : i * T], preferred_element_type=F32)
        out[rows, :] = total


def total_kernel(*refs):
    pieces, out = refs[:4], refs[4]
    out[...] = sum(p[...].astype(F32) for p in pieces).astype(BF)


def combine_kernel(*refs):
    pieces, totals, outs = refs[:4], refs[4:8], refs[10:14]
    x, z = lax.axis_index("x"), lax.axis_index("z")
    base = jnp.zeros((PIECE, 128), F32)
    for k in range(1, 4):
        base = base + jnp.where(flip(x, k) < x, totals[k][...].astype(F32), 0.0)
    for k in range(4):
        acc = base
        for j in range(4):
            if j != k:
                acc = acc + jnp.where(flip(z, j) < flip(z, k), pieces[j][...].astype(F32), 0.0)
        outs[k][...] = acc.astype(BF)


def features_kernel(*refs):
    queries, phi, ext = refs[:4], refs[4], refs[5]
    for k in range(4):
        at = slice(k * PAIR, (k + 1) * PAIR)
        turned = queries[k][...].astype(F32).T
        for h in range(2):
            part = turned[h * HS : (h + 1) * HS]
            ext[h, 0:HS, at] = part
            ext[h, HS : 2 * HS, at] = part
    for h in range(2):
        fill_queries(ext, h, phi, h * LEN)


def attend(turned, phi, inside, gain, first, last):
    halves = [
        jnp.dot(
            turned[h * HS : (h + 1) * HS],
            phi[:, h * LEN + first * PAIR : h * LEN + last * PAIR],
            preferred_element_type=F32,
        )
        for h in range(2)
    ]
    numer = jnp.concatenate(halves, axis=0).T
    low = lax.broadcasted_iota(jnp.int32, (PAIR, 128), 1) < HS
    outs = []
    for k in range(first, last):
        at = slice((k - first) * PAIR, (k - first + 1) * PAIR)
        mine = numer[at] + inside[pair_rows(k), :]
        square = mine * mine
        one = jnp.sum(jnp.where(low, square, 0.0), axis=-1, keepdims=True)
        two = jnp.sum(jnp.where(low, 0.0, square), axis=-1, keepdims=True)
        mean = jnp.where(low, one, two) * (1.0 / HS)
        outs.append((mine * lax.rsqrt(mean + 1e-05) * gain[...]).astype(BF))
    return outs


def apply_kernel(*refs):
    phi, states, inside, gain, outs, turned = refs[0], refs[1:5], refs[5], refs[6], refs[7:10], refs[10]
    state = refs[11]
    z = lax.axis_index("z")
    for k in range(4):
        c = flip(z, k)
        piece = states[k][...].astype(F32)
        state[pl.ds(pl.multiple_of(c * MAIN, MAIN), MAIN), :] = piece[0:MAIN]
        state[pl.ds(pl.multiple_of(4 * MAIN + 8 * c, 8), 8), :] = piece[MAIN:PIECE]
    turned[...] = state[...].T.astype(BF)
    for out, value in zip(outs, attend(turned[...], phi, inside, gain, 1, 4)):
        out[...] = value


def own_kernel(phi, turned, inside, gain, out):
    out[...] = attend(turned[...], phi, inside, gain, 0, 1)[0]


def merge_kernel(*refs):
    parts, out = refs[:4], refs[4]
    row = pl.multiple_of((1 - lax.axis_index("c")) * ROWS, ROWS)
    for k in range(4):
        col = pl.multiple_of(flip(lax.axis_index("y"), k) * 128, 128)
        out[:, pl.ds(col, 128)] = parts[k][pl.ds(row, ROWS), :]


FB = 2048


def mlp_kernel(*refs):
    parts, other, tok, gain, wo, wi, wf = refs[:4], *refs[4:10]
    att, res = refs[10:12]
    y, c = lax.axis_index("y"), lax.axis_index("c")
    row = pl.multiple_of(c * ROWS, ROWS)
    for k in range(4):
        col = 2 * flip(y, k) + ((1 - c) if k else c)
        att[:, pl.ds(pl.multiple_of(col * 128, 128), 128)] = parts[k][pl.ds(row, ROWS), :]
        col = 2 * k + jnp.where(y == k, 1 - c, c)
        att[:, pl.ds(pl.multiple_of(col * 128, 128), 128)] = other[:, k * 128 : (k + 1) * 128]
    stream = tok[...].astype(F32) + jnp.dot(att[...], wo[...], preferred_element_type=F32)
    stream = stream.astype(BF).astype(F32)
    normed = rms(stream, gain[...]).astype(BF)
    acc = stream
    for j in range(FF // FB):
        at = slice(j * FB, (j + 1) * FB)
        u = jnp.dot(normed, wi[:, at], preferred_element_type=F32)
        hidden = 0.5 * u * (1.0 + jnp.tanh(0.7978845608028654 * (u + 0.044715 * u * u * u)))
        acc = acc + jnp.dot(hidden.astype(BF), wf[at, :], preferred_element_type=F32)
    res[...] = acc.astype(BF)


def call(kernel, outs, scratch, specs, limit, flops=0, moved=0):
    return pl.pallas_call(
        kernel,
        out_shape=outs,
        in_specs=specs,
        out_specs=jax.tree.map(lambda _: VM, outs),
        scratch_shapes=scratch,
        compiler_params=pltpu.CompilerParams(vmem_limit_bytes=limit * MIB),
        cost_estimate=pl.CostEstimate(flops=flops, bytes_accessed=moved, transcendentals=0),
    )


def arr(*shape, dtype=BF):
    return jax.ShapeDtypeStruct(shape, dtype)


def fixed(array):
    return pltpu.with_memory_space_constraint(array, pltpu.HBM)


def exchange(parts, axes, pairs):
    moved = [parts[0]]
    for k in range(1, 4):
        moved.append(lax.ppermute(parts[k], axes, pairs[k]))
    return moved


ALONG = {k: xor_pairs(4, k) for k in range(1, 4)}
SWAPS = {k: [(i, i ^ (2 * k + 1)) for i in range(8)] for k in range(1, 4)}


def body(tokens, attn_gain, w_query, w_key, w_value, head_gain, w_output, mlp_gain, w_in, w_out):
    swapped = lax.ppermute(tokens, "c", xor_pairs(2, 1))
    own, gain, wkv = call(
        load_kernel,
        [arr(ROWS, D), arr(1, D, dtype=F32), arr(3, D, 256)],
        [
            pltpu.VMEM((ROWS, D), BF),
            pltpu.SemaphoreType.DMA((3, 2)),
            pltpu.SemaphoreType.DMA((2,)),
        ],
        [HBM] * 4,
        4,
        flops=128 * 1024 * 1024,
        moved=4 * MIB,
    )(fixed(tokens), fixed(attn_gain.reshape(1, D)), fixed(w_key), fixed(w_value))
    *pairs, normed = call(
        kv_kernel,
        [arr(PAIR, 256)] * 3 + [arr(PAIR, D)],
        [],
        [VM] * 4,
        6,
        flops=2 * 256 * 1024 * 1024,
        moved=3 * MIB,
    )(own, swapped, gain, wkv)
    pairs = exchange([None, *pairs], "y", ALONG)
    *queries, pairs[0] = call(
        q_kernel,
        [arr(PAIR, 128)] * 4 + [arr(PAIR, 256)],
        [pltpu.VMEM((D, 256), BF), pltpu.SemaphoreType.DMA((2,))],
        [VM] * 2 + [HBM] * 2,
        6,
        flops=2 * 256 * 1024 * 512,
        moved=4 * MIB,
    )(normed, w_query, fixed(w_key), fixed(w_value))
    spare = [pltpu.VMEM((2, PIECE, LEN), BF), pltpu.VMEM((2, HS + 8, LEN), F32)]
    twice = [pltpu.VMEM((2, 2, PIECE, LEN), BF), pltpu.VMEM((2, 2, HS + 8, LEN), F32)]
    cost = 2 * PIECE * 2 * LEN * 256
    first, second, ext, vz = call(
        state_kernel,
        [arr(PIECE, 128)] * 2 + [arr(2, 2 * HS, LEN, dtype=F32), arr(2 * LEN, 128)],
        twice,
        [VM] * 4,
        12,
        flops=2 * cost,
        moved=2 * MIB,
    )(*pairs)
    third = call(third_kernel, arr(PIECE, 128), spare, [VM] * 2, 8, flops=cost, moved=MIB)(ext, vz)
    own = call(
        rest_kernel, arr(PIECE, 128), spare, [VM] * 2 + [ANY], 8, flops=cost, moved=MIB
    )(ext, vz, third)
    pieces = exchange([own, third, first, second], "z", ALONG)
    queries = lax.optimization_barrier((queries, third))[0]
    queries = exchange(queries, "y", ALONG)
    inside = call(
        inside_kernel,
        arr(LEN, 128, dtype=F32),
        [pltpu.VMEM((LEN, 128), BF)] * 3,
        [VM] * 8,
        16,
        flops=2 * 1024 * 1024 * 256 * 2,
        moved=2 * MIB,
    )(*pairs, *queries)

    total = call(total_kernel, arr(PIECE, 128), [], [VM] * 4, 4, moved=MIB)(*pieces)
    totals = exchange([total] * 4, "x", ALONG)
    phi = call(
        features_kernel,
        arr(NF, 2 * LEN),
        [pltpu.VMEM((2, 2 * HS, LEN), F32)],
        [VM] * 4,
        6,
        flops=NF * 2 * LEN * 128,
        moved=9 * MIB,
    )(*queries)
    states = call(
        combine_kernel, [arr(PIECE, 128)] * 4, [], [VM] * 8 + [ANY] * 2, 8, moved=MIB
    )(*pieces, *totals, phi, inside)
    states = exchange(states, "z", ALONG)

    scale = head_gain.reshape(1, 128)
    *parts, turned = call(
        apply_kernel,
        [arr(PAIR, 128)] * 3 + [arr(128, NF)],
        [pltpu.VMEM((NF, 128), F32)],
        [VM] * 7,
        12,
        flops=2 * NF * 2 * LEN * 192,
        moved=2 * MIB,
    )(phi, *states, inside, scale)
    home = exchange([None, *parts], ("y", "c"), SWAPS)
    mine = call(
        own_kernel, arr(PAIR, 128), [], [VM] * 4, 8, flops=2 * NF * 2 * LEN * 64, moved=2 * MIB
    )(phi, turned, inside, scale)
    parts = [mine, *home[1:]]
    other = call(merge_kernel, arr(ROWS, 512), [], [VM] * 4, 4)(*parts)
    other = lax.ppermute(other, "c", xor_pairs(2, 1))

    return call(
        mlp_kernel,
        [arr(ROWS, D)] * 2,
        [],
        [VM] * 10,
        8,
        flops=2 * 128 * 1024 * 9216,
        moved=18 * MIB,
    )(*parts, other, tokens, mlp_gain.reshape(1, D), w_output, w_in, w_out)


def solution(mesh):
    finer = Mesh(mesh.devices.reshape(4, 4, 4, 2), SPLIT)
    placed = (P(SPLIT, None), P(), P(), P(), P(), P(BA), P(), P(), P(), P())
    return jax.shard_map(
        body,
        mesh=finer,
        in_specs=placed,
        out_specs=(P(SPLIT, None), P(SPLIT, None)),
        check_vma=False,
    )
```

```python
import jax
import jax.numpy as jnp
from jax import lax
from jax.experimental import pallas as pl
from jax.experimental.pallas import tpu as pltpu
from jax.sharding import Mesh
from jax.sharding import PartitionSpec as P

D = 1024
FF = 4096
HS = 64
NF = HS * (HS + 1) // 2
PIECE = NF // 4
ROWS = 128
PAIR = 2 * ROWS
LEN = 1024
F32 = jnp.float32
BF = jnp.bfloat16
SPLIT = ("x", "z", "y", "c")
BA = ("y", "c")
MIB = 1 << 20


VM = pl.BlockSpec(memory_space=pltpu.VMEM)
HBM = pl.BlockSpec(memory_space=pltpu.HBM)
ANY = pl.BlockSpec(memory_space=pl.ANY)


def xor_pairs(n, k):
    return [(i, i ^ k) for i in range(n)]


def flip(index, k):
    return jnp.bitwise_xor(index, k) if k else index


def rms(matrix, gain):
    return matrix * lax.rsqrt(jnp.mean(matrix * matrix, axis=-1, keepdims=True) + 1e-05) * gain


def columns(k):
    return pl.multiple_of((2 * flip(lax.axis_index("y"), k) + lax.axis_index("c")) * 128, 128)


def load_kernel(tok, gain, wk, wv, normed, gout, wout, tbuf, sems, tsems):
    first = [
        pltpu.make_async_copy(gain, gout, tsems.at[0]),
        pltpu.make_async_copy(tok, tbuf, tsems.at[1]),
    ]
    for copy in first:
        copy.start()
    copies = []
    for k in range(1, 4):
        for j, w in enumerate((wk, wv)):
            copy = pltpu.make_async_copy(
                w.at[:, pl.ds(columns(k), 128)],
                wout.at[k - 1, :, j * 128 : (j + 1) * 128],
                sems.at[k - 1, j],
            )
            copy.start()
            copies.append(copy)
    for copy in first:
        copy.wait()
    normed[...] = rms(tbuf[...].astype(F32), gout[...]).astype(BF)
    for copy in copies:
        copy.wait()


def kv_kernel(own, other, gain, wkv, *rest):
    outs, normed = rest[:3], rest[3]
    c = lax.axis_index("c")
    normed[pl.ds(pl.multiple_of(c * ROWS, ROWS), ROWS), :] = own[...]
    at = pl.ds(pl.multiple_of((1 - c) * ROWS, ROWS), ROWS)
    normed[at, :] = rms(other[...].astype(F32), gain[...]).astype(BF)
    for k in range(3):
        outs[k][...] = jnp.dot(normed[...], wkv[k], preferred_element_type=F32).astype(BF)


def q_kernel(normed, wq, wk, wv, *rest):
    outs, own, wbuf, sems = rest[:4], rest[4], rest[5], rest[6]
    copies = []
    for j, w in enumerate((wk, wv)):
        copy = pltpu.make_async_copy(
            w.at[:, pl.ds(columns(0), 128)], wbuf.at[:, j * 128 : (j + 1) * 128], sems.at[j]
        )
        copy.start()
        copies.append(copy)
    for k in range(4):
        outs[k][...] = jnp.dot(
            normed[...], wq[:, pl.ds(columns(k), 128)], preferred_element_type=F32
        ).astype(BF)
    for copy in copies:
        copy.wait()
    own[...] = jnp.dot(normed[...], wbuf[...], preferred_element_type=F32).astype(BF)


MAIN = 8 * HS


def fill_queries(ext, h, phi, col):
    for d in range(32):
        phi[d * HS : (d + 1) * HS, col : col + LEN] = (
            ext[h, 0:HS, :] * ext[h, d : d + HS, :]
        ).astype(BF)
    phi[4 * MAIN : NF, col : col + LEN] = (ext[h, 0:32, :] * ext[h, 32:HS, :]).astype(BF)


def key_piece(ext, vz, phi, turned, k):
    c = flip(lax.axis_index("z"), k)
    total = None
    for h in range(2):
        turned[h] = ext[h, pl.ds(pl.multiple_of(8 * c, 8), HS + 8), :]
        for j in range(8):
            left = ext[h, 0:HS, :]
            twice = left + left
            if j == 0:
                twice = jnp.where(c == 0, left, twice)
            phi[h, j * HS : (j + 1) * HS, :] = (twice * turned[h, j : j + HS, :]).astype(BF)
        low = ext[h, pl.ds(pl.multiple_of(8 * c, 8), 8), :]
        high = ext[h, pl.ds(pl.multiple_of(8 * c + 32, 8), 8), :]
        phi[h, MAIN:PIECE, :] = ((low + low) * high).astype(BF)
        part = jnp.dot(phi[h], vz[h * LEN : (h + 1) * LEN], preferred_element_type=F32)
        total = part if total is None else total + part
    return total.astype(BF)


def state_kernel(*refs):
    chunks, outs = refs[:4], refs[4:6]
    ext, vz, phi, turned = refs[6:]
    lane = lax.broadcasted_iota(jnp.int32, (PAIR, 128), 1)
    zero = jnp.zeros((PAIR, 128), BF)
    for k in range(4):
        at = slice(k * PAIR, (k + 1) * PAIR)
        keys = chunks[k][:, 0:128].astype(F32).T
        value = chunks[k][:, 128:256]
        for h in range(2):
            part = keys[h * HS : (h + 1) * HS]
            ext[h, 0:HS, at] = part
            ext[h, HS : 2 * HS, at] = part
            mine = (lane >= HS) if h else (lane < HS)
            vz[h * LEN + k * PAIR : h * LEN + (k + 1) * PAIR, :] = jnp.where(mine, value, zero)
    for i, (out, k) in enumerate(zip(outs, (1, 2))):
        out[...] = key_piece(ext, vz, phi.at[i], turned.at[i], k)


def third_kernel(ext, vz, out, phi, turned):
    out[...] = key_piece(ext, vz, phi, turned, 3)


def rest_kernel(ext, vz, after, out, phi, turned):
    out[...] = key_piece(ext, vz, phi, turned, 0)


def pair_rows(k):
    return pl.ds(pl.multiple_of(flip(lax.axis_index("y"), k) * PAIR, PAIR), PAIR)


def inside_kernel(*refs):
    pairs, queries, out = refs[:4], refs[4:8], refs[8]
    q, kk, v = refs[9:]
    for k in range(4):
        at = pair_rows(k)
        q[at, :] = queries[k][...]
        kk[at, :] = pairs[k][:, 0:128]
        v[at, :] = pairs[k][:, 128:256]
    T = 256
    lane_q = lax.broadcasted_iota(jnp.int32, (T, 128), 1)
    lane_v = lax.broadcasted_iota(jnp.int32, (LEN, 128), 1)
    causal = lax.broadcasted_iota(jnp.int32, (T, T), 0) >= lax.broadcasted_iota(
        jnp.int32, (T, T), 1
    )
    nt = (((1,), (1,)), ((), ()))
    vh = [jnp.where((lane_v >= HS) if h else (lane_v < HS), v[...], jnp.zeros((), BF)) for h in range(2)]
    for i in range(LEN // T):
        rows = slice(i * T, (i + 1) * T)
        total = None
        for h in range(2):
            qh = jnp.where((lane_q >= HS) if h else (lane_q < HS), q[rows, :], jnp.zeros((), BF))
            last = lax.dot_general(qh, kk[rows, :], nt, preferred_element_type=F32)
            last = jnp.where(causal, last * last, 0.0).astype(BF)
            add = jnp.dot(last, vh[h][rows], preferred_element_type=F32)
            total = add if total is None else total + add
            if i:
                full = lax.dot_general(qh, kk[0 : i * T, :], nt, preferred_element_type=F32)
                full = (full * full).astype(BF)
                total = total + jnp.dot(full, vh[h][0 : i * T], preferred_element_type=F32)
        out[rows, :] = total


def total_kernel(*refs):
    pieces, out = refs[:4], refs[4]
    out[...] = sum(p[...].astype(F32) for p in pieces).astype(BF)


def combine_kernel(*refs):
    pieces, totals, outs = refs[:4], refs[4:8], refs[9:13]
    x, z = lax.axis_index("x"), lax.axis_index("z")
    base = jnp.zeros((PIECE, 128), F32)
    for k in range(1, 4):
        base = base + jnp.where(flip(x, k) < x, totals[k][...].astype(F32), 0.0)
    for k in range(4):
        acc = base
        for j in range(4):
            if j != k:
                acc = acc + jnp.where(flip(z, j) < flip(z, k), pieces[j][...].astype(F32), 0.0)
        outs[k][...] = acc.astype(BF)


def features_kernel(*refs):
    queries, phi, ext = refs[:4], refs[4], refs[5]
    for k in range(4):
        at = slice(k * PAIR, (k + 1) * PAIR)
        turned = queries[k][...].astype(F32).T
        for h in range(2):
            part = turned[h * HS : (h + 1) * HS]
            ext[h, 0:HS, at] = part
            ext[h, HS : 2 * HS, at] = part
    for h in range(2):
        fill_queries(ext, h, phi, h * LEN)


def attend(turned, phi, inside, gain, first, last):
    halves = [
        jnp.dot(
            turned[h * HS : (h + 1) * HS],
            phi[:, h * LEN + first * PAIR : h * LEN + last * PAIR],
            preferred_element_type=F32,
        )
        for h in range(2)
    ]
    numer = jnp.concatenate(halves, axis=0).T
    low = lax.broadcasted_iota(jnp.int32, (PAIR, 128), 1) < HS
    outs = []
    for k in range(first, last):
        at = slice((k - first) * PAIR, (k - first + 1) * PAIR)
        mine = numer[at] + inside[pair_rows(k), :]
        square = mine * mine
        one = jnp.sum(jnp.where(low, square, 0.0), axis=-1, keepdims=True)
        two = jnp.sum(jnp.where(low, 0.0, square), axis=-1, keepdims=True)
        mean = jnp.where(low, one, two) * (1.0 / HS)
        outs.append((mine * lax.rsqrt(mean + 1e-05) * gain[...]).astype(BF))
    return outs


def apply_kernel(*refs):
    phi, states, inside, gain, outs, turned = refs[0], refs[1:5], refs[5], refs[6], refs[7:10], refs[10]
    state = refs[11]
    z = lax.axis_index("z")
    for k in range(4):
        c = flip(z, k)
        piece = states[k][...].astype(F32)
        state[pl.ds(pl.multiple_of(c * MAIN, MAIN), MAIN), :] = piece[0:MAIN]
        state[pl.ds(pl.multiple_of(4 * MAIN + 8 * c, 8), 8), :] = piece[MAIN:PIECE]
    turned[...] = state[...].T.astype(BF)
    for out, value in zip(outs, attend(turned[...], phi, inside, gain, 1, 4)):
        out[...] = value


def own_kernel(phi, turned, inside, gain, out):
    out[...] = attend(turned[...], phi, inside, gain, 0, 1)[0]


def merge_kernel(*refs):
    parts, out = refs[:4], refs[4]
    row = pl.multiple_of((1 - lax.axis_index("c")) * ROWS, ROWS)
    for k in range(4):
        col = pl.multiple_of(flip(lax.axis_index("y"), k) * 128, 128)
        out[:, pl.ds(col, 128)] = parts[k][pl.ds(row, ROWS), :]


FB = 2048


def mlp_kernel(*refs):
    parts, other, tok, gain, wo, wi, wf = refs[:4], *refs[4:10]
    att, res = refs[10:12]
    y, c = lax.axis_index("y"), lax.axis_index("c")
    row = pl.multiple_of(c * ROWS, ROWS)
    for k in range(4):
        col = 2 * flip(y, k) + ((1 - c) if k else c)
        att[:, pl.ds(pl.multiple_of(col * 128, 128), 128)] = parts[k][pl.ds(row, ROWS), :]
        col = 2 * k + jnp.where(y == k, 1 - c, c)
        att[:, pl.ds(pl.multiple_of(col * 128, 128), 128)] = other[:, k * 128 : (k + 1) * 128]
    stream = tok[...].astype(F32) + jnp.dot(att[...], wo[...], preferred_element_type=F32)
    stream = stream.astype(BF).astype(F32)
    normed = rms(stream, gain[...]).astype(BF)
    acc = stream
    for j in range(FF // FB):
        at = slice(j * FB, (j + 1) * FB)
        u = jnp.dot(normed, wi[:, at], preferred_element_type=F32)
        hidden = 0.5 * u * (1.0 + jnp.tanh(0.7978845608028654 * (u + 0.044715 * u * u * u)))
        acc = acc + jnp.dot(hidden.astype(BF), wf[at, :], preferred_element_type=F32)
    res[...] = acc.astype(BF)


def call(kernel, outs, scratch, specs, limit, flops=0, moved=0):
    return pl.pallas_call(
        kernel,
        out_shape=outs,
        in_specs=specs,
        out_specs=jax.tree.map(lambda _: VM, outs),
        scratch_shapes=scratch,
        compiler_params=pltpu.CompilerParams(vmem_limit_bytes=limit * MIB),
        cost_estimate=pl.CostEstimate(flops=flops, bytes_accessed=moved, transcendentals=0),
    )


def arr(*shape, dtype=BF):
    return jax.ShapeDtypeStruct(shape, dtype)


def fixed(array):
    return pltpu.with_memory_space_constraint(array, pltpu.HBM)


def exchange(parts, axes, pairs):
    moved = [parts[0]]
    for k in range(1, 4):
        moved.append(lax.ppermute(parts[k], axes, pairs[k]))
    return moved


ALONG = {k: xor_pairs(4, k) for k in range(1, 4)}
SWAPS = {k: [(i, i ^ (2 * k + 1)) for i in range(8)] for k in range(1, 4)}


def body(tokens, attn_gain, w_query, w_key, w_value, head_gain, w_output, mlp_gain, w_in, w_out):
    swapped = lax.ppermute(tokens, "c", xor_pairs(2, 1))
    own, gain, wkv = call(
        load_kernel,
        [arr(ROWS, D), arr(1, D, dtype=F32), arr(3, D, 256)],
        [
            pltpu.VMEM((ROWS, D), BF),
            pltpu.SemaphoreType.DMA((3, 2)),
            pltpu.SemaphoreType.DMA((2,)),
        ],
        [HBM] * 4,
        4,
        flops=128 * 1024 * 1024,
        moved=4 * MIB,
    )(fixed(tokens), fixed(attn_gain.reshape(1, D)), fixed(w_key), fixed(w_value))
    *pairs, normed = call(
        kv_kernel,
        [arr(PAIR, 256)] * 3 + [arr(PAIR, D)],
        [],
        [VM] * 4,
        6,
        flops=2 * 256 * 1024 * 1024,
        moved=3 * MIB,
    )(own, swapped, gain, wkv)
    pairs = exchange([None, *pairs], "y", ALONG)
    *queries, pairs[0] = call(
        q_kernel,
        [arr(PAIR, 128)] * 4 + [arr(PAIR, 256)],
        [pltpu.VMEM((D, 256), BF), pltpu.SemaphoreType.DMA((2,))],
        [VM] * 2 + [HBM] * 2,
        6,
        flops=2 * 256 * 1024 * 512,
        moved=4 * MIB,
    )(normed, w_query, fixed(w_key), fixed(w_value))
    spare = [pltpu.VMEM((2, PIECE, LEN), BF), pltpu.VMEM((2, HS + 8, LEN), F32)]
    twice = [pltpu.VMEM((2, 2, PIECE, LEN), BF), pltpu.VMEM((2, 2, HS + 8, LEN), F32)]
    cost = 2 * PIECE * 2 * LEN * 256
    first, second, ext, vz = call(
        state_kernel,
        [arr(PIECE, 128)] * 2 + [arr(2, 2 * HS, LEN, dtype=F32), arr(2 * LEN, 128)],
        twice,
        [VM] * 4,
        12,
        flops=2 * cost,
        moved=2 * MIB,
    )(*pairs)
    third = call(third_kernel, arr(PIECE, 128), spare, [VM] * 2, 8, flops=cost, moved=MIB)(ext, vz)
    own = call(
        rest_kernel, arr(PIECE, 128), spare, [VM] * 2 + [ANY], 8, flops=cost, moved=MIB
    )(ext, vz, third)
    pieces = exchange([own, first, second, third], "z", ALONG)
    queries = lax.optimization_barrier((queries, third))[0]
    queries = exchange(queries, "y", ALONG)
    inside = call(
        inside_kernel,
        arr(LEN, 128, dtype=F32),
        [pltpu.VMEM((LEN, 128), BF)] * 3,
        [VM] * 8,
        16,
        flops=2 * 1024 * 1024 * 256 * 2,
        moved=2 * MIB,
    )(*pairs, *queries)

    total = call(total_kernel, arr(PIECE, 128), [], [VM] * 4, 4, moved=MIB)(*pieces)
    totals = exchange([total] * 4, "x", ALONG)
    phi = call(
        features_kernel,
        arr(NF, 2 * LEN),
        [pltpu.VMEM((2, 2 * HS, LEN), F32)],
        [VM] * 4,
        6,
        flops=NF * 2 * LEN * 128,
        moved=9 * MIB,
    )(*queries)
    states = call(
        combine_kernel, [arr(PIECE, 128)] * 4, [], [VM] * 8 + [ANY], 8, moved=MIB
    )(*pieces, *totals, phi)
    states = exchange(states, "z", ALONG)

    scale = head_gain.reshape(1, 128)
    *parts, turned = call(
        apply_kernel,
        [arr(PAIR, 128)] * 3 + [arr(128, NF)],
        [pltpu.VMEM((NF, 128), F32)],
        [VM] * 7,
        12,
        flops=2 * NF * 2 * LEN * 192,
        moved=2 * MIB,
    )(phi, *states, inside, scale)
    home = exchange([None, *parts], ("y", "c"), SWAPS)
    mine = call(
        own_kernel, arr(PAIR, 128), [], [VM] * 4, 8, flops=2 * NF * 2 * LEN * 64, moved=2 * MIB
    )(phi, turned, inside, scale)
    parts = [mine, *home[1:]]
    other = call(merge_kernel, arr(ROWS, 512), [], [VM] * 4, 4)(*parts)
    other = lax.ppermute(other, "c", xor_pairs(2, 1))

    return call(
        mlp_kernel,
        [arr(ROWS, D)] * 2,
        [],
        [VM] * 10,
        8,
        flops=2 * 128 * 1024 * 9216,
        moved=18 * MIB,
    )(*parts, other, tokens, mlp_gain.reshape(1, D), w_output, w_in, w_out)


def solution(mesh):
    finer = Mesh(mesh.devices.reshape(4, 4, 4, 2), SPLIT)
    placed = (P(SPLIT, None), P(), P(), P(), P(), P(BA), P(), P(), P(), P())
    return jax.shard_map(
        body,
        mesh=finer,
        in_specs=placed,
        out_specs=(P(SPLIT, None), P(SPLIT, None)),
        check_vma=False,
    )
```
